32 devices in a mesh: dp: 8 (over y, x, core), mp: 4 (over z).
Axes of the slice: x: 2, y: 2, z: 4, core: 2. Of those that a mesh axis runs over, the one named last changes fastest.
Arguments:
- inputs: bfloat16 [16, 1088, 1024], P('dp'), may hold values from -6 to 6
- encoded: bfloat16 [16, 512, 1024], P('dp'), may hold values from -6 to 6
- decoder_segments: int32 [16, 1088], P('dp'), may hold values from 0 to 3, as said below
- encoder_segments: int32 [16, 512], P('dp'), may hold values from 0 to 3, as said below
- buckets: int32 [1088], replicated, may hold values from 0 to 31, as said below
- self_gain: bfloat16 [1024], P('dp'), may hold values from 0.5 to 1.5
- self_query: bfloat16 [1024, 1024], P('dp', 'mp'), may hold values from -0.09375 to 0.09375
- self_key: bfloat16 [1024, 512], P('dp', 'mp'), may hold values from -0.09375 to 0.09375
- self_value: bfloat16 [1024, 512], P('dp', 'mp'), may hold values from -0.1875 to 0.1875
- self_out: bfloat16 [1024, 1024], P('mp', 'dp'), may hold values from -0.75 to 0.75
- position_bias: bfloat16 [32, 16], P('dp', 'mp'), may hold values from -4 to 4
- cross_gain: bfloat16 [1024], P('dp'), may hold values from 0.5 to 1.5
- cross_query: bfloat16 [1024, 1024], P('dp', 'mp'), may hold values from -0.09375 to 0.09375
- cross_key: bfloat16 [1024, 512], P('dp', 'mp'), may hold values from -0.09375 to 0.09375
- cross_value: bfloat16 [1024, 512], P('dp', 'mp'), may hold values from -0.1875 to 0.1875
- cross_out: bfloat16 [1024, 1024], P('mp', 'dp'), may hold values from -0.75 to 0.75
- feed_gain: bfloat16 [1024], P('dp'), may hold values from 0.5 to 1.5
- feed_gate: bfloat16 [1024, 2816], P('dp', 'mp'), may hold values from -0.1875 to 0.1875
- feed_up: bfloat16 [1024, 2816], P('dp', 'mp'), may hold values from -0.1875 to 0.1875
- feed_down: bfloat16 [2816, 1024], P('mp', 'dp'), may hold values from -0.21875 to 0.21875
- cotangent: bfloat16 [16, 1088, 1024], P('dp'), may hold values from -6 to 6
Outputs:
- outputs: bfloat16 [16, 1088, 1024], P('dp')
- grad_inputs: bfloat16 [16, 1088, 1024], P('dp')
- grad_encoded: bfloat16 [16, 512, 1024], P('dp')
- grad_self_gain: float32 [1024], P('dp')
- grad_self_query: float32 [1024, 1024], P('dp', 'mp')
- grad_self_key: float32 [1024, 512], P('dp', 'mp')
- grad_self_value: float32 [1024, 512], P('dp', 'mp')
- grad_self_out: float32 [1024, 1024], P('mp', 'dp')
- grad_position_bias: float32 [32, 16], P('dp', 'mp')
- grad_cross_gain: float32 [1024], P('dp')
- grad_cross_query: float32 [1024, 1024], P('dp', 'mp')
- grad_cross_key: float32 [1024, 512], P('dp', 'mp')
- grad_cross_value: float32 [1024, 512], P('dp', 'mp')
- grad_cross_out: float32 [1024, 1024], P('mp', 'dp')
- grad_feed_gain: float32 [1024], P('dp')
- grad_feed_gate: float32 [1024, 2816], P('dp', 'mp')
- grad_feed_up: float32 [1024, 2816], P('dp', 'mp')
- grad_feed_down: float32 [2816, 1024], P('mp', 'dp')
The draws below stay inside these ranges and needn't reach their ends.
Inputs may be any that keep to these rules, and one draw needn't show every extreme that they name: `decoder_segments`: in each sequence the numbers never fall and run through 0 to 3; every document has 60 to 800 tokens, and one of each sequence has exactly 800. `encoder_segments`: in each sequence the numbers never fall and run through 0 to 3; every document has 32 encoder outputs or more. `buckets`: entry d is the bucket of a key d positions before its query.
All inputs are finite; a program needn't handle non-finite values.
Results may differ from the reference program's by a relative error of at most 0.025.
The reference program's roundings to bfloat16 on the way count: a program that leaves them out, or rounds other values in their place, can miss the bound.
Values may be sent and summed in bfloat16 or wider, within the bound.
A program may use at most 448 MiB of HBM per device.

```python
import jax
import jax.numpy as jnp
from jax import lax

D = 1024
HEADS = 16
HEAD_DIM = 64
KV_HEADS = 8
FF = 2816
BUCKETS = 32
SEQ_TOKENS = 1088
ENC_TOKENS = 512
DOCS = 4
DOC_MOST = 800
DOC_LEAST = 60
ENC_LEAST = 32
SEQUENCES = 16


def split_pool(key, pool, parts, least):
    cuts = jnp.sort(jax.random.randint(key, (parts - 1,), 0, pool + 1)).astype(jnp.int32)
    edges = jnp.concatenate([jnp.zeros((1,), jnp.int32), cuts, jnp.full((1,), pool, jnp.int32)])
    return edges[1:] - edges[:-1] + least


def numbers_from_lengths(lengths, total):
    bounds = jnp.cumsum(lengths)[:-1]
    positions = jnp.arange(total, dtype=jnp.int32)
    return jnp.sum((positions[:, None] >= bounds[None, :]).astype(jnp.int32), axis=1)


def decoder_row(key):
    pool_key, place_key = jax.random.split(key)
    others = split_pool(pool_key, SEQ_TOKENS - DOC_MOST - (DOCS - 1) * DOC_LEAST, DOCS - 1, DOC_LEAST)
    place = jax.random.randint(place_key, (), 0, DOCS)
    slots = jnp.arange(DOCS, dtype=jnp.int32)
    shifted = jnp.clip(slots - (slots > place).astype(jnp.int32), 0, DOCS - 2)
    lengths = jnp.where(slots == place, DOC_MOST, others[shifted]).astype(jnp.int32)
    return numbers_from_lengths(lengths, SEQ_TOKENS)


def encoder_row(key):
    lengths = split_pool(key, ENC_TOKENS - DOCS * ENC_LEAST, DOCS, ENC_LEAST)
    return numbers_from_lengths(lengths, ENC_TOKENS)


def draw_decoder_segments(key, part):
    return jax.vmap(decoder_row)(jax.random.split(jax.random.fold_in(key, 11), SEQUENCES))


def draw_encoder_segments(key, part):
    return jax.vmap(encoder_row)(jax.random.split(jax.random.fold_in(key, 12), SEQUENCES))


def draw_buckets(key, part):
    order = jax.random.permutation(jax.random.fold_in(key, 13), SEQ_TOKENS - 1).astype(jnp.int32)
    cuts = jnp.sort(order[:BUCKETS - 1]) + 1
    distance = jnp.arange(SEQ_TOKENS, dtype=jnp.int32)
    return jnp.sum((distance[:, None] >= cuts[None, :]).astype(jnp.int32), axis=1)


def level_of(stream_key, extent, shards, low, high):
    factor_of = 1.0
    for position, blocks in shards:
        steps = jax.random.uniform(jax.random.fold_in(jax.random.fold_in(stream_key, 6), position), (blocks,), jnp.float32, low / len(shards), high / len(shards))
        factor_of = factor_of * jnp.repeat(jnp.exp(steps), extent[position] // blocks).reshape((-1,) + (1,) * (len(extent) - 1 - position))
    return factor_of


def noise(rng, shape, width, bound, shards=(), held_as=jnp.bfloat16):
    values = jax.random.normal(rng, shape, jnp.float32) * width
    if len(shards) > 0:
        values = level_of(rng, shape, shards, -0.22, 0.18) * values
    return jnp.clip(values, min=-bound, max=bound).astype(held_as)


def setup_inputs(seed: int = 0) -> dict:
    splits = jax.random.split(jax.random.key(seed), 22)
    return {
        "inputs": noise(splits[0], (SEQUENCES, SEQ_TOKENS, D), 1.0, 6.0, ((0, 8),)),
        "encoded": noise(splits[1], (SEQUENCES, ENC_TOKENS, D), 1.0, 6.0, ((0, 8),)),
        "decoder_segments": draw_decoder_segments(jax.random.fold_in(splits[21], 71), 0),
        "encoder_segments": draw_encoder_segments(jax.random.fold_in(splits[21], 71), 0),
        "buckets": draw_buckets(jax.random.fold_in(splits[21], 71), 0),
        "self_gain": jnp.clip(1.0 + 0.1 * jax.random.normal(splits[5], (D,), jnp.float32), 0.5, 1.5).astype(jnp.bfloat16),
        "self_query": noise(splits[6], (D, HEADS * HEAD_DIM), (4 * D) ** -0.5, 0.09375, ((0, 8), (1, 4))),
        "self_key": noise(splits[7], (D, KV_HEADS * HEAD_DIM), (4 * D) ** -0.5, 0.09375, ((0, 8), (1, 4))),
        "self_value": noise(splits[8], (D, KV_HEADS * HEAD_DIM), D ** -0.5, 0.1875, ((0, 8), (1, 4))),
        "self_out": noise(splits[9], (HEADS * HEAD_DIM, D), (HEADS * HEAD_DIM // 16) ** -0.5, 0.75, ((0, 4), (1, 8))),
        "position_bias": noise(splits[10], (BUCKETS, HEADS), 1.0, 4.0, ((0, 8), (1, 4))),
        "cross_gain": jnp.clip(1.0 + 0.1 * jax.random.normal(splits[11], (D,), jnp.float32), 0.5, 1.5).astype(jnp.bfloat16),
        "cross_query": noise(splits[12], (D, HEADS * HEAD_DIM), (4 * D) ** -0.5, 0.09375, ((0, 8), (1, 4))),
        "cross_key": noise(splits[13], (D, KV_HEADS * HEAD_DIM), (4 * D) ** -0.5, 0.09375, ((0, 8), (1, 4))),
        "cross_value": noise(splits[14], (D, KV_HEADS * HEAD_DIM), D ** -0.5, 0.1875, ((0, 8), (1, 4))),
        "cross_out": noise(splits[15], (HEADS * HEAD_DIM, D), (HEADS * HEAD_DIM // 16) ** -0.5, 0.75, ((0, 4), (1, 8))),
        "feed_gain": jnp.clip(1.0 + 0.1 * jax.random.normal(splits[16], (D,), jnp.float32), 0.5, 1.5).astype(jnp.bfloat16),
        "feed_gate": noise(splits[17], (D, FF), D ** -0.5, 0.1875, ((0, 8), (1, 4))),
        "feed_up": noise(splits[18], (D, FF), D ** -0.5, 0.1875, ((0, 8), (1, 4))),
        "feed_down": noise(splits[19], (FF, D), (FF // 4) ** -0.5, 0.21875, ((0, 4), (1, 8))),
        "cotangent": noise(splits[20], (SEQUENCES, SEQ_TOKENS, D), 1.0, 6.0, ((0, 8),)),
    }


epsilon = 1e-06
negative_fill = -1e+30
highest = lax.Precision.HIGHEST

@jax.custom_vjp
def low(v):
    return lax.optimization_barrier(v.astype(jnp.bfloat16)).astype(jnp.float32)

@jax.custom_vjp
def low_back(v):
    return v

def low_keep(v):
    return (low(v), None)

def low_pass(kept, grad):
    return (grad,)

def back_keep(v):
    return (v, None)

def back_low(kept, grad):
    return (low(grad),)
low.defvjp(low_keep, low_pass)
low_back.defvjp(back_keep, back_low)

def product(left, right):
    return jnp.dot(left, right, precision=highest, preferred_element_type=jnp.float32)

def normalize(state, gain):
    return state * lax.rsqrt(lax.optimization_barrier(jnp.mean(state * state, axis=-1, keepdims=True)) + epsilon) * gain

def smooth_gate(value):
    return 0.5 * value * (1.0 + jnp.tanh(0.7978845608028654 * (value + 0.044715 * value * value * value)))

def attention(query, keys, values, bias, mask):
    rows = query.shape[0]
    group = HEADS // KV_HEADS
    grouped = query.reshape(rows, KV_HEADS, group, HEAD_DIM)
    keyed = keys.reshape(keys.shape[0], KV_HEADS, HEAD_DIM)
    valued = values.reshape(values.shape[0], KV_HEADS, HEAD_DIM)
    scores = low_back(jnp.einsum('qgjd,kgd->gjqk', grouped, keyed, precision=highest))
    scores = jnp.where(mask, scores + bias, negative_fill)
    softened = jax.nn.softmax(scores, axis=-1)
    mixed = jnp.einsum('gjqk,kgd->qgjd', low(softened), valued, precision=highest)
    return mixed.reshape(rows, HEADS * HEAD_DIM)

def layer(weights, rows, memory, decoder_docs, encoder_docs, bucket_table):
    self_gain, self_query, self_key, self_value, self_out, position_bias, cross_gain, cross_query, cross_key, cross_value, cross_out, feed_gain, feed_gate, feed_up, feed_down = weights
    positions = jnp.arange(SEQ_TOKENS, dtype=jnp.int32)
    causal = (positions[:, None] >= positions[None, :]) & (decoder_docs[:, None] == decoder_docs[None, :])
    group = HEADS // KV_HEADS
    bias = jnp.transpose(position_bias[bucket_table], (2, 0, 1)).reshape(KV_HEADS, group, SEQ_TOKENS, SEQ_TOKENS)
    normed = low(normalize(rows, self_gain))
    query = low_back(low(product(normed, self_query)))
    keys = low_back(low(product(normed, self_key)))
    values = low_back(low(product(normed, self_value)))
    mixed = low_back(low(attention(query, keys, values, bias, causal)))
    first = rows + low_back(product(mixed, self_out))
    normed = low(normalize(first, cross_gain))
    query = low_back(low(product(normed, cross_query)))
    keys = low_back(low(product(memory, cross_key)))
    values = low_back(low(product(memory, cross_value)))
    crossing = decoder_docs[:, None] == encoder_docs[None, :]
    mixed = low_back(low(attention(query, keys, values, 0.0, crossing)))
    second = first + low_back(product(mixed, cross_out))
    normed = low(normalize(second, feed_gain))
    gate = low_back(product(normed, feed_gate))
    upward = low_back(product(normed, feed_up))
    hidden = low(smooth_gate(gate) * upward)
    return second + low_back(product(hidden, feed_down))

def reference(inputs, encoded, decoder_segments, encoder_segments, buckets, self_gain, self_query, self_key, self_value, self_out, position_bias, cross_gain, cross_query, cross_key, cross_value, cross_out, feed_gain, feed_gate, feed_up, feed_down, cotangent):
    weights = tuple((item.astype(jnp.float32) for item in (self_gain, self_query, self_key, self_value, self_out, position_bias, cross_gain, cross_query, cross_key, cross_value, cross_out, feed_gain, feed_gate, feed_up, feed_down)))
    positions = jnp.arange(SEQ_TOKENS, dtype=jnp.int32)
    distance = jnp.clip(positions[:, None] - positions[None, :], 0, SEQ_TOKENS - 1).astype(jnp.int32)
    bucket_table = buckets[distance].astype(jnp.int32)

    def one_sequence(totals, item):
        rows, memory, decoder_docs, encoder_docs, upstream = item

        def forward(params, state, encoder_rows):
            return layer(params, state, encoder_rows, decoder_docs, encoder_docs, bucket_table)
        result, pull = jax.vjp(forward, weights, rows.astype(jnp.float32), memory.astype(jnp.float32))
        grad_weights, grad_rows, grad_memory = pull(upstream.astype(jnp.float32))
        totals = jax.tree.map(jnp.add, totals, grad_weights)
        return (totals, (result.astype(jnp.bfloat16), grad_rows.astype(jnp.bfloat16), grad_memory.astype(jnp.bfloat16)))
    start = tuple((jnp.zeros(item.shape, jnp.float32) for item in weights))
    totals, stacked = lax.scan(one_sequence, start, (inputs, encoded, decoder_segments, encoder_segments, cotangent))
    return (stacked[0], stacked[1], stacked[2], totals[0], totals[1], totals[2], totals[3], totals[4], totals[5], totals[6], totals[7], totals[8], totals[9], totals[10], totals[11], totals[12], totals[13], totals[14])
```

```python
import functools

import jax
import jax.numpy as jnp
from jax import lax
from jax.experimental import pallas as pl
from jax.experimental.pallas import tpu as pltpu
from jax.sharding import PartitionSpec as P

HEAD_DIM = 64
TILE_Q = 128
TILE_K = 256
EPSILON = 1e-06
NEGATIVE = -1e30
HIGHEST = lax.Precision.HIGHEST
F32 = jnp.float32
BF16 = jnp.bfloat16


def dot(left, right, dims, precision=None):
    return lax.dot_general(
        left, right, ((dims[0], dims[1]), ((), ())), precision=precision, preferred_element_type=F32
    )


def mm(left, right):
    return dot(left, right, ((1,), (0,)))


def mm_nt(left, right):
    return dot(left, right, ((1,), (1,)))


def mm_tn(left, right):
    return dot(left, right, ((0,), (0,)))


def round_up(value, unit):
    return (value + unit - 1) // unit * unit


def skew(row, height):
    wide = jnp.broadcast_to(row, (height, row.shape[1]))
    return pltpu.roll(wide, 0, axis=1, stride=1, stride_axis=0)


def stacked(tile, g):
    base = 2 * HEAD_DIM * g
    return jnp.concatenate(
        [tile[:, base : base + HEAD_DIM], tile[:, base + HEAD_DIM : base + 2 * HEAD_DIM]], axis=0
    )


def unstacked(pair):
    return jnp.concatenate([pair[:TILE_Q], pair[TILE_Q:]], axis=1)


def twice(row):
    return jnp.concatenate([row, row], axis=1)


def tile_mask(biased, mask_ref, keys_ref, a, u0):
    cols = pl.ds(pl.multiple_of(a * TILE_Q, TILE_Q), TILE_Q)
    row = twice(mask_ref[0:1, cols])
    if biased:
        index = lax.broadcasted_iota(jnp.int32, (TILE_K, 2 * TILE_Q), 0)
        return index >= row - u0
    keys = keys_ref[pl.ds(u0, TILE_K), :]
    return jnp.concatenate([keys, keys], axis=1) == row


def tile_bias(strip_ref, g, off):
    lanes = pl.ds(off, TILE_Q)
    return jnp.concatenate([strip_ref[2 * g, :, lanes], strip_ref[2 * g + 1, :, lanes]], axis=1)


def forward_kernel(biased, front, lead, lo_ref, hi_ref, *refs):
    if biased:
        q_ref, k_ref, v_ref, mask_ref, vec_ref, o_ref, lse_ref, strip, m_s, l_s, acc_s = refs
        keys_ref = None
        for h in range(4):
            strip[h] = skew(vec_ref[0, h : h + 1, :], TILE_K)
    else:
        q_ref, k_ref, v_ref, mask_ref, keys_ref, o_ref, lse_ref, m_s, l_s, acc_s = refs
    tiles = q_ref.shape[0] // TILE_Q

    def q_tile(a, carry):
        rows = pl.ds(pl.multiple_of(a * TILE_Q, TILE_Q), TILE_Q)
        qt = q_ref[rows, :]
        q2 = [stacked(qt, g) for g in range(2)]
        m_s[...] = jnp.full_like(m_s, NEGATIVE)
        l_s[...] = jnp.zeros_like(l_s)
        acc_s[...] = jnp.zeros_like(acc_s)

        def k_tile(m, carry):
            u0 = pl.multiple_of(m * TILE_K, TILE_K)
            kt = k_ref[pl.ds(u0, TILE_K), :]
            vt = v_ref[pl.ds(u0, TILE_K), :]
            valid = tile_mask(biased, mask_ref, keys_ref, a, u0)
            for g in range(2):
                head = slice(HEAD_DIM * g, HEAD_DIM * (g + 1))
                s = mm_nt(kt[:, head], q2[g])
                if biased:
                    off = pl.multiple_of(a * TILE_Q - m * TILE_K + front + lead, TILE_Q)
                    s = s + tile_bias(strip, g, off)
                s = jnp.where(valid, s, NEGATIVE)
                top = m_s[g : g + 1, :]
                new = jnp.maximum(top, jnp.max(s, axis=0, keepdims=True))
                alpha = jnp.exp(top - new)
                p = jnp.exp(s - new)
                m_s[g : g + 1, :] = new
                l_s[g : g + 1, :] = l_s[g : g + 1, :] * alpha + jnp.sum(p, axis=0, keepdims=True)
                acc_s[g] = acc_s[g] * alpha + mm_tn(vt[:, head], p.astype(BF16))
            return carry

        lax.fori_loop(lo_ref[a], hi_ref[a], k_tile, 0)
        for g in range(2):
            total = l_s[g : g + 1, :]
            mixed = (acc_s[g] / total).T
            o_ref[rows, 2 * HEAD_DIM * g : 2 * HEAD_DIM * (g + 1)] = unstacked(mixed).astype(BF16)
            lse = m_s[g : g + 1, :] + jnp.log(total)
            lse_ref[0, 2 * g : 2 * g + 1, rows] = lse[:, :TILE_Q]
            lse_ref[0, 2 * g + 1 : 2 * g + 2, rows] = lse[:, TILE_Q:]
        return carry

    lax.fori_loop(0, tiles, q_tile, 0)


def backward_kernel(biased, front, lead, lo_ref, hi_ref, *refs):
    if biased:
        (
            q_ref, k_ref, v_ref, o_ref, do_ref, lse_ref, mask_ref, vec_ref,
            dq_ref, dk_ref, dv_ref, dist_ref, strip, slope, dk_s, dv_s, dq_s,
        ) = refs
        keys_ref = None
        for h in range(4):
            strip[h] = skew(vec_ref[0, h : h + 1, :], TILE_K)
        slope[...] = jnp.zeros_like(slope)
    else:
        (
            q_ref, k_ref, v_ref, o_ref, do_ref, lse_ref, mask_ref, keys_ref,
            dq_ref, dk_ref, dv_ref, dk_s, dv_s, dq_s,
        ) = refs
    tiles = q_ref.shape[0] // TILE_Q
    dk_s[...] = jnp.zeros_like(dk_s)
    dv_s[...] = jnp.zeros_like(dv_s)

    def q_tile(a, carry):
        rows = pl.ds(pl.multiple_of(a * TILE_Q, TILE_Q), TILE_Q)
        qt = q_ref[rows, :]
        ot = o_ref[rows, :]
        dot_ = do_ref[rows, :]
        q2 = [stacked(qt, g) for g in range(2)]
        do2 = [stacked(dot_, g) for g in range(2)]
        lse = []
        delta = []
        for g in range(2):
            both = stacked(ot, g).astype(F32) * do2[g].astype(F32)
            delta.append(jnp.sum(both.T, axis=0, keepdims=True))
            lse.append(
                jnp.concatenate(
                    [lse_ref[0, 2 * g : 2 * g + 1, rows], lse_ref[0, 2 * g + 1 : 2 * g + 2, rows]],
                    axis=1,
                )
            )
        dq_s[...] = jnp.zeros_like(dq_s)

        def k_tile(m, carry):
            u0 = pl.multiple_of(m * TILE_K, TILE_K)
            keys = pl.ds(u0, TILE_K)
            kt = k_ref[keys, :]
            vt = v_ref[keys, :]
            valid = tile_mask(biased, mask_ref, keys_ref, a, u0)
            grad_k = []
            grad_v = []
            for g in range(2):
                head = slice(HEAD_DIM * g, HEAD_DIM * (g + 1))
                s = mm_nt(kt[:, head], q2[g])
                if biased:
                    off = pl.multiple_of(a * TILE_Q - m * TILE_K + front + lead, TILE_Q)
                    s = s + tile_bias(strip, g, off)
                p = jnp.exp(jnp.where(valid, s - lse[g], NEGATIVE))
                dp = mm_nt(vt[:, head], do2[g])
                ds = p * (dp - delta[g])
                low = ds.astype(BF16)
                if biased:
                    lanes = pl.ds(off, TILE_Q)
                    slope[2 * g, :, lanes] += ds[:, :TILE_Q]
                    slope[2 * g + 1, :, lanes] += ds[:, TILE_Q:]
                grad_v.append(mm(p.astype(BF16), do2[g]))
                grad_k.append(mm(low, q2[g]))
                dq_s[g] += mm_tn(kt[:, head], low)
            dk_s[keys, :] += jnp.concatenate(grad_k, axis=1)
            dv_s[keys, :] += jnp.concatenate(grad_v, axis=1)
            return carry

        lax.fori_loop(lo_ref[a], hi_ref[a], k_tile, 0)
        for g in range(2):
            dq_ref[rows, 2 * HEAD_DIM * g : 2 * HEAD_DIM * (g + 1)] = unstacked(dq_s[g].T).astype(
                BF16
            )
        return carry

    lax.fori_loop(0, tiles, q_tile, 0)
    dk_ref[...] = dk_s[...].astype(BF16)
    dv_ref[...] = dv_s[...].astype(BF16)
    if biased:
        width = slope.shape[2]
        for h in range(4):
            part = slope[h]
            height = TILE_K
            while height > 8:
                height //= 2
                part = part[:height] + pltpu.roll(part[height:], width - height, axis=1)
            row = part[0:1]
            for j in range(1, 8):
                row = row + pltpu.roll(part, width - j, axis=1)[j : j + 1]
            dist_ref[0, h : h + 1, :] = row


def spec(shape, index):
    return pl.BlockSpec(shape, index)


def attention_call(kernel, biased, outs, scratch, args, bounds, front, lead, name, flops):
    rows = args[0].shape[0]
    steps = args[1].shape[1] // (2 * HEAD_DIM)

    def column(array, lanes):
        return spec((array.shape[0], lanes), lambda i, *_: (0, i))

    specs = []
    for array, kind in args_kinds(args, biased, kernel):
        if kind == "wide":
            specs.append(column(array, 4 * HEAD_DIM))
        elif kind == "key":
            specs.append(column(array, 2 * HEAD_DIM))
        elif kind == "head":
            specs.append(spec((1,) + array.shape[1:], lambda i, *_: (i, 0, 0)))
        else:
            specs.append(spec(array.shape, lambda i, *_: (0, 0)))
    out_specs = []
    for item, kind in outs:
        if kind == "wide":
            out_specs.append(column(item, 4 * HEAD_DIM))
        elif kind == "key":
            out_specs.append(column(item, 2 * HEAD_DIM))
        else:
            out_specs.append(spec((1,) + item.shape[1:], lambda i, *_: (i, 0, 0)))
    return pl.pallas_call(
        functools.partial(kernel, biased, front, lead),
        out_shape=[item for item, _ in outs],
        grid_spec=pltpu.PrefetchScalarGridSpec(
            num_scalar_prefetch=2,
            grid=(steps,),
            in_specs=specs,
            out_specs=out_specs,
            scratch_shapes=scratch,
        ),
        compiler_params=pltpu.CompilerParams(vmem_limit_bytes=56 << 20),
        cost_estimate=pl.CostEstimate(flops=flops, bytes_accessed=16 << 20, transcendentals=0),
        name=name,
    )(*bounds, *args)


def args_kinds(args, biased, kernel):
    tail = ["flat", "head" if biased else "flat"]
    if kernel is forward_kernel:
        kinds = ["wide", "key", "key"] + tail
    else:
        kinds = ["wide", "key", "key", "wide", "wide", "head"] + tail
    return list(zip(args, kinds))


def attend_forward(q, k, v, mask, extra, bounds, front, lead, biased, name):
    rows = q.shape[0]
    steps = k.shape[1] // (2 * HEAD_DIM)
    outs = [
        (jax.ShapeDtypeStruct(q.shape, BF16), "wide"),
        (jax.ShapeDtypeStruct((steps, 4, rows), F32), "head"),
    ]
    scratch = []
    if biased:
        scratch.append(pltpu.VMEM((4, TILE_K, extra.shape[2]), F32))
    scratch += [
        pltpu.VMEM((2, 2 * TILE_Q), F32),
        pltpu.VMEM((2, 2 * TILE_Q), F32),
        pltpu.VMEM((2, HEAD_DIM, 2 * TILE_Q), F32),
    ]
    flops = 4 * rows * k.shape[0] * q.shape[1]
    return attention_call(
        forward_kernel, biased, outs, scratch, (q, k, v, mask, extra), bounds, front, lead, name, flops
    )


def attend_backward(q, k, v, o, do, lse, mask, extra, bounds, front, lead, biased, name):
    rows = q.shape[0]
    keys = k.shape[0]
    outs = [
        (jax.ShapeDtypeStruct(q.shape, BF16), "wide"),
        (jax.ShapeDtypeStruct(k.shape, BF16), "key"),
        (jax.ShapeDtypeStruct(k.shape, BF16), "key"),
    ]
    scratch = []
    if biased:
        outs.append((jax.ShapeDtypeStruct(extra.shape, F32), "head"))
        scratch += [pltpu.VMEM((4, TILE_K, extra.shape[2]), F32)] * 2
    scratch += [
        pltpu.VMEM((keys, 2 * HEAD_DIM), F32),
        pltpu.VMEM((keys, 2 * HEAD_DIM), F32),
        pltpu.VMEM((2, HEAD_DIM, 2 * TILE_Q), F32),
    ]
    flops = 10 * rows * keys * q.shape[1]
    return attention_call(
        backward_kernel, biased, outs, scratch, (q, k, v, o, do, lse, mask, extra), bounds, front,
        lead, name, flops,
    )


MESH = pl.DeviceIdType.MESH


class Place:
    def __init__(self, mp):
        self.mp = mp
        self.i = lax.axis_index("dp")
        self.z = lax.axis_index("mp")
        core = lax.rem(self.i, 2)
        across = lax.rem(lax.div(self.i, 2), 2)
        up = lax.div(self.i, 4)
        self.core, self.across, self.up = core, across, up
        self.ic = self.i + 1 - 2 * core
        self.ix = self.i + 2 - 4 * across
        self.iy = self.i + 4 - 8 * up
        self.ixy = self.ix + 4 - 8 * up


def enter(place):
    barrier = pltpu.get_barrier_semaphore()
    z, mp = place.z, place.mp
    for near in (place.ic, place.ix, place.iy):
        pl.semaphore_signal(barrier, 1, device_id=(near, z), device_id_type=MESH)

    @pl.when(z > 0)
    def _():
        pl.semaphore_signal(barrier, 1, device_id=(place.i, z - 1), device_id_type=MESH)

    @pl.when(z < mp - 1)
    def _():
        pl.semaphore_signal(barrier, 1, device_id=(place.i, z + 1), device_id_type=MESH)

    low = jnp.minimum(z, 1)
    high = jnp.minimum(mp - 1 - z, 1)
    pl.semaphore_wait(barrier, 3 + low + high)


def region(ref, i, z, shard):
    if len(ref.shape) == 4:
        return ref.at[z, i]
    rows, cols = shard
    return ref.at[pl.ds(pl.multiple_of(z * rows, rows), rows), pl.ds(pl.multiple_of(i * cols, cols), cols)]


def gather_steps(place, shards, outs, send, recv, local):
    mp, i, z = place.mp, place.i, place.z
    units = range(len(shards))

    def here(u, i2, z2):
        return region(outs[u], i2, z2, shards[u].shape)

    def copy(u, kind, i2, z2, to, src=None):
        spot = here(u, i2, z2)
        return pltpu.make_async_remote_copy(
            src_ref=spot if src is None else src, dst_ref=spot, send_sem=send.at[u, kind, z2],
            recv_sem=recv.at[u, kind, z2], device_id=to, device_id_type=MESH)

    def route(u, z2):
        odd = lax.rem(z2 + u, 2)
        first = place.ix + odd * (place.iy - place.ix)
        second = place.iy + odd * (place.ix - place.iy)
        return odd, first, second

    slots = [(0, 0)] + [(d, s) for d in range(1, mp) for s in (0, 1)]

    def when(slot, f):
        d, s = slot
        z2 = z if d == 0 else (z - d if s == 0 else z + d)
        if d == 0:
            f(z2)
        elif s == 0:
            pl.when(z >= d)(lambda: f(z2))
        else:
            pl.when(z < mp - d)(lambda: f(z2))

    def stage1(slot):
        d, s = slot

        def run(z2):
            for u in units:
                src = shards[u] if d == 0 else None
                if d > 0:
                    kind = 0 if s == 0 else 1
                    copy(u, kind, i, z2, (i, z)).wait_recv()
                if d == 0 or s == 0:
                    pl.when(z < mp - 1)(lambda u=u, src=src: copy(u, 0, i, z2, (i, z + 1), src).start())
                if d == 0 or s == 1:
                    pl.when(z > 0)(lambda u=u, src=src: copy(u, 1, i, z2, (i, z - 1), src).start())
                copy(u, 2, i, z2, (place.ix, z), src).start()
                copy(u, 3, i, z2, (place.iy, z), src).start()
                copy(u, 5, i, z2, (place.ic, z), src).start()
                if d == 0:
                    pltpu.make_async_copy(shards[u], here(u, i, z), local.at[u]).start()

        when(slot, run)

    def stage2(slot):
        def run(z2):
            for u in units:
                odd, first, second = route(u, z2)
                kind = 2 + odd
                spot = here(u, first, z2)
                pltpu.make_async_remote_copy(src_ref=spot, dst_ref=spot, send_sem=send.at[u, kind, z2],
                    recv_sem=recv.at[u, kind, z2], device_id=(first, z), device_id_type=MESH).wait_recv()
                copy(u, 4, first, z2, (second, z)).start()
                copy(u, 6, first, z2, (place.ic, z)).start()

        when(slot, run)

    def stage3(slot):
        def run(z2):
            for u in units:
                odd, first, second = route(u, z2)
                kind = 3 - odd
                spot = here(u, second, z2)
                pltpu.make_async_remote_copy(src_ref=spot, dst_ref=spot, send_sem=send.at[u, kind, z2],
                    recv_sem=recv.at[u, kind, z2], device_id=(second, z), device_id_type=MESH).wait_recv()
                copy(u, 7, second, z2, (place.ic, z)).start()
                copy(u, 4, place.ixy, z2, (second, z)).wait_recv()
                copy(u, 8, place.ixy, z2, (place.ic, z)).start()

        when(slot, run)

    def other(i2):
        return i2 + place.ic - i

    def finish(slot):
        d, s = slot

        def run(z2):
            for u in units:
                odd, first, second = route(u, z2)
                for kind, i2 in ((5, i), (6, first), (7, second), (8, place.ixy)):
                    copy(u, kind, other(i2), z2, (place.ic, z)).wait_recv()
                if d == 0 or s == 0:
                    pl.when(z < mp - 1)(lambda u=u: copy(u, 0, i, z2, (i, z)).wait_send())
                if d == 0 or s == 1:
                    pl.when(z > 0)(lambda u=u: copy(u, 1, i, z2, (i, z)).wait_send())
                for kind in range(2, 9):
                    copy(u, kind, i, z2, (i, z)).wait_send()
                if d == 0:
                    pltpu.make_async_copy(shards[u], here(u, i, z), local.at[u]).wait()

        when(slot, run)

    steps = []
    n = len(slots)
    for k in range(n + 2):
        if k < n:
            steps.append(functools.partial(stage1, slots[k]))
        if 0 <= k - 1 < n:
            steps.append(functools.partial(stage2, slots[k - 1]))
        if 0 <= k - 2 < n:
            steps.append(functools.partial(stage3, slots[k - 2]))
    for slot in slots:
        steps.append(functools.partial(finish, slot))
    return steps


def gather_shape(shard, kind, dp, mp):
    rows, cols = shard.shape
    if kind == "by_dp":
        return jax.ShapeDtypeStruct((mp, dp, rows, cols), shard.dtype)
    return jax.ShapeDtypeStruct((mp * rows, dp * cols), shard.dtype)


def gather_kernel(count, mp, *refs):
    shards, outs, (send, recv, local) = refs[:count], refs[count:2 * count], refs[2 * count:]
    place = Place(mp)
    enter(place)
    for step in gather_steps(place, shards, outs, send, recv, local):
        step()


def gather_weights(shards, kinds, dp, mp, cid, name):
    count = len(shards)
    any_space = pl.BlockSpec(memory_space=pl.ANY)
    sems = pltpu.SemaphoreType.DMA((count, 9, mp))
    return pl.pallas_call(
        functools.partial(gather_kernel, count, mp),
        out_shape=[gather_shape(s, k, dp, mp) for s, k in zip(shards, kinds)],
        in_specs=[any_space] * count, out_specs=[any_space] * count,
        scratch_shapes=[sems, sems, pltpu.SemaphoreType.DMA((count,))],
        compiler_params=pltpu.CompilerParams(collective_id=cid, has_side_effects=True),
        name=name,
    )(*shards)


def inverse_rms(state):
    return lax.rsqrt(jnp.mean(state * state, axis=-1, keepdims=True) + EPSILON)


def norm_back(state, gain, grad_normed):
    scale = inverse_rms(state)
    weighted = grad_normed * gain
    grad_gain = jnp.sum(grad_normed * state * scale, axis=0, keepdims=True)
    inner = jnp.mean(weighted * state, axis=-1, keepdims=True)
    return scale * weighted - state * (scale * scale * scale) * inner, grad_gain


def chunked(total, size, run):
    def once(n, carry):
        run(pl.multiple_of(n * size, size))
        return carry

    lax.fori_loop(0, total // size, once, 0)


def row_chunk(rows):
    for size in (272, 256, 128):
        if rows % size == 0:
            return size
    return rows


def full(array):
    return pl.BlockSpec(array.shape, lambda j: (0,) * len(array.shape))


def lead_block(array):
    return pl.BlockSpec((1,) + array.shape[1:], lambda j: (j,) + (0,) * (len(array.shape) - 1))


def col_block(array, parts):
    return pl.BlockSpec((array.shape[0], array.shape[1] // parts), lambda j: (0, j))


def row_block(array, parts):
    return pl.BlockSpec((array.shape[0] // parts, array.shape[1]), lambda j: (j, 0))


def kernel_call(body, name, steps, ins, outs, scratch, flops):
    return pl.pallas_call(
        body,
        grid=(steps,),
        out_shape=[jax.ShapeDtypeStruct(a.shape, a.dtype) for a, _ in outs],
        in_specs=[s for _, s in ins],
        out_specs=[s for _, s in outs],
        scratch_shapes=scratch,
        compiler_params=pltpu.CompilerParams(vmem_limit_bytes=60 << 20),
        cost_estimate=pl.CostEstimate(flops=flops, bytes_accessed=16 << 20, transcendentals=0),
        name=name,
    )(*[a for a, _ in ins])


def shape(dims, dtype=BF16):
    return jax.ShapeDtypeStruct(dims, dtype)


def project_kernel(front, x_ref, gain_ref, w_ref, q_ref, k_ref, v_ref, n_ref, normed):
    reach = x_ref.shape[0]
    padded, qcols = q_ref.shape
    kcols = k_ref.shape[1]
    rows = n_ref.shape[0]
    size = row_chunk(reach)

    @pl.when(pl.program_id(0) == 0)
    def _():
        def norm_rows(at):
            x = x_ref[pl.ds(at, size), :].astype(F32)
            normed[pl.ds(at, size), :] = (x * inverse_rms(x) * gain_ref[...]).astype(BF16)

        chunked(reach, size, norm_rows)
        n_ref[...] = normed[front : front + rows, :]

    q_ref[...] = mm(normed[front : front + padded, :], w_ref[0, :, :qcols]).astype(BF16)

    def keys(at):
        kv = mm(normed[pl.ds(at, size), :], w_ref[0, :, qcols:]).astype(BF16)
        k_ref[pl.ds(at, size), :] = kv[:, :kcols]
        v_ref[pl.ds(at, size), :] = kv[:, kcols:]

    chunked(reach, size, keys)


def self_project(x, gain, w, front, padded, rows):
    reach, width = x.shape
    groups, _, cols = w.shape
    q, k = shape((padded, groups * cols // 2)), shape((reach, groups * cols // 4))
    n = shape((rows, width))
    return kernel_call(
        functools.partial(project_kernel, front), "self_project", groups,
        [(x, full(x)), (gain, full(gain)), (w, lead_block(w))],
        [(q, col_block(q, groups)), (k, col_block(k, groups)), (k, col_block(k, groups)), (n, full(n))],
        [pltpu.VMEM(x.shape, BF16)], 2 * (reach + padded) * width * groups * cols // 2,
    )


def middle_kernel(o_ref, wo_ref, x_ref, gain_ref, m_ref, w_ref, h_ref, n_ref, q_ref, k_ref, v_ref):
    rows = x_ref.shape[0]
    qcols = q_ref.shape[1]
    kcols = k_ref.shape[1]
    size = row_chunk(rows)

    @pl.when(pl.program_id(0) == 0)
    def _():
        def state(at):
            some = pl.ds(at, size)
            h = x_ref[some, :].astype(F32) + mm(o_ref[some, :], wo_ref[...])
            h_ref[some, :] = h
            n_ref[some, :] = (h * inverse_rms(h) * gain_ref[...]).astype(BF16)

        chunked(rows, size, state)

    q_ref[0:rows, :] = mm(n_ref[...], w_ref[0, :, :qcols]).astype(BF16)
    q_ref[rows:, :] = jnp.zeros((q_ref.shape[0] - rows, qcols), BF16)
    kv = mm(m_ref[...], w_ref[0, :, qcols:]).astype(BF16)
    k_ref[...] = kv[:, :kcols]
    v_ref[...] = kv[:, kcols:]


def cross_project(o, wo, x, gain, memory, w):
    rows, width = x.shape
    groups, _, cols = w.shape
    h, n = shape(x.shape, F32), shape(x.shape)
    q = shape((o.shape[0], groups * cols // 2))
    k = shape((memory.shape[0], groups * cols // 4))
    return kernel_call(
        middle_kernel, "cross_project", groups,
        [(o, full(o)), (wo, full(wo)), (x, full(x)), (gain, full(gain)), (memory, full(memory)),
         (w, lead_block(w))],
        [(h, full(h)), (n, full(n)), (q, col_block(q, groups)), (k, col_block(k, groups)),
         (k, col_block(k, groups))],
        [], 6 * rows * width * width,
    )


def gate_parts(value):
    square = value * value
    inner = jnp.tanh(0.7978845608028654 * (value + 0.044715 * square * value))
    half = 0.5 * (1.0 + inner)
    slope = 0.7978845608028654 * (1.0 + 3.0 * 0.044715 * square)
    return value * half, half + 0.5 * value * (1.0 - inner * inner) * slope


def feed_kernel(
    o_ref, wo_ref, h1_ref, gain_ref, up_ref, wg_ref, wu_ref, wd_ref,
    out_ref, g2_ref, gain_out, gwg_ref, gwu_ref, gwd_ref, do_ref, gwo_ref,
    h2, normed, total, back, hidden_s, dgate_s, dup_s,
):
    rows, width = h1_ref.shape
    j = pl.program_id(0)
    size = row_chunk(rows)

    @pl.when(j == 0)
    def _():
        def state(at):
            some = pl.ds(at, size)
            h = h1_ref[some, :] + mm(o_ref[some, :], wo_ref[...])
            h2[some, :] = h
            normed[some, :] = (h * inverse_rms(h) * gain_ref[...]).astype(BF16)
            total[some, :] = h
            back[some, :] = jnp.zeros((size, width), F32)

        chunked(rows, size, state)

    def hidden_rows(at):
        some = pl.ds(at, size)
        n = normed[some, :]
        g = up_ref[some, :]
        gate = mm(n, wg_ref[0])
        up = mm(n, wu_ref[0])
        grad_hidden = mm_nt(g, wd_ref[...])
        active, pull = gate_parts(gate)
        hidden = (active * up).astype(BF16)
        grad_gate = (grad_hidden * up * pull).astype(BF16)
        grad_up = (grad_hidden * active).astype(BF16)
        hidden_s[some, :] = hidden
        dgate_s[some, :] = grad_gate
        dup_s[some, :] = grad_up
        total[some, :] += mm(hidden, wd_ref[...])
        back[some, :] += mm_nt(grad_gate, wg_ref[0]) + mm_nt(grad_up, wu_ref[0])

    chunked(rows, size, hidden_rows)

    def weight_rows(at):
        some = pl.ds(at, 128)
        n = normed[:, some]
        gwg_ref[0, some, :] = mm_tn(n, dgate_s[...]).astype(BF16)
        gwu_ref[0, some, :] = mm_tn(n, dup_s[...]).astype(BF16)
        gwd_ref[:, some] = mm_tn(hidden_s[...], up_ref[:, some]).astype(BF16)

    chunked(width, 128, weight_rows)

    @pl.when(j == pl.num_programs(0) - 1)
    def _():
        gain_out[...] = jnp.zeros_like(gain_out)
        do_ref[...] = jnp.zeros_like(do_ref)

        def finish(at):
            some = pl.ds(at, size)
            out_ref[some, :] = total[some, :].astype(BF16)
            change, grad_gain = norm_back(h2[some, :], gain_ref[...], back[some, :])
            gain_out[...] += grad_gain
            g2 = up_ref[some, :].astype(F32) + change
            g2_ref[some, :] = g2
            low = g2.astype(BF16)
            normed[some, :] = low
            do_ref[some, :] = mm_nt(low, wo_ref[...]).astype(BF16)

        chunked(rows, size, finish)

        def out_rows(at):
            some = pl.ds(at, 256)
            gwo_ref[some, :] = mm_tn(o_ref[0:rows, some], normed[...]).astype(BF16)

        chunked(width, 256, out_rows)


def feed(o, wo, h1, gain, upstream, wg, wu, wd):
    rows, width = h1.shape
    groups, _, cols = wg.shape
    out, g2, gg = shape(h1.shape), shape(h1.shape, F32), shape((1, width), F32)
    return kernel_call(
        feed_kernel, "feed", groups,
        [(o, full(o)), (wo, full(wo)), (h1, full(h1)), (gain, full(gain)), (upstream, full(upstream)),
         (wg, lead_block(wg)), (wu, lead_block(wu)), (wd, row_block(wd, groups))],
        [(out, full(out)), (g2, full(g2)), (gg, full(gg)), (wg, lead_block(wg)), (wu, lead_block(wu)),
         (wd, row_block(wd, groups)), (o, full(o)), (wo, full(wo))],
        [pltpu.VMEM((rows, width), F32), pltpu.VMEM((rows, width), BF16), pltpu.VMEM((rows, width), F32),
         pltpu.VMEM((rows, width), F32)] + [pltpu.VMEM((rows, cols), BF16)] * 3,
        18 * rows * width * groups * cols,
    )


def back_kernel(
    dq_ref, w_ref, n_ref, h_ref, gain_ref, g2_ref, wo_ref, o_ref,
    gw_ref, g1_ref, gain_out, do_ref, gwo_ref, back, low_s,
):
    rows, width = h_ref.shape
    qcols = dq_ref.shape[1]
    j = pl.program_id(0)
    size = row_chunk(rows)

    @pl.when(j == 0)
    def _():
        back[...] = jnp.zeros_like(back)

    back[...] += mm_nt(dq_ref[0:rows, :], w_ref[0, :, :qcols])

    def weight_rows(at):
        some = pl.ds(at, 256)
        gw_ref[0, some, :] = mm_tn(n_ref[:, some], dq_ref[0:rows, :]).astype(BF16)

    chunked(width, 256, weight_rows)

    @pl.when(j == pl.num_programs(0) - 1)
    def _():
        gain_out[...] = jnp.zeros_like(gain_out)
        do_ref[...] = jnp.zeros_like(do_ref)

        def finish(at):
            some = pl.ds(at, size)
            change, grad_gain = norm_back(h_ref[some, :], gain_ref[...], back[some, :])
            gain_out[...] += grad_gain
            g1 = g2_ref[some, :] + change
            g1_ref[some, :] = g1
            low = g1.astype(BF16)
            low_s[some, :] = low
            do_ref[some, :] = mm_nt(low, wo_ref[...]).astype(BF16)

        chunked(rows, size, finish)

        def out_rows(at):
            some = pl.ds(at, 256)
            gwo_ref[some, :] = mm_tn(o_ref[0:rows, some], low_s[...]).astype(BF16)

        chunked(width, 256, out_rows)


def cross_back(dq, w, n, h, gain, g2, wo, o):
    rows, width = h.shape
    groups, _, cols = w.shape
    gw = shape((groups, width, cols // 2))
    gg = shape((1, width), F32)
    return kernel_call(
        back_kernel, "cross_back", groups,
        [(dq, col_block(dq, groups)), (w, lead_block(w)), (n, full(n)), (h, full(h)), (gain, full(gain)),
         (g2, full(g2)), (wo, full(wo)), (o, full(o))],
        [(gw, lead_block(gw)), (g2, full(g2)), (gg, full(gg)), (o, full(o)), (wo, full(wo))],
        [pltpu.VMEM((rows, width), F32), pltpu.VMEM((rows, width), BF16)],
        8 * rows * width * width,
    )


def memory_kernel(dk_ref, dv_ref, w_ref, m_ref, gw_ref, gm_ref, back):
    j = pl.program_id(0)
    qcols = w_ref.shape[2] // 2
    kcols = qcols // 2

    @pl.when(j == 0)
    def _():
        back[...] = jnp.zeros_like(back)

    both = jnp.concatenate([dk_ref[...], dv_ref[...]], axis=1)
    back[...] += mm_nt(both, w_ref[0, :, qcols:])
    gw_ref[0] = mm_tn(m_ref[...], both).astype(BF16)

    @pl.when(j == pl.num_programs(0) - 1)
    def _():
        gm_ref[...] = back[...].astype(BF16)


def memory_back(dk, dv, w, memory):
    groups, width, cols = w.shape
    gw = shape((groups, width, cols // 2))
    return kernel_call(
        memory_kernel, "memory_back", groups,
        [(dk, col_block(dk, groups)), (dv, col_block(dv, groups)), (w, lead_block(w)), (memory, full(memory))],
        [(gw, lead_block(gw)), (memory, full(memory))],
        [pltpu.VMEM(memory.shape, F32)], 4 * memory.shape[0] * width * width,
    )


def last_kernel(
    dq_ref, dk_ref, dv_ref, w_ref, n_ref, x_ref, gain_ref, g1_ref,
    gwq_ref, gwkv_ref, gx_ref, gain_out, back,
):
    rows, width = x_ref.shape
    j = pl.program_id(0)
    size = row_chunk(rows)

    @pl.when(j == 0)
    def _():
        back[...] = jnp.zeros_like(back)

    dq = dq_ref[0:rows, :]
    dkv = jnp.concatenate([dk_ref[...], dv_ref[...]], axis=1)
    both = jnp.concatenate([dq, dkv], axis=1)
    back[...] += mm_nt(both, w_ref[0])

    def weight_rows(at):
        some = pl.ds(at, 256)
        gwq_ref[0, some, :] = mm_tn(n_ref[:, some], dq).astype(BF16)
        gwkv_ref[0, some, :] = mm_tn(n_ref[:, some], dkv).astype(BF16)

    chunked(width, 256, weight_rows)

    @pl.when(j == pl.num_programs(0) - 1)
    def _():
        gain_out[...] = jnp.zeros_like(gain_out)

        def finish(at):
            some = pl.ds(at, size)
            change, grad_gain = norm_back(x_ref[some, :].astype(F32), gain_ref[...], back[some, :])
            gain_out[...] += grad_gain
            gx_ref[some, :] = (g1_ref[some, :] + change).astype(BF16)

        chunked(rows, size, finish)


def self_back(dq, dk, dv, w, n, x, gain, g1):
    rows, width = x.shape
    groups, _, cols = w.shape
    gw = shape((groups, width, cols // 2))
    gg = shape((1, width), F32)
    return kernel_call(
        last_kernel, "self_back", groups,
        [(dq, col_block(dq, groups)), (dk, col_block(dk, groups)), (dv, col_block(dv, groups)),
         (w, lead_block(w)), (n, full(n)), (x, full(x)), (gain, full(gain)), (g1, full(g1))],
        [(gw, lead_block(gw)), (gw, lead_block(gw)), (x, full(x)), (gg, full(gg))],
        [pltpu.VMEM((rows, width), F32)],
        8 * rows * width * width,
    )


def gather(shard, dims):
    for axis, name in dims:
        shard = lax.all_gather(shard, name, axis=axis, tiled=True)
    return shard


ROWS_BY_DP = ((0, "dp"), (1, "mp"))
ROWS_BY_MP = ((1, "dp"), (0, "mp"))


def scatter(grad, dims):
    for axis, name in dims:
        grad = lax.psum_scatter(grad, name, scatter_dimension=axis, tiled=True)
    return grad.astype(F32)


def grouped(weight, groups):
    rows, cols = weight.shape
    return weight.reshape(rows, groups, cols // groups).transpose(1, 0, 2)


def ungrouped(weight):
    groups, rows, cols = weight.shape
    return weight.transpose(1, 0, 2).reshape(rows, groups * cols)


def body(
    inputs,
    encoded,
    decoder_segments,
    encoder_segments,
    buckets,
    self_gain,
    self_query,
    self_key,
    self_value,
    self_out,
    position_bias,
    cross_gain,
    cross_query,
    cross_key,
    cross_value,
    cross_out,
    feed_gain,
    feed_gate,
    feed_up,
    feed_down,
    cotangent,
    *,
    dp,
    mp,
):
    batches, length, width = inputs.shape
    enc_length = encoded.shape[1]
    parts = mp // batches
    rows = length // parts
    enc_rows = enc_length // parts
    place = lax.axis_index("mp")
    sequence = place // parts
    part = place % parts
    first = part * rows
    enc_first = part * enc_rows

    groups = self_key.shape[1] * mp // (2 * HEAD_DIM)
    native = mp == groups and dp == 8 and rows % 16 == 0

    gains = [gather(g, ((0, "dp"),)).astype(F32)[None] for g in (self_gain, cross_gain, feed_gain)]
    gain_one, gain_two, gain_three = gains
    table = gather(position_bias, ROWS_BY_DP).astype(F32)
    if native:
        order = ["by_dp", "by_mp"]
        w1 = jnp.concatenate([self_query, self_key, self_value], axis=1)
        w2 = jnp.concatenate([cross_query, cross_key, cross_value], axis=1)
        w1, wo1 = gather_weights([w1, self_out], order, dp, mp, 1, "gather_self")
        w2, wo2 = gather_weights([w2, cross_out], order, dp, mp, 2, "gather_cross")
        wg, wu, wd = gather_weights(
            [feed_gate, feed_up, feed_down], ["by_dp"] + order, dp, mp, 3, "gather_feed"
        )
        w1, w2, wg, wu = (w.reshape(mp, width, w.shape[3]) for w in (w1, w2, wg, wu))
    else:

        def blocks(*shards):
            return jnp.concatenate([grouped(gather(s, ROWS_BY_DP), groups) for s in shards], axis=2)

        w1 = blocks(self_query, self_key, self_value)
        w2 = blocks(cross_query, cross_key, cross_value)
        wg, wu = blocks(feed_gate), blocks(feed_up)
        wo1, wo2, wd = (gather(s, ROWS_BY_MP) for s in (self_out, cross_out, feed_down))

    whole = lax.dynamic_index_in_dim(inputs, sequence, keepdims=False)
    memory = lax.dynamic_index_in_dim(encoded, sequence, keepdims=False)
    docs = lax.dynamic_index_in_dim(decoder_segments, sequence, keepdims=False)
    enc_docs = lax.dynamic_index_in_dim(encoder_segments, sequence, keepdims=False)
    upstream = lax.dynamic_slice(cotangent, (sequence, first, 0), (1, rows, width))[0]

    def own(array):
        return lax.dynamic_slice_in_dim(array, first, rows, axis=0)

    padded = round_up(rows, TILE_Q)
    tiles = padded // TILE_Q
    front = round_up(length - rows, TILE_K)
    reach = ((rows - 1 + front) // TILE_K + 1) * TILE_K
    lead = TILE_K
    spread = (tiles - 1) * TILE_Q + front + lead + TILE_Q
    kinds = jnp.arange(4, dtype=jnp.int32)
    before = jnp.sum((docs[None, :] < kinds[:, None]).astype(jnp.int32), axis=1)
    enc_before = jnp.sum((enc_docs[None, :] < kinds[:, None]).astype(jnp.int32), axis=1)
    enc_until = jnp.sum((enc_docs[None, :] <= kinds[:, None]).astype(jnp.int32), axis=1)
    own_docs = own(docs)
    is_doc = (own_docs[:, None] == kinds[None, :]).astype(jnp.int32)
    start = jnp.sum(is_doc * before[None, :], axis=1) - first + front
    start = jnp.pad(start, (0, padded - rows), constant_values=1 << 20)
    tile_first = jnp.arange(tiles, dtype=jnp.int32) * TILE_Q
    tile_last = jnp.minimum(tile_first + TILE_Q - 1, rows - 1)
    lo_one = start[::TILE_Q] // TILE_K
    hi_one = (tile_last + front) // TILE_K + 1
    doc_first = own_docs[::TILE_Q]
    doc_last = jnp.concatenate([own_docs[TILE_Q - 1 :: TILE_Q], own_docs[-1:]])[:tiles]
    lo_two = jnp.sum((doc_first[:, None] == kinds) * enc_before[None, :], axis=1) // TILE_K
    hi_two = (jnp.sum((doc_last[:, None] == kinds) * enc_until[None, :], axis=1) - 1) // TILE_K + 1
    bounds_one = (lo_one.astype(jnp.int32), hi_one.astype(jnp.int32))
    bounds_two = (lo_two.astype(jnp.int32), hi_two.astype(jnp.int32))
    mask_one = start[None, :]
    mask_two = jnp.pad(own_docs, (0, padded - rows), constant_values=-1)[None, :]
    keys_two = jnp.broadcast_to(enc_docs[:, None], (enc_length, TILE_Q))

    onehot = (buckets[:, None] == jnp.arange(table.shape[0], dtype=jnp.int32)).astype(F32)
    by_distance = dot(table, onehot, ((0,), (1,)), HIGHEST)
    heads = by_distance.shape[0]
    vec = jnp.concatenate(
        [
            jnp.full((heads, lead), NEGATIVE, F32),
            by_distance,
            jnp.zeros((heads, max(0, spread - lead - length)), F32),
        ],
        axis=1,
    )[:, :spread]
    vec = vec.reshape(heads // 4, 4, spread)

    back_pad = max(0, reach - front - rows)
    window = jnp.pad(whole, ((front, back_pad), (0, 0)))
    window = lax.dynamic_slice_in_dim(window, first, reach, axis=0)
    x = own(whole)
    q1, k1, v1, n1 = self_project(window, gain_one, w1, front, padded, rows)
    o1, lse_one = attend_forward(
        q1, k1, v1, mask_one, vec, bounds_one, front, lead, True, "self_forward"
    )
    h1, n2, q2, k2, v2 = cross_project(o1, wo1, x, gain_two, memory, w2)
    o2, lse_two = attend_forward(
        q2, k2, v2, mask_two, keys_two, bounds_two, 0, 0, False, "cross_forward"
    )

    result, grad_two, grad_gain_three, gwg, gwu, gwd, do2, gwo2 = feed(
        o2, wo2, h1, gain_three, upstream, wg, wu, wd
    )
    outputs = lax.all_gather(result, "mp", axis=0, tiled=True).reshape(inputs.shape)

    dq2, dk2, dv2 = attend_backward(
        q2, k2, v2, o2, do2, lse_two, mask_two, keys_two, bounds_two, 0, 0, False, "cross_backward"
    )
    sharing = [[s * parts + p for p in range(parts)] for s in range(batches)]

    def share(array):
        return lax.psum_scatter(
            array, "mp", scatter_dimension=0, axis_index_groups=sharing, tiled=True
        )

    gwq2, grad_one, grad_gain_two, do1, gwo1 = cross_back(
        dq2, w2, n2, h1, gain_two, grad_two, wo1, o1
    )
    dkv2 = share(jnp.concatenate([dk2, dv2], axis=1))
    half = dkv2.shape[1] // 2
    own_memory = lax.dynamic_slice_in_dim(memory, enc_first, enc_rows, axis=0)
    gwkv2, grad_memory = memory_back(dkv2[:, :half], dkv2[:, half:], w2, own_memory)
    grad_encoded = lax.all_gather(grad_memory, "mp", axis=0, tiled=True).reshape(encoded.shape)

    dq1, dk1, dv1, slopes = attend_backward(
        q1, k1, v1, o1, do1, lse_one, mask_one, vec, bounds_one, front, lead, True, "self_backward"
    )
    dkv1 = jnp.concatenate([dk1, dv1], axis=1)
    dkv1 = jnp.pad(dkv1, ((0, max(0, front + length - reach)), (0, 0)))
    dkv1 = share(lax.dynamic_slice_in_dim(dkv1, front - first, length, axis=0))
    gwq1, gwkv1, grad_rows, grad_gain_one = self_back(
        dq1, dkv1[:, :half], dkv1[:, half:], w1, n1, x, gain_one, grad_one
    )
    grad_inputs = lax.all_gather(grad_rows, "mp", axis=0, tiled=True).reshape(inputs.shape)
    slopes = slopes.reshape(heads, spread)[:, lead : lead + length]
    slopes = jnp.pad(slopes, ((0, 0), (0, length - slopes.shape[1])))
    grad_table = dot(onehot, slopes, ((0,), (1,)), HIGHEST)

    small = jnp.concatenate(
        [grad_gain_one[0], grad_gain_two[0], grad_gain_three[0], grad_table.reshape(-1)]
    )
    small = lax.psum(small, ("dp", "mp"))
    data = lax.axis_index("dp")

    def gain_block(index):
        size = width // dp
        return lax.dynamic_slice_in_dim(small, index * width + data * size, size, axis=0)

    grad_table = small[3 * width :].reshape(table.shape)
    grad_table = lax.dynamic_slice(
        grad_table,
        (data * position_bias.shape[0], place * position_bias.shape[1]),
        position_bias.shape,
    )
    kcols = gwkv1.shape[2] // 2

    def summed(grad):
        if native:
            grad = lax.psum_scatter(grad, "mp", scatter_dimension=0, tiled=True)
            return lax.psum_scatter(grad[0], "dp", scatter_dimension=0, tiled=True).astype(F32)
        return scatter(ungrouped(grad), ROWS_BY_DP)

    return (
        outputs,
        grad_inputs,
        grad_encoded,
        gain_block(0),
        summed(gwq1),
        summed(gwkv1[:, :, :kcols]),
        summed(gwkv1[:, :, kcols:]),
        scatter(gwo1, ROWS_BY_MP),
        grad_table,
        gain_block(1),
        summed(gwq2),
        summed(gwkv2[:, :, :kcols]),
        summed(gwkv2[:, :, kcols:]),
        scatter(gwo2, ROWS_BY_MP),
        gain_block(2),
        summed(gwg),
        summed(gwu),
        scatter(gwd, ROWS_BY_MP),
    )


def solution(mesh):
    rows3 = P("dp", None, None)
    by_dp = P("dp", "mp")
    by_mp = P("mp", "dp")
    gain = P("dp")
    return jax.shard_map(
        functools.partial(body, dp=mesh.shape["dp"], mp=mesh.shape["mp"]),
        mesh=mesh,
        in_specs=(
            rows3, rows3, P("dp", None), P("dp", None), P(),
            gain, by_dp, by_dp, by_dp, by_mp, by_dp,
            gain, by_dp, by_dp, by_dp, by_mp,
            gain, by_dp, by_dp, by_mp, rows3,
        ),
        out_specs=(
            rows3, rows3, rows3,
            gain, by_dp, by_dp, by_dp, by_mp, by_dp,
            gain, by_dp, by_dp, by_dp, by_mp,
            gain, by_dp, by_dp, by_mp,
        ),
        check_vma=False,
    )
```

```python
import functools

import jax
import jax.numpy as jnp
from jax import lax
from jax.experimental import pallas as pl
from jax.experimental.pallas import tpu as pltpu
from jax.sharding import PartitionSpec as P

HEAD_DIM = 64
TILE_Q = 128
TILE_K = 256
EPSILON = 1e-06
NEGATIVE = -1e30
HIGHEST = lax.Precision.HIGHEST
F32 = jnp.float32
BF16 = jnp.bfloat16


def dot(left, right, dims, precision=None):
    return lax.dot_general(
        left, right, ((dims[0], dims[1]), ((), ())), precision=precision, preferred_element_type=F32
    )


def mm(left, right):
    return dot(left, right, ((1,), (0,)))


def mm_nt(left, right):
    return dot(left, right, ((1,), (1,)))


def mm_tn(left, right):
    return dot(left, right, ((0,), (0,)))


def round_up(value, unit):
    return (value + unit - 1) // unit * unit


def chunked(total, size, run):
    def once(n, carry):
        run(pl.multiple_of(n * size, size))
        return carry

    lax.fori_loop(0, total // size, once, 0)


MESH = pl.DeviceIdType.MESH


class Place:
    def __init__(self, mp):
        self.mp = mp
        self.i = lax.axis_index("dp")
        self.z = lax.axis_index("mp")
        core = lax.rem(self.i, 2)
        across = lax.rem(lax.div(self.i, 2), 2)
        up = lax.div(self.i, 4)
        self.core, self.across, self.up = core, across, up
        self.ic = self.i + 1 - 2 * core
        self.ix = self.i + 2 - 4 * across
        self.iy = self.i + 4 - 8 * up
        self.ixy = self.ix + 4 - 8 * up


def enter(place):
    barrier = pltpu.get_barrier_semaphore()
    z, mp = place.z, place.mp
    for near in (place.ic, place.ix, place.iy):
        pl.semaphore_signal(barrier, 1, device_id=(near, z), device_id_type=MESH)

    @pl.when(z > 0)
    def _():
        pl.semaphore_signal(barrier, 1, device_id=(place.i, z - 1), device_id_type=MESH)

    @pl.when(z < mp - 1)
    def _():
        pl.semaphore_signal(barrier, 1, device_id=(place.i, z + 1), device_id_type=MESH)

    low = jnp.minimum(z, 1)
    high = jnp.minimum(mp - 1 - z, 1)
    pl.semaphore_wait(barrier, 3 + low + high)


def all_slots(mp):
    return [(0, 0)] + [(d, s) for d in range(1, mp) for s in (0, 1)]


def for_slot(place, slot, run):
    d, side = slot
    if d == 0:
        run(place.z)
    elif side == 0:
        pl.when(place.z >= d)(lambda: run(place.z - d))
    else:
        pl.when(place.z < place.mp - d)(lambda: run(place.z + d))


def region(ref, i, z, shard):
    if len(ref.shape) == 4:
        return ref.at[z, i]
    rows, cols = shard
    return ref.at[pl.ds(pl.multiple_of(z * rows, rows), rows), pl.ds(pl.multiple_of(i * cols, cols), cols)]


def gather_steps(place, shards, outs, send, recv, local):
    mp, i, z = place.mp, place.i, place.z
    units = range(len(shards))

    def here(u, i2, z2):
        return region(outs[u], i2, z2, shards[u].shape)

    def copy(u, kind, i2, z2, to, src=None):
        spot = here(u, i2, z2)
        return pltpu.make_async_remote_copy(
            src_ref=spot if src is None else src, dst_ref=spot, send_sem=send.at[u, kind, z2],
            recv_sem=recv.at[u, kind, z2], device_id=to, device_id_type=MESH)

    def route(u, z2):
        odd = lax.rem(z2 + u, 2)
        first = place.ix + odd * (place.iy - place.ix)
        second = place.iy + odd * (place.ix - place.iy)
        return odd, first, second

    slots = all_slots(mp)

    def stage1(slot):
        d, s = slot

        def run(z2):
            for u in units:
                src = shards[u] if d == 0 else None
                if d > 0:
                    kind = 0 if s == 0 else 1
                    copy(u, kind, i, z2, (i, z)).wait_recv()
                if d == 0 or s == 0:
                    pl.when(z < mp - 1)(lambda u=u, src=src: copy(u, 0, i, z2, (i, z + 1), src).start())
                if d == 0 or s == 1:
                    pl.when(z > 0)(lambda u=u, src=src: copy(u, 1, i, z2, (i, z - 1), src).start())
                copy(u, 2, i, z2, (place.ix, z), src).start()
                copy(u, 3, i, z2, (place.iy, z), src).start()
                copy(u, 5, i, z2, (place.ic, z), src).start()
                if d == 0:
                    pltpu.make_async_copy(shards[u], here(u, i, z), local.at[u]).start()

        for_slot(place, slot, run)

    def stage2(slot):
        def run(z2):
            for u in units:
                odd, first, second = route(u, z2)
                kind = 2 + odd
                spot = here(u, first, z2)
                pltpu.make_async_remote_copy(src_ref=spot, dst_ref=spot, send_sem=send.at[u, kind, z2],
                    recv_sem=recv.at[u, kind, z2], device_id=(first, z), device_id_type=MESH).wait_recv()
                copy(u, 4, first, z2, (second, z)).start()
                copy(u, 6, first, z2, (place.ic, z)).start()

        for_slot(place, slot, run)

    def stage3(slot):
        def run(z2):
            for u in units:
                odd, first, second = route(u, z2)
                kind = 3 - odd
                spot = here(u, second, z2)
                pltpu.make_async_remote_copy(src_ref=spot, dst_ref=spot, send_sem=send.at[u, kind, z2],
                    recv_sem=recv.at[u, kind, z2], device_id=(second, z), device_id_type=MESH).wait_recv()
                copy(u, 7, second, z2, (place.ic, z)).start()
                copy(u, 4, place.ixy, z2, (second, z)).wait_recv()
                copy(u, 8, place.ixy, z2, (place.ic, z)).start()

        for_slot(place, slot, run)

    def other(i2):
        return i2 + place.ic - i

    def finish(slot):
        d, s = slot

        def run(z2):
            for u in units:
                odd, first, second = route(u, z2)
                for kind, i2 in ((5, i), (6, first), (7, second), (8, place.ixy)):
                    copy(u, kind, other(i2), z2, (place.ic, z)).wait_recv()
                if d == 0 or s == 0:
                    pl.when(z < mp - 1)(lambda u=u: copy(u, 0, i, z2, (i, z)).wait_send())
                if d == 0 or s == 1:
                    pl.when(z > 0)(lambda u=u: copy(u, 1, i, z2, (i, z)).wait_send())
                for kind in range(2, 9):
                    copy(u, kind, i, z2, (i, z)).wait_send()
                if d == 0:
                    pltpu.make_async_copy(shards[u], here(u, i, z), local.at[u]).wait()

        for_slot(place, slot, run)

    steps = []
    n = len(slots)
    for k in range(n + 2):
        if k < n:
            steps.append(functools.partial(stage1, slots[k]))
        if 0 <= k - 1 < n:
            steps.append(functools.partial(stage2, slots[k - 1]))
        if 0 <= k - 2 < n:
            steps.append(functools.partial(stage3, slots[k - 2]))
    for slot in slots:
        steps.append(functools.partial(finish, slot))
    return steps


def gather_shape(shard, kind, dp, mp):
    rows, cols = shard.shape
    if kind == "by_dp":
        return jax.ShapeDtypeStruct((mp, dp, rows, cols), shard.dtype)
    return jax.ShapeDtypeStruct((mp * rows, dp * cols), shard.dtype)


def add_into(target, *others):
    rows = target.shape[0]
    size = 64 if rows % 64 == 0 else rows

    def some(at):
        part = pl.ds(at, size)
        total = target[part, :].astype(F32)
        for other in others:
            total = total + other[part, :].astype(F32)
        target[part, :] = total.astype(target.dtype)

    chunked(rows, size, some)


def scatter_scratch(shards, mp):
    scratch = []
    for dims, dtype in shards:
        scratch += [
            pltpu.VMEM((mp, 4) + dims, dtype),
            pltpu.VMEM((mp, 4) + dims, dtype),
            pltpu.VMEM((mp, 3) + dims, dtype),
            pltpu.VMEM((mp, 2) + dims, dtype),
        ]
    sems = pltpu.SemaphoreType.DMA((len(shards), 9, mp))
    return scratch + [sems, sems, pltpu.SemaphoreType.DMA((len(shards), 4, mp))]


def scatter_steps(place, grads, outs, scratch):
    mp, i, z = place.mp, place.i, place.z
    units = range(len(grads))
    send, recv, local = scratch[-3:]
    own = [scratch[4 * u] for u in units]
    sibling = [scratch[4 * u + 1] for u in units]
    plane = [scratch[4 * u + 2] for u in units]
    line = [scratch[4 * u + 3] for u in units]
    chips = (place.i, place.ix, place.iy, place.ixy)
    slots = all_slots(mp)[::-1]

    def piece(u, i2, z2):
        return region(grads[u], i2, z2, own[u].shape[2:])

    def copy(u, kind, z2, src, dst, to):
        return pltpu.make_async_remote_copy(
            src_ref=src, dst_ref=dst, send_sem=send.at[u, kind, z2], recv_sem=recv.at[u, kind, z2],
            device_id=to, device_id_type=MESH)

    def load(u, k, z2):
        return pltpu.make_async_copy(piece(u, chips[k], z2), own[u].at[z2, k], local.at[u, k, z2])

    def across(u, k, z2):
        other = chips[k] + place.ic - i
        return copy(u, k, z2, piece(u, other, z2), sibling[u].at[z2, k], (place.ic, z))

    def route(u, z2):
        odd = lax.rem(z2 + u, 2)
        first = place.ix + odd * (place.iy - place.ix)
        second = place.iy + odd * (place.ix - place.iy)
        return 1 + odd, 2 - odd, first, second

    def to_second(u, z2, far):
        _, ks, _, second = route(u, z2)
        src = own[u].at[z2, 3] if far else own[u].at[z2, ks]
        return copy(u, 4 if far else 5, z2, src, plane[u].at[z2, 0 if far else 1], (second, z))

    def to_first(u, z2):
        kf, _, first, _ = route(u, z2)
        return copy(u, 6, z2, own[u].at[z2, kf], plane[u].at[z2, 2], (first, z))

    def along(u, z2, up):
        to = (i, z + 1) if up else (i, z - 1)
        return copy(u, 7 if up else 8, z2, own[u].at[z2, 0], line[u].at[z2, 0 if up else 1], to)

    def begin(slot):
        def run(z2):
            for u in units:
                for k in (3, 2, 1, 0):
                    load(u, k, z2).start()
                    across(u, k, z2).start()

        for_slot(place, slot, run)

    def stage1(slot):
        def run(z2):
            for u in units:
                for k in (3, 2, 1, 0):
                    load(u, k, z2).wait()
                    across(u, k, z2).wait_recv()
                for k in range(4):
                    add_into(own[u].at[z2, k], sibling[u].at[z2, k])
                to_second(u, z2, True).start()
                to_second(u, z2, False).start()

        for_slot(place, slot, run)

    def stage2(slot):
        def run(z2):
            for u in units:
                kf = route(u, z2)[0]
                to_second(u, z2, True).wait_recv()
                add_into(own[u].at[z2, kf], plane[u].at[z2, 0])
                to_first(u, z2).start()

        for_slot(place, slot, run)

    def stage3(slot):
        d, side = slot

        def run(z2):
            for u in units:
                mine = own[u].at[z2, 0]
                to_second(u, z2, False).wait_recv()
                to_first(u, z2).wait_recv()
                add_into(mine, plane[u].at[z2, 1], plane[u].at[z2, 2])
                if d == 0 or side == 1:

                    @pl.when(z > 0)
                    def _(u=u, mine=mine):
                        along(u, z2, True).wait_recv()
                        add_into(mine, line[u].at[z2, 0])

                if d == 0 or side == 0:

                    @pl.when(z < mp - 1)
                    def _(u=u, mine=mine):
                        along(u, z2, False).wait_recv()
                        add_into(mine, line[u].at[z2, 1])

                if d == 0:
                    outs[u][...] = mine[...].astype(F32)
                else:
                    along(u, z2, side == 1).start()

        for_slot(place, slot, run)

    def finish(slot):
        d, side = slot

        def run(z2):
            for u in units:
                for k in range(4):
                    across(u, k, z2).wait_send()
                to_second(u, z2, True).wait_send()
                to_second(u, z2, False).wait_send()
                to_first(u, z2).wait_send()
                if d > 0:
                    along(u, z2, side == 1).wait_send()

        for_slot(place, slot, run)

    steps = [functools.partial(begin, slot) for slot in slots]
    n = len(slots)
    for k in range(n + 2):
        if k < n:
            steps.append(functools.partial(stage1, slots[k]))
        if 0 <= k - 1 < n:
            steps.append(functools.partial(stage2, slots[k - 1]))
        if 0 <= k - 2 < n:
            steps.append(functools.partial(stage3, slots[k - 2]))
    for slot in slots:
        steps.append(functools.partial(finish, slot))
    return steps


def shard_of(grad, dp, mp):
    if len(grad.shape) == 4:
        return grad.shape[2:]
    return (grad.shape[0] // mp, grad.shape[1] // dp)


class Transfers:
    def __init__(self, dp, mp, cid, shards=(), kinds=(), grads=()):
        self.dp, self.mp, self.cid = dp, mp, cid
        self.shards, self.kinds, self.grads = list(shards), list(kinds), list(grads)
        self.args = self.shards + self.grads
        spots = [(shard_of(g, dp, mp), g.dtype) for g in self.grads]
        self.outs = [gather_shape(s, k, dp, mp) for s, k in zip(shards, kinds)]
        self.outs += [jax.ShapeDtypeStruct(s, F32) for s, _ in spots]
        any_space = pl.BlockSpec(memory_space=pl.ANY)
        self.in_specs = [any_space] * len(self.args)
        self.out_specs = [any_space] * len(self.shards)
        self.out_specs += [pl.BlockSpec(s, lambda *_: (0, 0)) for s, _ in spots]
        self.scratch = []
        if self.shards:
            sems = pltpu.SemaphoreType.DMA((len(self.shards), 9, mp))
            self.scratch += [sems, sems, pltpu.SemaphoreType.DMA((len(self.shards),))]
        if self.grads:
            self.scratch += scatter_scratch(spots, mp)

    def steps(self, ins, outs, scratch):
        place = Place(self.mp)
        count = len(self.shards)
        found = [functools.partial(enter, place)]
        if count:
            found += gather_steps(place, ins[:count], outs[:count], *scratch[:3])
            scratch = scratch[3:]
        if self.grads:
            found += scatter_steps(place, ins[count:], outs[count:], scratch)
        return found

    def params(self, limit):
        return pltpu.CompilerParams(
            collective_id=self.cid, has_side_effects=True, vmem_limit_bytes=limit
        )

    def run(self, name):
        count = len(self.args)

        def kernel(*refs):
            outs = refs[count : count + len(self.outs)]
            for step in self.steps(refs[:count], outs, refs[count + len(self.outs) :]):
                step()

        return pl.pallas_call(
            kernel, grid=(1,), out_shape=self.outs, in_specs=self.in_specs, out_specs=self.out_specs,
            scratch_shapes=self.scratch, compiler_params=self.params(60 << 20), name=name,
        )(*self.args)


def spread_steps(steps, at, total):
    for n, step in enumerate(steps):
        pl.when(at == n * total // len(steps))(step)


def skew(row, height):
    wide = jnp.broadcast_to(row, (height, row.shape[1]))
    return pltpu.roll(wide, 0, axis=1, stride=1, stride_axis=0)


def stacked(tile, g):
    base = 2 * HEAD_DIM * g
    return jnp.concatenate(
        [tile[:, base : base + HEAD_DIM], tile[:, base + HEAD_DIM : base + 2 * HEAD_DIM]], axis=0
    )


def unstacked(pair):
    return jnp.concatenate([pair[:TILE_Q], pair[TILE_Q:]], axis=1)


def twice(row):
    return jnp.concatenate([row, row], axis=1)


def tile_mask(biased, mask_ref, keys_ref, a, u0):
    cols = pl.ds(pl.multiple_of(a * TILE_Q, TILE_Q), TILE_Q)
    row = twice(mask_ref[0:1, cols])
    if biased:
        index = lax.broadcasted_iota(jnp.int32, (TILE_K, 2 * TILE_Q), 0)
        return index >= row - u0
    keys = keys_ref[pl.ds(u0, TILE_K), :]
    return jnp.concatenate([keys, keys], axis=1) == row


def tile_bias(strip_ref, g, off):
    lanes = pl.ds(off, TILE_Q)
    return jnp.concatenate([strip_ref[2 * g, :, lanes], strip_ref[2 * g + 1, :, lanes]], axis=1)


def split_refs(refs, host, ins, outs):
    if host is None:
        return refs[2:], [], lambda a: (refs[0][a], refs[1][a])
    a, b = len(host.args), len(host.outs)
    cut = [0, ins, ins + a, ins + a + outs, ins + a + outs + b, len(refs) - len(host.scratch), len(refs)]
    part = [refs[i:j] for i, j in zip(cut, cut[1:])]
    return part[0] + part[2] + part[4], host.steps(part[1], part[3], part[5]), host.bounds


def forward_kernel(biased, front, lead, host, *refs):
    refs, steps, bounds = split_refs(refs, host, 5, 2)
    if biased:
        q_ref, k_ref, v_ref, mask_ref, vec_ref, o_ref, lse_ref, strip, m_s, l_s, acc_s = refs
        keys_ref = None
        for h in range(4):
            strip[h] = skew(vec_ref[0, h : h + 1, :], TILE_K)
    else:
        q_ref, k_ref, v_ref, mask_ref, keys_ref, o_ref, lse_ref, m_s, l_s, acc_s = refs
    tiles = q_ref.shape[0] // TILE_Q
    group = pl.program_id(0)
    places = pl.num_programs(0) * tiles

    def q_tile(a, carry):
        spread_steps(steps, group * tiles + a, places)
        rows = pl.ds(pl.multiple_of(a * TILE_Q, TILE_Q), TILE_Q)
        qt = q_ref[rows, :]
        q2 = [stacked(qt, g) for g in range(2)]
        m_s[...] = jnp.full_like(m_s, NEGATIVE)
        l_s[...] = jnp.zeros_like(l_s)
        acc_s[...] = jnp.zeros_like(acc_s)

        def k_tile(m, carry):
            u0 = pl.multiple_of(m * TILE_K, TILE_K)
            kt = k_ref[pl.ds(u0, TILE_K), :]
            vt = v_ref[pl.ds(u0, TILE_K), :]
            valid = tile_mask(biased, mask_ref, keys_ref, a, u0)
            for g in range(2):
                head = slice(HEAD_DIM * g, HEAD_DIM * (g + 1))
                s = mm_nt(kt[:, head], q2[g])
                if biased:
                    off = pl.multiple_of(a * TILE_Q - m * TILE_K + front + lead, TILE_Q)
                    s = s + tile_bias(strip, g, off)
                s = jnp.where(valid, s, NEGATIVE)
                top = m_s[g : g + 1, :]
                new = jnp.maximum(top, jnp.max(s, axis=0, keepdims=True))
                alpha = jnp.exp(top - new)
                p = jnp.exp(s - new)
                m_s[g : g + 1, :] = new
                l_s[g : g + 1, :] = l_s[g : g + 1, :] * alpha + jnp.sum(p, axis=0, keepdims=True)
                acc_s[g] = acc_s[g] * alpha + mm_tn(vt[:, head], p.astype(BF16))
            return carry

        lax.fori_loop(*bounds(a), k_tile, 0)
        for g in range(2):
            total = l_s[g : g + 1, :]
            mixed = (acc_s[g] / total).T
            o_ref[rows, 2 * HEAD_DIM * g : 2 * HEAD_DIM * (g + 1)] = unstacked(mixed).astype(BF16)
            lse = m_s[g : g + 1, :] + jnp.log(total)
            lse_ref[0, 2 * g : 2 * g + 1, rows] = lse[:, :TILE_Q]
            lse_ref[0, 2 * g + 1 : 2 * g + 2, rows] = lse[:, TILE_Q:]
        return carry

    lax.fori_loop(0, tiles, q_tile, 0)


def backward_kernel(biased, front, lead, host, *refs):
    refs, steps, bounds = split_refs(refs, host, 8, 4 if biased else 3)
    if biased:
        (
            q_ref, k_ref, v_ref, o_ref, do_ref, lse_ref, mask_ref, vec_ref,
            dq_ref, dk_ref, dv_ref, dist_ref, strip, slope, dk_s, dv_s, dq_s,
        ) = refs
        keys_ref = None
        for h in range(4):
            strip[h] = skew(vec_ref[0, h : h + 1, :], TILE_K)
        slope[...] = jnp.zeros_like(slope)
    else:
        (
            q_ref, k_ref, v_ref, o_ref, do_ref, lse_ref, mask_ref, keys_ref,
            dq_ref, dk_ref, dv_ref, dk_s, dv_s, dq_s,
        ) = refs
    tiles = q_ref.shape[0] // TILE_Q
    group = pl.program_id(0)
    places = pl.num_programs(0) * tiles
    dk_s[...] = jnp.zeros_like(dk_s)
    dv_s[...] = jnp.zeros_like(dv_s)

    def q_tile(a, carry):
        spread_steps(steps, group * tiles + a, places)
        rows = pl.ds(pl.multiple_of(a * TILE_Q, TILE_Q), TILE_Q)
        qt = q_ref[rows, :]
        ot = o_ref[rows, :]
        dot_ = do_ref[rows, :]
        q2 = [stacked(qt, g) for g in range(2)]
        do2 = [stacked(dot_, g) for g in range(2)]
        lse = []
        delta = []
        for g in range(2):
            both = stacked(ot, g).astype(F32) * do2[g].astype(F32)
            delta.append(jnp.sum(both.T, axis=0, keepdims=True))
            lse.append(
                jnp.concatenate(
                    [lse_ref[0, 2 * g : 2 * g + 1, rows], lse_ref[0, 2 * g + 1 : 2 * g + 2, rows]],
                    axis=1,
                )
            )
        dq_s[...] = jnp.zeros_like(dq_s)

        def k_tile(m, carry):
            u0 = pl.multiple_of(m * TILE_K, TILE_K)
            keys = pl.ds(u0, TILE_K)
            kt = k_ref[keys, :]
            vt = v_ref[keys, :]
            valid = tile_mask(biased, mask_ref, keys_ref, a, u0)
            grad_k = []
            grad_v = []
            for g in range(2):
                head = slice(HEAD_DIM * g, HEAD_DIM * (g + 1))
                s = mm_nt(kt[:, head], q2[g])
                if biased:
                    off = pl.multiple_of(a * TILE_Q - m * TILE_K + front + lead, TILE_Q)
                    s = s + tile_bias(strip, g, off)
                p = jnp.exp(jnp.where(valid, s - lse[g], NEGATIVE))
                dp = mm_nt(vt[:, head], do2[g])
                ds = p * (dp - delta[g])
                low = ds.astype(BF16)
                if biased:
                    lanes = pl.ds(off, TILE_Q)
                    slope[2 * g, :, lanes] += ds[:, :TILE_Q]
                    slope[2 * g + 1, :, lanes] += ds[:, TILE_Q:]
                grad_v.append(mm(p.astype(BF16), do2[g]))
                grad_k.append(mm(low, q2[g]))
                dq_s[g] += mm_tn(kt[:, head], low)
            dk_s[keys, :] += jnp.concatenate(grad_k, axis=1)
            dv_s[keys, :] += jnp.concatenate(grad_v, axis=1)
            return carry

        lax.fori_loop(*bounds(a), k_tile, 0)
        for g in range(2):
            dq_ref[rows, 2 * HEAD_DIM * g : 2 * HEAD_DIM * (g + 1)] = unstacked(dq_s[g].T).astype(
                BF16
            )
        return carry

    lax.fori_loop(0, tiles, q_tile, 0)
    dk_ref[...] = dk_s[...].astype(BF16)
    dv_ref[...] = dv_s[...].astype(BF16)
    if biased:
        width = slope.shape[2]
        for h in range(4):
            part = slope[h]
            height = TILE_K
            while height > 8:
                height //= 2
                part = part[:height] + pltpu.roll(part[height:], width - height, axis=1)
            row = part[0:1]
            for j in range(1, 8):
                row = row + pltpu.roll(part, width - j, axis=1)[j : j + 1]
            dist_ref[0, h : h + 1, :] = row


def spec(shape, index):
    return pl.BlockSpec(shape, index)


def attention_call(kernel, biased, outs, scratch, args, bounds, front, lead, name, flops, host):
    steps = args[1].shape[1] // (2 * HEAD_DIM)

    def column(array, lanes):
        return spec((array.shape[0], lanes), lambda i, *_: (0, i))

    specs = []
    for array, kind in args_kinds(args, biased, kernel):
        if kind == "wide":
            specs.append(column(array, 4 * HEAD_DIM))
        elif kind == "key":
            specs.append(column(array, 2 * HEAD_DIM))
        elif kind == "head":
            specs.append(spec((1,) + array.shape[1:], lambda i, *_: (i, 0, 0)))
        else:
            specs.append(spec(array.shape, lambda i, *_: (0, 0)))
    out_specs = []
    for item, kind in outs:
        if kind == "wide":
            out_specs.append(column(item, 4 * HEAD_DIM))
        elif kind == "key":
            out_specs.append(column(item, 2 * HEAD_DIM))
        else:
            out_specs.append(spec((1,) + item.shape[1:], lambda i, *_: (i, 0, 0)))
    shapes = [item for item, _ in outs]
    own = len(shapes)
    scalars = list(bounds)
    params = pltpu.CompilerParams(vmem_limit_bytes=56 << 20)
    args = list(args)
    if host is not None:
        scalars = []
        args += host.args
        specs += host.in_specs
        shapes += host.outs
        out_specs += host.out_specs
        scratch = scratch + host.scratch
        params = host.params(60 << 20)
    found = pl.pallas_call(
        functools.partial(kernel, biased, front, lead, host),
        out_shape=shapes,
        grid_spec=pltpu.PrefetchScalarGridSpec(
            num_scalar_prefetch=len(scalars),
            grid=(steps,),
            in_specs=specs,
            out_specs=out_specs,
            scratch_shapes=scratch,
        ),
        compiler_params=params,
        cost_estimate=pl.CostEstimate(flops=flops, bytes_accessed=16 << 20, transcendentals=0),
        name=name,
    )(*scalars, *args)
    return found[:own], found[own:]


def args_kinds(args, biased, kernel):
    tail = ["flat", "head" if biased else "flat"]
    if kernel is forward_kernel:
        kinds = ["wide", "key", "key"] + tail
    else:
        kinds = ["wide", "key", "key", "wide", "wide", "head"] + tail
    return list(zip(args, kinds))


def attend_forward(q, k, v, mask, extra, bounds, front, lead, biased, name, host=None):
    rows = q.shape[0]
    steps = k.shape[1] // (2 * HEAD_DIM)
    outs = [
        (jax.ShapeDtypeStruct(q.shape, BF16), "wide"),
        (jax.ShapeDtypeStruct((steps, 4, rows), F32), "head"),
    ]
    scratch = []
    if biased:
        scratch.append(pltpu.VMEM((4, TILE_K, extra.shape[2]), F32))
    scratch += [
        pltpu.VMEM((2, 2 * TILE_Q), F32),
        pltpu.VMEM((2, 2 * TILE_Q), F32),
        pltpu.VMEM((2, HEAD_DIM, 2 * TILE_Q), F32),
    ]
    flops = 4 * rows * k.shape[0] * q.shape[1]
    return attention_call(
        forward_kernel, biased, outs, scratch, (q, k, v, mask, extra), bounds, front, lead, name,
        flops, host,
    )


def attend_backward(
    q, k, v, o, do, lse, mask, extra, bounds, front, lead, biased, name, host=None
):
    rows = q.shape[0]
    keys = k.shape[0]
    outs = [
        (jax.ShapeDtypeStruct(q.shape, BF16), "wide"),
        (jax.ShapeDtypeStruct(k.shape, BF16), "key"),
        (jax.ShapeDtypeStruct(k.shape, BF16), "key"),
    ]
    scratch = []
    if biased:
        outs.append((jax.ShapeDtypeStruct(extra.shape, F32), "head"))
        scratch += [pltpu.VMEM((4, TILE_K, extra.shape[2]), F32)] * 2
    scratch += [
        pltpu.VMEM((keys, 2 * HEAD_DIM), F32),
        pltpu.VMEM((keys, 2 * HEAD_DIM), F32),
        pltpu.VMEM((2, HEAD_DIM, 2 * TILE_Q), F32),
    ]
    flops = 10 * rows * keys * q.shape[1]
    return attention_call(
        backward_kernel, biased, outs, scratch, (q, k, v, o, do, lse, mask, extra), bounds, front,
        lead, name, flops, host,
    )


def inverse_rms(state):
    return lax.rsqrt(jnp.mean(state * state, axis=-1, keepdims=True) + EPSILON)


def norm_back(state, gain, grad_normed):
    scale = inverse_rms(state)
    weighted = grad_normed * gain
    grad_gain = jnp.sum(grad_normed * state * scale, axis=0, keepdims=True)
    inner = jnp.mean(weighted * state, axis=-1, keepdims=True)
    return scale * weighted - state * (scale * scale * scale) * inner, grad_gain


def row_chunk(rows):
    for size in (272, 256, 128):
        if rows % size == 0:
            return size
    return rows


def full(array):
    return pl.BlockSpec(array.shape, lambda j: (0,) * len(array.shape))


def lead_block(array):
    return pl.BlockSpec((1,) + array.shape[1:], lambda j: (j,) + (0,) * (len(array.shape) - 1))


def col_block(array, parts):
    return pl.BlockSpec((array.shape[0], array.shape[1] // parts), lambda j: (0, j))


def row_block(array, parts):
    return pl.BlockSpec((array.shape[0] // parts, array.shape[1]), lambda j: (j, 0))


def kernel_call(body, name, steps, ins, outs, scratch, flops):
    return pl.pallas_call(
        body,
        grid=(steps,),
        out_shape=[jax.ShapeDtypeStruct(a.shape, a.dtype) for a, _ in outs],
        in_specs=[s for _, s in ins],
        out_specs=[s for _, s in outs],
        scratch_shapes=scratch,
        compiler_params=pltpu.CompilerParams(vmem_limit_bytes=60 << 20),
        cost_estimate=pl.CostEstimate(flops=flops, bytes_accessed=16 << 20, transcendentals=0),
        name=name,
    )(*[a for a, _ in ins])


def shape(dims, dtype=BF16):
    return jax.ShapeDtypeStruct(dims, dtype)


def project_kernel(front, x_ref, gain_ref, w_ref, q_ref, k_ref, v_ref, n_ref, normed):
    reach = x_ref.shape[0]
    padded, qcols = q_ref.shape
    kcols = k_ref.shape[1]
    rows = n_ref.shape[0]
    size = row_chunk(reach)

    @pl.when(pl.program_id(0) == 0)
    def _():
        def norm_rows(at):
            x = x_ref[pl.ds(at, size), :].astype(F32)
            normed[pl.ds(at, size), :] = (x * inverse_rms(x) * gain_ref[...]).astype(BF16)

        chunked(reach, size, norm_rows)
        n_ref[...] = normed[front : front + rows, :]

    q_ref[...] = mm(normed[front : front + padded, :], w_ref[0, :, :qcols]).astype(BF16)

    def keys(at):
        kv = mm(normed[pl.ds(at, size), :], w_ref[0, :, qcols:]).astype(BF16)
        k_ref[pl.ds(at, size), :] = kv[:, :kcols]
        v_ref[pl.ds(at, size), :] = kv[:, kcols:]

    chunked(reach, size, keys)


def self_project(x, gain, w, front, padded, rows):
    reach, width = x.shape
    groups, _, cols = w.shape
    q, k = shape((padded, groups * cols // 2)), shape((reach, groups * cols // 4))
    n = shape((rows, width))
    return kernel_call(
        functools.partial(project_kernel, front), "self_project", groups,
        [(x, full(x)), (gain, full(gain)), (w, lead_block(w))],
        [(q, col_block(q, groups)), (k, col_block(k, groups)), (k, col_block(k, groups)), (n, full(n))],
        [pltpu.VMEM(x.shape, BF16)], 2 * (reach + padded) * width * groups * cols // 2,
    )


def middle_kernel(o_ref, wo_ref, x_ref, gain_ref, m_ref, w_ref, h_ref, n_ref, q_ref, k_ref, v_ref):
    rows = x_ref.shape[0]
    qcols = q_ref.shape[1]
    kcols = k_ref.shape[1]
    size = row_chunk(rows)

    @pl.when(pl.program_id(0) == 0)
    def _():
        def state(at):
            some = pl.ds(at, size)
            h = x_ref[some, :].astype(F32) + mm(o_ref[some, :], wo_ref[...])
            h_ref[some, :] = h
            n_ref[some, :] = (h * inverse_rms(h) * gain_ref[...]).astype(BF16)

        chunked(rows, size, state)

    q_ref[0:rows, :] = mm(n_ref[...], w_ref[0, :, :qcols]).astype(BF16)
    q_ref[rows:, :] = jnp.zeros((q_ref.shape[0] - rows, qcols), BF16)
    kv = mm(m_ref[...], w_ref[0, :, qcols:]).astype(BF16)
    k_ref[...] = kv[:, :kcols]
    v_ref[...] = kv[:, kcols:]


def cross_project(o, wo, x, gain, memory, w):
    rows, width = x.shape
    groups, _, cols = w.shape
    h, n = shape(x.shape, F32), shape(x.shape)
    q = shape((o.shape[0], groups * cols // 2))
    k = shape((memory.shape[0], groups * cols // 4))
    return kernel_call(
        middle_kernel, "cross_project", groups,
        [(o, full(o)), (wo, full(wo)), (x, full(x)), (gain, full(gain)), (memory, full(memory)),
         (w, lead_block(w))],
        [(h, full(h)), (n, full(n)), (q, col_block(q, groups)), (k, col_block(k, groups)),
         (k, col_block(k, groups))],
        [], 6 * rows * width * width,
    )


def gate_parts(value):
    square = value * value
    inner = jnp.tanh(0.7978845608028654 * (value + 0.044715 * square * value))
    half = 0.5 * (1.0 + inner)
    slope = 0.7978845608028654 * (1.0 + 3.0 * 0.044715 * square)
    return value * half, half + 0.5 * value * (1.0 - inner * inner) * slope


def feed_kernel(
    o_ref, wo_ref, h1_ref, gain_ref, up_ref, wg_ref, wu_ref, wd_ref,
    out_ref, g2_ref, gain_out, gwg_ref, gwu_ref, gwd_ref, do_ref, gwo_ref,
    h2, normed, total, back, hidden_s, dgate_s, dup_s,
):
    rows, width = h1_ref.shape
    j = pl.program_id(0)
    size = row_chunk(rows)

    @pl.when(j == 0)
    def _():
        def state(at):
            some = pl.ds(at, size)
            h = h1_ref[some, :] + mm(o_ref[some, :], wo_ref[...])
            h2[some, :] = h
            normed[some, :] = (h * inverse_rms(h) * gain_ref[...]).astype(BF16)
            total[some, :] = h
            back[some, :] = jnp.zeros((size, width), F32)

        chunked(rows, size, state)

    def hidden_rows(at):
        some = pl.ds(at, size)
        n = normed[some, :]
        g = up_ref[some, :]
        gate = mm(n, wg_ref[0])
        up = mm(n, wu_ref[0])
        grad_hidden = mm_nt(g, wd_ref[...])
        active, pull = gate_parts(gate)
        hidden = (active * up).astype(BF16)
        grad_gate = (grad_hidden * up * pull).astype(BF16)
        grad_up = (grad_hidden * active).astype(BF16)
        hidden_s[some, :] = hidden
        dgate_s[some, :] = grad_gate
        dup_s[some, :] = grad_up
        total[some, :] += mm(hidden, wd_ref[...])
        back[some, :] += mm_nt(grad_gate, wg_ref[0]) + mm_nt(grad_up, wu_ref[0])

    chunked(rows, size, hidden_rows)

    def weight_rows(at):
        some = pl.ds(at, 128)
        n = normed[:, some]
        gwg_ref[0, some, :] = mm_tn(n, dgate_s[...]).astype(BF16)
        gwu_ref[0, some, :] = mm_tn(n, dup_s[...]).astype(BF16)
        gwd_ref[:, some] = mm_tn(hidden_s[...], up_ref[:, some]).astype(BF16)

    chunked(width, 128, weight_rows)

    @pl.when(j == pl.num_programs(0) - 1)
    def _():
        gain_out[...] = jnp.zeros_like(gain_out)
        do_ref[...] = jnp.zeros_like(do_ref)

        def finish(at):
            some = pl.ds(at, size)
            out_ref[some, :] = total[some, :].astype(BF16)
            change, grad_gain = norm_back(h2[some, :], gain_ref[...], back[some, :])
            gain_out[...] += grad_gain
            g2 = up_ref[some, :].astype(F32) + change
            g2_ref[some, :] = g2
            low = g2.astype(BF16)
            normed[some, :] = low
            do_ref[some, :] = mm_nt(low, wo_ref[...]).astype(BF16)

        chunked(rows, size, finish)

        def out_rows(at):
            some = pl.ds(at, 256)
            gwo_ref[some, :] = mm_tn(o_ref[0:rows, some], normed[...]).astype(BF16)

        chunked(width, 256, out_rows)


def feed(o, wo, h1, gain, upstream, wg, wu, wd):
    rows, width = h1.shape
    groups, _, cols = wg.shape
    out, g2, gg = shape(h1.shape), shape(h1.shape, F32), shape((1, width), F32)
    return kernel_call(
        feed_kernel, "feed", groups,
        [(o, full(o)), (wo, full(wo)), (h1, full(h1)), (gain, full(gain)), (upstream, full(upstream)),
         (wg, lead_block(wg)), (wu, lead_block(wu)), (wd, row_block(wd, groups))],
        [(out, full(out)), (g2, full(g2)), (gg, full(gg)), (wg, lead_block(wg)), (wu, lead_block(wu)),
         (wd, row_block(wd, groups)), (o, full(o)), (wo, full(wo))],
        [pltpu.VMEM((rows, width), F32), pltpu.VMEM((rows, width), BF16), pltpu.VMEM((rows, width), F32),
         pltpu.VMEM((rows, width), F32)] + [pltpu.VMEM((rows, cols), BF16)] * 3,
        18 * rows * width * groups * cols,
    )


def back_kernel(
    dq_ref, w_ref, n_ref, h_ref, gain_ref, g2_ref, wo_ref, o_ref,
    gw_ref, g1_ref, gain_out, do_ref, gwo_ref, back, low_s,
):
    rows, width = h_ref.shape
    qcols = dq_ref.shape[1]
    j = pl.program_id(0)
    size = row_chunk(rows)

    @pl.when(j == 0)
    def _():
        back[...] = jnp.zeros_like(back)

    back[...] += mm_nt(dq_ref[0:rows, :], w_ref[0, :, :qcols])

    def weight_rows(at):
        some = pl.ds(at, 256)
        gw_ref[0, some, :] = mm_tn(n_ref[:, some], dq_ref[0:rows, :]).astype(BF16)

    chunked(width, 256, weight_rows)

    @pl.when(j == pl.num_programs(0) - 1)
    def _():
        gain_out[...] = jnp.zeros_like(gain_out)
        do_ref[...] = jnp.zeros_like(do_ref)

        def finish(at):
            some = pl.ds(at, size)
            change, grad_gain = norm_back(h_ref[some, :], gain_ref[...], back[some, :])
            gain_out[...] += grad_gain
            g1 = g2_ref[some, :] + change
            g1_ref[some, :] = g1
            low = g1.astype(BF16)
            low_s[some, :] = low
            do_ref[some, :] = mm_nt(low, wo_ref[...]).astype(BF16)

        chunked(rows, size, finish)

        def out_rows(at):
            some = pl.ds(at, 256)
            gwo_ref[some, :] = mm_tn(o_ref[0:rows, some], low_s[...]).astype(BF16)

        chunked(width, 256, out_rows)


def cross_back(dq, w, n, h, gain, g2, wo, o):
    rows, width = h.shape
    groups, _, cols = w.shape
    gw = shape((groups, width, cols // 2))
    gg = shape((1, width), F32)
    return kernel_call(
        back_kernel, "cross_back", groups,
        [(dq, col_block(dq, groups)), (w, lead_block(w)), (n, full(n)), (h, full(h)), (gain, full(gain)),
         (g2, full(g2)), (wo, full(wo)), (o, full(o))],
        [(gw, lead_block(gw)), (g2, full(g2)), (gg, full(gg)), (o, full(o)), (wo, full(wo))],
        [pltpu.VMEM((rows, width), F32), pltpu.VMEM((rows, width), BF16)],
        8 * rows * width * width,
    )


def memory_kernel(dk_ref, dv_ref, w_ref, m_ref, gw_ref, gm_ref, back):
    j = pl.program_id(0)
    qcols = w_ref.shape[2] // 2
    kcols = qcols // 2

    @pl.when(j == 0)
    def _():
        back[...] = jnp.zeros_like(back)

    both = jnp.concatenate([dk_ref[...], dv_ref[...]], axis=1)
    back[...] += mm_nt(both, w_ref[0, :, qcols:])
    gw_ref[0] = mm_tn(m_ref[...], both).astype(BF16)

    @pl.when(j == pl.num_programs(0) - 1)
    def _():
        gm_ref[...] = back[...].astype(BF16)


def memory_back(dk, dv, w, memory):
    groups, width, cols = w.shape
    gw = shape((groups, width, cols // 2))
    return kernel_call(
        memory_kernel, "memory_back", groups,
        [(dk, col_block(dk, groups)), (dv, col_block(dv, groups)), (w, lead_block(w)), (memory, full(memory))],
        [(gw, lead_block(gw)), (memory, full(memory))],
        [pltpu.VMEM(memory.shape, F32)], 4 * memory.shape[0] * width * width,
    )


def last_kernel(
    dq_ref, dk_ref, dv_ref, w_ref, n_ref, x_ref, gain_ref, g1_ref,
    gwq_ref, gwkv_ref, gx_ref, gain_out, back,
):
    rows, width = x_ref.shape
    j = pl.program_id(0)
    size = row_chunk(rows)

    @pl.when(j == 0)
    def _():
        back[...] = jnp.zeros_like(back)

    dq = dq_ref[0:rows, :]
    dkv = jnp.concatenate([dk_ref[...], dv_ref[...]], axis=1)
    both = jnp.concatenate([dq, dkv], axis=1)
    back[...] += mm_nt(both, w_ref[0])

    def weight_rows(at):
        some = pl.ds(at, 256)
        gwq_ref[0, some, :] = mm_tn(n_ref[:, some], dq).astype(BF16)
        gwkv_ref[0, some, :] = mm_tn(n_ref[:, some], dkv).astype(BF16)

    chunked(width, 256, weight_rows)

    @pl.when(j == pl.num_programs(0) - 1)
    def _():
        gain_out[...] = jnp.zeros_like(gain_out)

        def finish(at):
            some = pl.ds(at, size)
            change, grad_gain = norm_back(x_ref[some, :].astype(F32), gain_ref[...], back[some, :])
            gain_out[...] += grad_gain
            gx_ref[some, :] = (g1_ref[some, :] + change).astype(BF16)

        chunked(rows, size, finish)


def self_back(dq, dk, dv, w, n, x, gain, g1):
    rows, width = x.shape
    groups, _, cols = w.shape
    gw = shape((groups, width, cols // 2))
    gg = shape((1, width), F32)
    return kernel_call(
        last_kernel, "self_back", groups,
        [(dq, col_block(dq, groups)), (dk, col_block(dk, groups)), (dv, col_block(dv, groups)),
         (w, lead_block(w)), (n, full(n)), (x, full(x)), (gain, full(gain)), (g1, full(g1))],
        [(gw, lead_block(gw)), (gw, lead_block(gw)), (x, full(x)), (gg, full(gg))],
        [pltpu.VMEM((rows, width), F32)],
        8 * rows * width * width,
    )


def gather(shard, dims):
    for axis, name in dims:
        shard = lax.all_gather(shard, name, axis=axis, tiled=True)
    return shard


ROWS_BY_DP = ((0, "dp"), (1, "mp"))
ROWS_BY_MP = ((1, "dp"), (0, "mp"))


def scatter(grad, dims):
    for axis, name in dims:
        grad = lax.psum_scatter(grad, name, scatter_dimension=axis, tiled=True)
    return grad.astype(F32)


def grouped(weight, groups):
    rows, cols = weight.shape
    return weight.reshape(rows, groups, cols // groups).transpose(1, 0, 2)


def ungrouped(weight):
    groups, rows, cols = weight.shape
    return weight.transpose(1, 0, 2).reshape(rows, groups * cols)


def body(
    inputs,
    encoded,
    decoder_segments,
    encoder_segments,
    buckets,
    self_gain,
    self_query,
    self_key,
    self_value,
    self_out,
    position_bias,
    cross_gain,
    cross_query,
    cross_key,
    cross_value,
    cross_out,
    feed_gain,
    feed_gate,
    feed_up,
    feed_down,
    cotangent,
    *,
    dp,
    mp,
):
    batches, length, width = inputs.shape
    enc_length = encoded.shape[1]
    parts = mp // batches
    rows = length // parts
    enc_rows = enc_length // parts
    place = lax.axis_index("mp")
    sequence = place // parts
    part = place % parts
    first = part * rows
    enc_first = part * enc_rows

    groups = self_key.shape[1] * mp // (2 * HEAD_DIM)
    native = mp == groups and dp == 8 and rows % 16 == 0

    if native:
        order = ["by_dp", "by_mp"]
        size = width // dp
        gains = jnp.stack([self_gain, cross_gain, feed_gain])
        little = jnp.pad(position_bias.reshape(1, -1), ((0, 0), (0, size - position_bias.size)))
        little = jnp.pad(jnp.concatenate([gains, little]), ((0, 12), (0, 0)))
        w1 = jnp.concatenate([self_query, self_key, self_value], axis=1)
        w2 = jnp.concatenate([cross_query, cross_key, cross_value], axis=1)
        w1, little, wo1 = Transfers(
            dp, mp, 1, [w1, little, self_out], ["by_dp"] + order
        ).run("gather_self")
        gains = little[0, :, :3].transpose(1, 0, 2).reshape(3, 1, width).astype(F32)
        table = little[:, :, 3, : position_bias.size].reshape((mp, dp) + position_bias.shape)
        table = table.transpose(1, 2, 0, 3).reshape(dp * position_bias.shape[0], -1).astype(F32)
        w1 = w1.reshape(mp, width, w1.shape[3])
    else:
        gains = [gather(g, ((0, "dp"),)).astype(F32)[None] for g in (self_gain, cross_gain, feed_gain)]
        table = gather(position_bias, ROWS_BY_DP).astype(F32)

        def blocks(*shards):
            return jnp.concatenate([grouped(gather(s, ROWS_BY_DP), groups) for s in shards], axis=2)

        w1 = blocks(self_query, self_key, self_value)
        w2 = blocks(cross_query, cross_key, cross_value)
        wg, wu = blocks(feed_gate), blocks(feed_up)
        wo1, wo2, wd = (gather(s, ROWS_BY_MP) for s in (self_out, cross_out, feed_down))
    gain_one, gain_two, gain_three = gains

    whole = lax.dynamic_index_in_dim(inputs, sequence, keepdims=False)
    memory = lax.dynamic_index_in_dim(encoded, sequence, keepdims=False)
    docs = lax.dynamic_index_in_dim(decoder_segments, sequence, keepdims=False)
    enc_docs = lax.dynamic_index_in_dim(encoder_segments, sequence, keepdims=False)
    upstream = lax.dynamic_slice(cotangent, (sequence, first, 0), (1, rows, width))[0]

    def own(array):
        return lax.dynamic_slice_in_dim(array, first, rows, axis=0)

    padded = round_up(rows, TILE_Q)
    tiles = padded // TILE_Q
    front = round_up(length - rows, TILE_K)
    reach = ((rows - 1 + front) // TILE_K + 1) * TILE_K
    lead = TILE_K
    spread = (tiles - 1) * TILE_Q + front + lead + TILE_Q
    kinds = jnp.arange(4, dtype=jnp.int32)
    before = jnp.sum((docs[None, :] < kinds[:, None]).astype(jnp.int32), axis=1)
    enc_before = jnp.sum((enc_docs[None, :] < kinds[:, None]).astype(jnp.int32), axis=1)
    enc_until = jnp.sum((enc_docs[None, :] <= kinds[:, None]).astype(jnp.int32), axis=1)
    own_docs = own(docs)
    is_doc = (own_docs[:, None] == kinds[None, :]).astype(jnp.int32)
    start = jnp.sum(is_doc * before[None, :], axis=1) - first + front
    start = jnp.pad(start, (0, padded - rows), constant_values=1 << 20)
    tile_first = jnp.arange(tiles, dtype=jnp.int32) * TILE_Q
    tile_last = jnp.minimum(tile_first + TILE_Q - 1, rows - 1)
    lo_one = start[::TILE_Q] // TILE_K
    hi_one = (tile_last + front) // TILE_K + 1
    doc_first = own_docs[::TILE_Q]
    doc_last = jnp.concatenate([own_docs[TILE_Q - 1 :: TILE_Q], own_docs[-1:]])[:tiles]
    lo_two = jnp.sum((doc_first[:, None] == kinds) * enc_before[None, :], axis=1) // TILE_K
    hi_two = (jnp.sum((doc_last[:, None] == kinds) * enc_until[None, :], axis=1) - 1) // TILE_K + 1
    bounds_one = (lo_one.astype(jnp.int32), hi_one.astype(jnp.int32))
    bounds_two = (lo_two.astype(jnp.int32), hi_two.astype(jnp.int32))
    mask_one = start[None, :]
    mask_two = jnp.pad(own_docs, (0, padded - rows), constant_values=-1)[None, :]
    keys_two = jnp.broadcast_to(enc_docs[:, None], (enc_length, TILE_Q))

    onehot = (buckets[:, None] == jnp.arange(table.shape[0], dtype=jnp.int32)).astype(F32)
    by_distance = dot(table, onehot, ((0,), (1,)), HIGHEST)
    heads = by_distance.shape[0]
    vec = jnp.concatenate(
        [
            jnp.full((heads, lead), NEGATIVE, F32),
            by_distance,
            jnp.zeros((heads, max(0, spread - lead - length)), F32),
        ],
        axis=1,
    )[:, :spread]
    vec = vec.reshape(heads // 4, 4, spread)

    back_pad = max(0, reach - front - rows)
    window = jnp.pad(whole, ((front, back_pad), (0, 0)))
    window = lax.dynamic_slice_in_dim(window, first, reach, axis=0)
    x = own(whole)
    q1, k1, v1, n1 = self_project(window, gain_one, w1, front, padded, rows)

    def self_bounds(a):
        here = lax.rem(lax.axis_index("mp"), parts)
        last = jnp.minimum(a * TILE_Q + TILE_Q - 1, rows - 1)
        return lax.div(front - here * rows, TILE_K), lax.div(last + front, TILE_K) + 1

    def cross_bounds(a):
        return 0, enc_length // TILE_K

    def carried(bounds, *args, **more):
        host = Transfers(dp, mp, *args, **more)
        host.bounds = bounds
        return host

    hosts = [None] * 4
    if native:
        hosts[0] = carried(self_bounds, 2, [w2, cross_out, feed_gate], order + ["by_dp"])
        hosts[1] = carried(cross_bounds, 3, [feed_up, feed_down], order)
    (o1, lse_one), found = attend_forward(
        q1, k1, v1, mask_one, vec, bounds_one, front, lead, True, "self_forward", hosts[0]
    )
    if native:
        w2, wo2, wg = found
        w2, wg = (w.reshape(mp, width, w.shape[3]) for w in (w2, wg))
    h1, n2, q2, k2, v2 = cross_project(o1, wo1, x, gain_two, memory, w2)
    (o2, lse_two), found = attend_forward(
        q2, k2, v2, mask_two, keys_two, bounds_two, 0, 0, False, "cross_forward", hosts[1]
    )
    if native:
        wu, wd = found
        wu = wu.reshape(mp, width, wu.shape[3])

    result, grad_two, grad_gain_three, gwg, gwu, gwd, do2, gwo2 = feed(
        o2, wo2, h1, gain_three, upstream, wg, wu, wd
    )
    outputs = lax.all_gather(result, "mp", axis=0, tiled=True).reshape(inputs.shape)

    def pieces(grad):
        return grad.reshape(grad.shape[0], dp, grad.shape[1] // dp, grad.shape[2])

    if native:
        hosts[2] = carried(cross_bounds, 4, grads=[gwd])
        hosts[3] = carried(self_bounds, 5, grads=[pieces(gwg), pieces(gwu)])
    (dq2, dk2, dv2), sums_down = attend_backward(
        q2, k2, v2, o2, do2, lse_two, mask_two, keys_two, bounds_two, 0, 0, False,
        "cross_backward", hosts[2],
    )
    sharing = [[s * parts + p for p in range(parts)] for s in range(batches)]

    def share(array):
        return lax.psum_scatter(
            array, "mp", scatter_dimension=0, axis_index_groups=sharing, tiled=True
        )

    gwq2, grad_one, grad_gain_two, do1, gwo1 = cross_back(
        dq2, w2, n2, h1, gain_two, grad_two, wo1, o1
    )
    dkv2 = share(jnp.concatenate([dk2, dv2], axis=1))
    half = dkv2.shape[1] // 2
    own_memory = lax.dynamic_slice_in_dim(memory, enc_first, enc_rows, axis=0)
    gwkv2, grad_memory = memory_back(dkv2[:, :half], dkv2[:, half:], w2, own_memory)
    grad_encoded = lax.all_gather(grad_memory, "mp", axis=0, tiled=True).reshape(encoded.shape)

    (dq1, dk1, dv1, slopes), sums_feed = attend_backward(
        q1, k1, v1, o1, do1, lse_one, mask_one, vec, bounds_one, front, lead, True,
        "self_backward", hosts[3],
    )
    dkv1 = jnp.concatenate([dk1, dv1], axis=1)
    dkv1 = jnp.pad(dkv1, ((0, max(0, front + length - reach)), (0, 0)))
    dkv1 = share(lax.dynamic_slice_in_dim(dkv1, front - first, length, axis=0))
    gwq1, gwkv1, grad_rows, grad_gain_one = self_back(
        dq1, dkv1[:, :half], dkv1[:, half:], w1, n1, x, gain_one, grad_one
    )
    grad_inputs = lax.all_gather(grad_rows, "mp", axis=0, tiled=True).reshape(inputs.shape)
    slopes = slopes.reshape(heads, spread)[:, lead : lead + length]
    slopes = jnp.pad(slopes, ((0, 0), (0, length - slopes.shape[1])))
    grad_table = dot(onehot, slopes, ((0,), (1,)), HIGHEST)
    grad_gains = jnp.concatenate([grad_gain_one, grad_gain_two, grad_gain_three])

    kcols = gwkv1.shape[2] // 2
    if native:
        little = grad_gains.reshape(3, dp, size).transpose(1, 0, 2)
        little = jnp.broadcast_to(little[None], (mp, dp, 3, size))
        spots = grad_table.reshape(dp, position_bias.shape[0], mp, position_bias.shape[1])
        spots = spots.transpose(2, 0, 1, 3).reshape(mp, dp, 1, position_bias.size)
        spots = jnp.pad(spots, ((0, 0), (0, 0), (0, 4), (0, size - position_bias.size)))
        little = jnp.concatenate([little, spots], axis=2)
        grads = [pieces(g) for g in (gwq2, gwkv2, gwq1, gwkv1)] + [gwo2, gwo1, little]
        *sums, little = Transfers(dp, mp, 6, grads=grads).run("scatter_rest")
        sums = sums + list(sums_feed) + list(sums_down)
        sums[1:2] = sums[1][:, :kcols], sums[1][:, kcols:]
        sums[4:5] = sums[4][:, :kcols], sums[4][:, kcols:]
        gwq2, gwk2, gwv2, gwq1, gwk1, gwv1, gwo2, gwo1, gwg, gwu, gwd = sums
        grad_gains = [little[n] for n in range(3)]
        grad_table = little[3, : position_bias.size].reshape(position_bias.shape)
    else:

        def summed(grad):
            return scatter(ungrouped(grad), ROWS_BY_DP)

        gwk1, gwv1 = summed(gwkv1[:, :, :kcols]), summed(gwkv1[:, :, kcols:])
        gwk2, gwv2 = summed(gwkv2[:, :, :kcols]), summed(gwkv2[:, :, kcols:])
        gwq1, gwq2, gwg, gwu = (summed(g) for g in (gwq1, gwq2, gwg, gwu))
        gwo1, gwo2, gwd = (scatter(g, ROWS_BY_MP) for g in (gwo1, gwo2, gwd))
        small = jnp.concatenate([grad_gains.reshape(-1), grad_table.reshape(-1)])
        small = lax.psum(small, ("dp", "mp"))
        data = lax.axis_index("dp")
        grad_gains = lax.dynamic_slice_in_dim(
            small[: 3 * width].reshape(3, dp, width // dp), data, 1, axis=1
        )
        grad_gains = [grad_gains[n, 0] for n in range(3)]
        grad_table = lax.dynamic_slice(
            small[3 * width :].reshape(table.shape),
            (data * position_bias.shape[0], place * position_bias.shape[1]),
            position_bias.shape,
        )

    return (
        outputs, grad_inputs, grad_encoded,
        grad_gains[0], gwq1, gwk1, gwv1, gwo1, grad_table,
        grad_gains[1], gwq2, gwk2, gwv2, gwo2,
        grad_gains[2], gwg, gwu, gwd,
    )


def solution(mesh):
    rows3 = P("dp", None, None)
    by_dp = P("dp", "mp")
    by_mp = P("mp", "dp")
    gain = P("dp")
    return jax.shard_map(
        functools.partial(body, dp=mesh.shape["dp"], mp=mesh.shape["mp"]),
        mesh=mesh,
        in_specs=(
            rows3, rows3, P("dp", None), P("dp", None), P(),
            gain, by_dp, by_dp, by_dp, by_mp, by_dp,
            gain, by_dp, by_dp, by_dp, by_mp,
            gain, by_dp, by_dp, by_mp, rows3,
        ),
        out_specs=(
            rows3, rows3, rows3,
            gain, by_dp, by_dp, by_dp, by_mp, by_dp,
            gain, by_dp, by_dp, by_dp, by_mp,
            gain, by_dp, by_dp, by_mp,
        ),
        check_vma=False,
    )
```

```python
import functools

import jax
import jax.numpy as jnp
from jax import lax
from jax.experimental import pallas as pl
from jax.experimental.pallas import tpu as pltpu
from jax.sharding import PartitionSpec as P

HEAD_DIM = 64
TILE_Q = 128
TILE_K = 256
EPSILON = 1e-06
NEGATIVE = -1e30
HIGHEST = lax.Precision.HIGHEST
F32 = jnp.float32
BF16 = jnp.bfloat16


def dot(left, right, dims, precision=None):
    return lax.dot_general(
        left, right, ((dims[0], dims[1]), ((), ())), precision=precision, preferred_element_type=F32
    )


def mm(left, right):
    return dot(left, right, ((1,), (0,)))


def mm_nt(left, right):
    return dot(left, right, ((1,), (1,)))


def mm_tn(left, right):
    return dot(left, right, ((0,), (0,)))


def round_up(value, unit):
    return (value + unit - 1) // unit * unit


def chunked(total, size, run):
    def once(n, carry):
        run(pl.multiple_of(n * size, size))
        return carry

    lax.fori_loop(0, total // size, once, 0)


MESH = pl.DeviceIdType.MESH


class Place:
    def __init__(self, mp):
        self.mp = mp
        self.i = lax.axis_index("dp")
        self.z = lax.axis_index("mp")
        core = lax.rem(self.i, 2)
        across = lax.rem(lax.div(self.i, 2), 2)
        up = lax.div(self.i, 4)
        self.core, self.across, self.up = core, across, up
        self.ic = self.i + 1 - 2 * core
        self.ix = self.i + 2 - 4 * across
        self.iy = self.i + 4 - 8 * up
        self.ixy = self.ix + 4 - 8 * up


def enter(place):
    barrier = pltpu.get_barrier_semaphore()
    z, mp = place.z, place.mp
    for near in (place.ic, place.ix, place.iy):
        pl.semaphore_signal(barrier, 1, device_id=(near, z), device_id_type=MESH)

    for d in range(1, mp):
        far = lax.rem(z + d, mp)
        pl.semaphore_signal(barrier, 1, device_id=(place.i, far), device_id_type=MESH)
    pl.semaphore_wait(barrier, 3 + mp - 1)


def all_slots(mp):
    return [(0, 0)] + [(d, s) for d in range(1, mp) for s in (0, 1)]


def for_slot(place, slot, run):
    d, side = slot
    if d == 0:
        run(place.z)
    elif side == 0:
        pl.when(place.z >= d)(lambda: run(place.z - d))
    else:
        pl.when(place.z < place.mp - d)(lambda: run(place.z + d))


def region(ref, i, z, shard):
    if len(ref.shape) == 4:
        return ref.at[z, i]
    rows, cols = shard
    return ref.at[pl.ds(pl.multiple_of(z * rows, rows), rows), pl.ds(pl.multiple_of(i * cols, cols), cols)]


def gather_steps(place, shards, outs, send, recv, local):
    mp, i, z = place.mp, place.i, place.z
    units = range(len(shards))

    def here(u, i2, z2):
        return region(outs[u], i2, z2, shards[u].shape)

    def copy(u, kind, i2, z2, to, src=None):
        spot = here(u, i2, z2)
        return pltpu.make_async_remote_copy(
            src_ref=spot if src is None else src, dst_ref=spot, send_sem=send.at[u, kind, z2],
            recv_sem=recv.at[u, kind, z2], device_id=to, device_id_type=MESH)

    def route(u, z2):
        odd = lax.rem(z2 + u, 2)
        first = place.ix + odd * (place.iy - place.ix)
        second = place.iy + odd * (place.ix - place.iy)
        return odd, first, second

    slots = all_slots(mp)

    def stage1(slot):
        d, s = slot

        def run(z2):
            for u in units:
                src = shards[u] if d == 0 else None
                if d > 0:
                    copy(u, s, i, z2, (i, z)).wait_recv()
                copy(u, 2, i, z2, (place.ix, z), src).start()
                copy(u, 3, i, z2, (place.iy, z), src).start()
                copy(u, 5, i, z2, (place.ic, z), src).start()
                if d == 0:
                    pltpu.make_async_copy(shards[u], here(u, i, z), local.at[u]).start()

        for_slot(place, slot, run)

    def along(u, d, up):
        return pltpu.make_async_remote_copy(
            src_ref=shards[u], dst_ref=here(u, i, z), send_sem=send.at[u, 0 if up else 1, d],
            recv_sem=recv.at[u, 0 if up else 1, z], device_id=(i, z + d if up else z - d),
            device_id_type=MESH)

    def depart():
        for d in range(1, mp):
            for u in units:
                pl.when(z < mp - d)(lambda u=u, d=d: along(u, d, True).start())
                pl.when(z >= d)(lambda u=u, d=d: along(u, d, False).start())

    def stage2(slot):
        def run(z2):
            for u in units:
                odd, first, second = route(u, z2)
                kind = 2 + odd
                spot = here(u, first, z2)
                pltpu.make_async_remote_copy(src_ref=spot, dst_ref=spot, send_sem=send.at[u, kind, z2],
                    recv_sem=recv.at[u, kind, z2], device_id=(first, z), device_id_type=MESH).wait_recv()
                copy(u, 4, first, z2, (second, z)).start()
                copy(u, 6, first, z2, (place.ic, z)).start()

        for_slot(place, slot, run)

    def stage3(slot):
        def run(z2):
            for u in units:
                odd, first, second = route(u, z2)
                kind = 3 - odd
                spot = here(u, second, z2)
                pltpu.make_async_remote_copy(src_ref=spot, dst_ref=spot, send_sem=send.at[u, kind, z2],
                    recv_sem=recv.at[u, kind, z2], device_id=(second, z), device_id_type=MESH).wait_recv()
                copy(u, 7, second, z2, (place.ic, z)).start()
                copy(u, 4, place.ixy, z2, (second, z)).wait_recv()
                copy(u, 8, place.ixy, z2, (place.ic, z)).start()

        for_slot(place, slot, run)

    def other(i2):
        return i2 + place.ic - i

    def finish(slot):
        d, s = slot

        def run(z2):
            for u in units:
                odd, first, second = route(u, z2)
                for kind, i2 in ((5, i), (6, first), (7, second), (8, place.ixy)):
                    copy(u, kind, other(i2), z2, (place.ic, z)).wait_recv()
                if d == 0:
                    for far in range(1, mp):
                        pl.when(z < mp - far)(lambda u=u, far=far: along(u, far, True).wait_send())
                        pl.when(z >= far)(lambda u=u, far=far: along(u, far, False).wait_send())
                for kind in range(2, 9):
                    copy(u, kind, i, z2, (i, z)).wait_send()
                if d == 0:
                    pltpu.make_async_copy(shards[u], here(u, i, z), local.at[u]).wait()

        for_slot(place, slot, run)

    steps = [depart]
    n = len(slots)
    for k in range(n + 2):
        if k < n:
            steps.append(functools.partial(stage1, slots[k]))
        if 0 <= k - 1 < n:
            steps.append(functools.partial(stage2, slots[k - 1]))
        if 0 <= k - 2 < n:
            steps.append(functools.partial(stage3, slots[k - 2]))
    return steps, [functools.partial(finish, slot) for slot in slots]


def gather_shape(shard, kind, dp, mp):
    rows, cols = shard.shape
    if kind == "by_dp":
        return jax.ShapeDtypeStruct((mp, dp, rows, cols), shard.dtype)
    return jax.ShapeDtypeStruct((mp * rows, dp * cols), shard.dtype)


def add_into(target, *others):
    rows = target.shape[0]
    size = 64 if rows % 64 == 0 else rows

    def some(at):
        part = pl.ds(at, size)
        total = target[part, :].astype(F32)
        for other in others:
            total = total + other[part, :].astype(F32)
        target[part, :] = total.astype(target.dtype)

    chunked(rows, size, some)


def scatter_scratch(shards, mp):
    scratch = []
    for dims, dtype in shards:
        scratch += [
            pltpu.VMEM((mp, 4) + dims, dtype),
            pltpu.VMEM((mp, 4) + dims, dtype),
            pltpu.VMEM((mp, 3) + dims, dtype),
            pltpu.VMEM((mp,) + dims, dtype),
        ]
    sems = pltpu.SemaphoreType.DMA((len(shards), 8, mp))
    return scratch + [sems, sems, pltpu.SemaphoreType.DMA((len(shards), 4, mp))]


def scatter_steps(place, grads, outs, scratch):
    mp, i, z = place.mp, place.i, place.z
    units = range(len(grads))
    send, recv, local = scratch[-3:]
    own = [scratch[4 * u] for u in units]
    sibling = [scratch[4 * u + 1] for u in units]
    plane = [scratch[4 * u + 2] for u in units]
    line = [scratch[4 * u + 3] for u in units]
    chips = (place.i, place.ix, place.iy, place.ixy)
    slots = all_slots(mp)[::-1]

    def piece(u, i2, z2):
        return region(grads[u], i2, z2, own[u].shape[2:])

    def copy(u, kind, z2, src, dst, to):
        return pltpu.make_async_remote_copy(
            src_ref=src, dst_ref=dst, send_sem=send.at[u, kind, z2], recv_sem=recv.at[u, kind, z2],
            device_id=to, device_id_type=MESH)

    def load(u, k, z2):
        return pltpu.make_async_copy(piece(u, chips[k], z2), own[u].at[z2, k], local.at[u, k, z2])

    def across(u, k, z2):
        other = chips[k] + place.ic - i
        return copy(u, k, z2, piece(u, other, z2), sibling[u].at[z2, k], (place.ic, z))

    def route(u, z2):
        odd = lax.rem(z2 + u, 2)
        first = place.ix + odd * (place.iy - place.ix)
        second = place.iy + odd * (place.ix - place.iy)
        return 1 + odd, 2 - odd, first, second

    def to_second(u, z2, far):
        _, ks, _, second = route(u, z2)
        src = own[u].at[z2, 3] if far else own[u].at[z2, ks]
        return copy(u, 4 if far else 5, z2, src, plane[u].at[z2, 0 if far else 1], (second, z))

    def to_first(u, z2):
        kf, _, first, _ = route(u, z2)
        return copy(u, 6, z2, own[u].at[z2, kf], plane[u].at[z2, 2], (first, z))

    def along(u, z2):
        return pltpu.make_async_remote_copy(
            src_ref=own[u].at[z2, 0], dst_ref=line[u].at[z], send_sem=send.at[u, 7, z2],
            recv_sem=recv.at[u, 7, z], device_id=(i, z2), device_id_type=MESH)

    def arrival(u, z2):
        return pltpu.make_async_remote_copy(
            src_ref=own[u].at[z, 0], dst_ref=line[u].at[z2], send_sem=send.at[u, 7, z],
            recv_sem=recv.at[u, 7, z2], device_id=(i, z), device_id_type=MESH)

    def begin(slot):
        def run(z2):
            for u in units:
                for k in (3, 2, 1, 0):
                    load(u, k, z2).start()
                    across(u, k, z2).start()

        for_slot(place, slot, run)

    def stage1(slot):
        def run(z2):
            for u in units:
                for k in (3, 2, 1, 0):
                    load(u, k, z2).wait()
                    across(u, k, z2).wait_recv()
                for k in range(4):
                    add_into(own[u].at[z2, k], sibling[u].at[z2, k])
                to_second(u, z2, True).start()
                to_second(u, z2, False).start()

        for_slot(place, slot, run)

    def stage2(slot):
        def run(z2):
            for u in units:
                kf = route(u, z2)[0]
                to_second(u, z2, True).wait_recv()
                add_into(own[u].at[z2, kf], plane[u].at[z2, 0])
                to_first(u, z2).start()

        for_slot(place, slot, run)

    def stage3(slot):
        d, side = slot

        def run(z2):
            for u in units:
                mine = own[u].at[z2, 0]
                to_second(u, z2, False).wait_recv()
                to_first(u, z2).wait_recv()
                add_into(mine, plane[u].at[z2, 1], plane[u].at[z2, 2])
                if d > 0:
                    along(u, z2).start()

        for_slot(place, slot, run)

    def finish(slot):
        d, side = slot

        def run(z2):
            for u in units:
                for k in range(4):
                    across(u, k, z2).wait_send()
                to_second(u, z2, True).wait_send()
                to_second(u, z2, False).wait_send()
                to_first(u, z2).wait_send()
                if d > 0:
                    along(u, z2).wait_send()

        for_slot(place, slot, run)

    def collect(slot):
        d, side = slot

        def run(z2):
            for u in units:
                if d == 0:
                    outs[u][...] = own[u][z, 0].astype(F32)
                else:
                    arrival(u, z2).wait_recv()
                    add_into(outs[u], line[u].at[z2])

        for_slot(place, slot, run)

    steps = [functools.partial(begin, slot) for slot in slots]
    n = len(slots)
    for k in range(n + 2):
        if k < n:
            steps.append(functools.partial(stage1, slots[k]))
        if 0 <= k - 1 < n:
            steps.append(functools.partial(stage2, slots[k - 1]))
        if 0 <= k - 2 < n:
            steps.append(functools.partial(stage3, slots[k - 2]))
    last = [functools.partial(collect, slot) for slot in all_slots(mp)]
    return steps, last + [functools.partial(finish, slot) for slot in slots]


def shard_of(grad, dp, mp):
    if len(grad.shape) == 4:
        return grad.shape[2:]
    return (grad.shape[0] // mp, grad.shape[1] // dp)


def line_steps(place, rows, outs, send, recv, local):
    mp, i, z = place.mp, place.i, place.z

    def spot(u, z2):
        parts = outs[u].shape[2]
        return outs[u].at[lax.div(z2, parts), :, lax.rem(z2, parts)]

    def copy(u, up, z2, to, src=None):
        here = spot(u, z2)
        kind = 0 if up else 1
        return pltpu.make_async_remote_copy(
            src_ref=here if src is None else src, dst_ref=here, send_sem=send.at[u, kind, z2],
            recv_sem=recv.at[u, kind, z2], device_id=(i, to), device_id_type=MESH)

    def keep(u):
        return pltpu.make_async_copy(rows[u], spot(u, z), local.at[u])

    def move(slot):
        d, side = slot

        def run(z2):
            for u in range(len(rows)):
                src = rows[u] if d == 0 else None
                if d > 0:
                    copy(u, side == 0, z2, z).wait_recv()
                else:
                    keep(u).start()
                if d == 0 or side == 0:
                    pl.when(z < mp - 1)(lambda u=u, src=src: copy(u, True, z2, z + 1, src).start())
                if d == 0 or side == 1:
                    pl.when(z > 0)(lambda u=u, src=src: copy(u, False, z2, z - 1, src).start())

        for_slot(place, slot, run)

    def finish(slot):
        d, side = slot

        def run(z2):
            for u in range(len(rows)):
                if d == 0:
                    keep(u).wait()
                if d == 0 or side == 0:
                    pl.when(z < mp - 1)(lambda u=u: copy(u, True, z2, z).wait_send())
                if d == 0 or side == 1:
                    pl.when(z > 0)(lambda u=u: copy(u, False, z2, z).wait_send())

        for_slot(place, slot, run)

    steps = [functools.partial(move, slot) for slot in all_slots(mp)]
    return steps, [functools.partial(finish, slot) for slot in all_slots(mp)]


def woven(*lists):
    total = [(n / len(steps), k, n) for k, steps in enumerate(lists) for n in range(len(steps))]
    return [lists[k][n] for _, k, n in sorted(total)]


class Transfers:
    swap = None

    def __init__(self, dp, mp, cid, shards=(), kinds=(), grads=(), rows=(), spread=()):
        self.dp, self.mp, self.cid = dp, mp, cid
        self.shards, self.kinds, self.grads = list(shards), list(kinds), list(grads)
        self.rows = list(rows)
        self.args = self.shards + self.grads + self.rows
        spots = [(shard_of(g, dp, mp), g.dtype) for g in self.grads]
        self.outs = [gather_shape(s, k, dp, mp) for s, k in zip(shards, kinds)]
        self.outs += [jax.ShapeDtypeStruct(s, F32) for s, _ in spots]
        any_space = pl.BlockSpec(memory_space=pl.ANY)
        self.in_specs = [any_space] * len(self.args)
        self.out_specs = [any_space] * len(self.shards)
        self.out_specs += [pl.BlockSpec(s, lambda *_: (0, 0)) for s, _ in spots]
        self.outs += [jax.ShapeDtypeStruct(dims, r.dtype) for r, dims in zip(self.rows, spread)]
        self.out_specs += [any_space] * len(self.rows)
        self.scratch = []
        if self.rows:
            sems = pltpu.SemaphoreType.DMA((len(self.rows), 2, mp))
            self.scratch += [sems, sems, pltpu.SemaphoreType.DMA((len(self.rows),))]
        if self.shards:
            sems = pltpu.SemaphoreType.DMA((len(self.shards), 9, mp))
            self.scratch += [sems, sems, pltpu.SemaphoreType.DMA((len(self.shards),))]
        if self.grads:
            self.scratch += scatter_scratch(spots, mp)

    def steps(self, ins, outs, scratch):
        place = Place(self.mp)
        lists, last = [], []

        def take(steps, ends):
            lists.append(steps)
            last.extend(ends)

        count, more = len(self.shards), len(self.shards) + len(self.grads)
        if self.rows:
            take(*line_steps(place, ins[more:], outs[more:], *scratch[:3]))
            scratch = scratch[3:]
        if count:
            take(*gather_steps(place, ins[:count], outs[:count], *scratch[:3]))
            scratch = scratch[3:]
        if self.grads:
            take(*scatter_steps(place, ins[count:more], outs[count:more], scratch))
        return [functools.partial(enter, place)] + woven(*lists), last

    def params(self, limit):
        return pltpu.CompilerParams(
            collective_id=self.cid, has_side_effects=True, vmem_limit_bytes=limit
        )

    def run(self, name):
        count = len(self.args)

        def kernel(*refs):
            outs = refs[count : count + len(self.outs)]
            steps, last = self.steps(refs[:count], outs, refs[count + len(self.outs) :])
            for step in steps + last:
                step()

        return pl.pallas_call(
            kernel, grid=(1,), out_shape=self.outs, in_specs=self.in_specs, out_specs=self.out_specs,
            scratch_shapes=self.scratch, compiler_params=self.params(60 << 20), name=name,
        )(*self.args)


class Pace:
    def __init__(self, found, each):
        self.steps, self.last = found
        self.group, self.groups, self.each, self.at = pl.program_id(0), pl.num_programs(0), each, 0

    def place(self):
        total = self.groups * self.each
        for n, step in enumerate(self.steps):
            group, at = divmod(n * total // len(self.steps), self.each)
            if at == self.at:
                pl.when(self.group == group)(step)
        self.at += 1

    def end(self):
        @pl.when(self.group == self.groups - 1)
        def _():
            for step in self.last:
                step()


def skew(row, height):
    wide = jnp.broadcast_to(row, (height, row.shape[1]))
    return pltpu.roll(wide, 0, axis=1, stride=1, stride_axis=0)


def widened(tile):
    zero = jnp.zeros((tile.shape[0], HEAD_DIM), tile.dtype)
    found = []
    for h in range(4):
        piece = tile[:, HEAD_DIM * h : HEAD_DIM * (h + 1)]
        found.append(jnp.concatenate([piece, zero] if h < 2 else [zero, piece], axis=1))
    return jnp.concatenate(found, axis=0)


def narrowed(wide):
    n = wide.shape[1] // 4
    found = []
    for h in range(4):
        base = HEAD_DIM * (h // 2)
        found.append(wide[base : base + HEAD_DIM, n * h : n * (h + 1)])
    return jnp.concatenate(found, axis=0).T


def four(row):
    return jnp.concatenate([row] * 4, axis=1)


class Tiles:
    def __init__(self, rows, length, parts):
        self.rows, self.parts, self.blk = rows, parts, 64 // parts
        self.list = [(at, min(TILE_Q, rows - at)) for at in range(0, rows, TILE_Q)]
        self.span = TILE_Q * parts // TILE_K
        self.reach = round_up(length, TILE_K)
        self.strips = len(self.list) * self.span
        self.lead = self.span * TILE_K
        self.width = self.lead + self.strips * TILE_K

    def keys(self, a):
        return min((a + 1) * self.span, self.reach // TILE_K)

    def strip(self, a, m):
        return (a + 1) * self.span - 1 - m

    def windows(self, n):
        runs = [(s * self.blk, 64 * s) for s in range(n // self.blk)]
        return [(e, self.lead + (e + 1 - self.span) * TILE_K, runs) for e in range(self.strips)]


def build_strips(tiles, vec_ref, strip, tail):
    for h in range(4):
        moved = skew(vec_ref[0, h : h + 1, :], TILE_K)
        for ref in (strip, tail):
            n = ref.shape[2] // 4
            for e, at, runs in tiles.windows(n):
                cut = [moved[:, at + far : at + far + tiles.blk] for _, far in runs]
                ref[e, :, n * h : n * (h + 1)] = jnp.concatenate(cut, axis=1)


def split_refs(refs, host, ins, outs):
    if host is None:
        return list(refs), ([], [])
    a, b = len(host.args), len(host.outs)
    cut = [0, ins, ins + a, ins + a + outs, ins + a + outs + b, len(refs) - len(host.scratch), len(refs)]
    part = [list(refs[i:j]) for i, j in zip(cut, cut[1:])]
    return part[0] + part[2] + part[4], host.steps(part[1], part[3], part[5])


def tile_valid(biased, mask, keys_ref, m):
    if biased:
        index = lax.broadcasted_iota(jnp.int32, (TILE_K, mask.shape[1]), 0)
        return index >= mask - m * TILE_K
    keys = keys_ref[pl.ds(m * TILE_K, TILE_K), :]
    reps = -(-mask.shape[1] // keys.shape[1])
    return jnp.concatenate([keys] * reps, axis=1)[:, : mask.shape[1]] == mask


def forward_kernel(biased, tiles, host, *refs):
    refs, steps = split_refs(refs, host, 5, 2)
    if biased:
        q_ref, k_ref, v_ref, mask_ref, vec_ref, o_ref, lse_ref, vt, s_s, strip, tail = refs
        keys_ref = None
        build_strips(tiles, vec_ref, strip, tail)
    else:
        q_ref, k_ref, v_ref, mask_ref, keys_ref, o_ref, lse_ref, vt, s_s = refs
    vt[...] = v_ref[...].T
    counts = [tiles.keys(a) if biased else k_ref.shape[0] // TILE_K for a in range(len(tiles.list))]
    pace = Pace(steps, 2 * sum(counts))
    for a, (at, n) in enumerate(tiles.list):
        lanes = 4 * n
        q4 = widened(q_ref[at : at + n, :])
        mask = mask_ref[a : a + 1, :lanes]
        count = counts[a]
        top = None
        for m in range(count):
            pace.place()
            some = slice(m * TILE_K, (m + 1) * TILE_K)
            s = mm_nt(k_ref[some, :], q4)
            if biased:
                s = s + (strip if n == TILE_Q else tail)[tiles.strip(a, m)]
            s = jnp.where(tile_valid(biased, mask, keys_ref, m), s, NEGATIVE)
            s_s[some, :lanes] = s
            here = jnp.max(s, axis=0, keepdims=True)
            top = here if top is None else jnp.maximum(top, here)
        total = jnp.zeros((1, lanes), F32)
        acc = jnp.zeros((2 * HEAD_DIM, lanes), F32)
        for m in range(count):
            pace.place()
            some = slice(m * TILE_K, (m + 1) * TILE_K)
            p = jnp.exp(s_s[some, :lanes] - top)
            total = total + jnp.sum(p, axis=0, keepdims=True)
            acc = acc + mm(vt[:, some], p.astype(BF16))
        o_ref[at : at + n, :] = narrowed(acc / total).astype(BF16)
        lse_ref[0, a : a + 1, :lanes] = top + jnp.log(total)
    pace.end()


class Exchange:
    def __init__(self, groups, blk, steps):
        self.groups, self.blk, self.steps = groups, blk, steps
        self.rows = groups * blk
        block = (steps, 2, groups, blk, 2 * HEAD_DIM)
        self.scratch = [pltpu.VMEM(block, BF16), pltpu.VMEM(block, BF16), pltpu.VMEM(block, F32)]
        sems = pltpu.SemaphoreType.DMA((steps,))
        self.scratch += [sems, sems]

    def copy(self, place, refs, n):
        gone, come, _, send, recv = refs
        mate = place.z + 1 - 2 * lax.rem(place.z, 2)
        return pltpu.make_async_remote_copy(
            src_ref=gone.at[n], dst_ref=come.at[n], send_sem=send.at[n], recv_sem=recv.at[n],
            device_id=(place.i, mate), device_id_type=MESH)

    def part_of(self, ref, part):
        base = pl.multiple_of(part * self.blk, self.blk)
        if self.groups == 1:
            return ref[pl.ds(base, self.blk), :][None]
        view = ref.reshape(ref.shape[0] // (2 * self.blk), 2 * self.blk, ref.shape[1])
        return view[0 : self.groups, pl.ds(base, self.blk), :]

    def give(self, place, refs, sums):
        n = pl.program_id(0)
        gone, _, kept, _, _ = refs
        part = lax.rem(place.z, 2)
        for which, ref in enumerate(sums):
            gone[n, which] = self.part_of(ref, 1 - part).astype(BF16)
            kept[n, which] = self.part_of(ref, part)
        self.copy(place, refs, n).start()

    def take(self, place, refs, out):
        _, come, kept, _, _ = refs
        cols = 2 * HEAD_DIM
        for n in range(self.steps):
            self.copy(place, refs, n).wait()
            for which in range(2):
                total = kept[n, which] + come[n, which].astype(F32)
                at = (which * self.steps + n) * cols
                out[:, at : at + cols] = total.reshape(self.rows, cols).astype(BF16)


def backward_kernel(biased, tiles, host, *refs):
    swap = None if host is None else host.swap
    refs, steps = split_refs(refs, host, 8, (4 if biased else 3) - (swap is not None))
    if swap is not None:
        swap_refs = refs[-len(swap.scratch) :]
        first = 10 + biased
        refs = refs[:first] + [None] + refs[first : -len(swap.scratch)]
    if biased:
        (
            q_ref, k_ref, v_ref, o_ref, do_ref, lse_ref, mask_ref, vec_ref,
            dq_ref, dist_ref, dv_ref, dk_ref, kt, dk_s, dv_s, strip, tail, slope, slope_tail, line,
        ) = refs
        keys_ref = None
        build_strips(tiles, vec_ref, strip, tail)
        slope[...] = jnp.zeros_like(slope)
        slope_tail[...] = jnp.zeros_like(slope_tail)
    else:
        (
            q_ref, k_ref, v_ref, o_ref, do_ref, lse_ref, mask_ref, keys_ref,
            dq_ref, dv_ref, dk_ref, kt, dk_s, dv_s,
        ) = refs
    kt[...] = k_ref[...].T
    dk_s[...] = jnp.zeros_like(dk_s)
    dv_s[...] = jnp.zeros_like(dv_s)
    counts = [tiles.keys(a) if biased else k_ref.shape[0] // TILE_K for a in range(len(tiles.list))]
    pace = Pace(steps, sum(counts))
    for a, (at, n) in enumerate(tiles.list):
        lanes = 4 * n
        q4 = widened(q_ref[at : at + n, :])
        do4 = widened(do_ref[at : at + n, :])
        mask = mask_ref[a : a + 1, :lanes]
        lse = lse_ref[0, a : a + 1, :lanes]
        both = widened(o_ref[at : at + n, :]).astype(F32) * do4.astype(F32)
        delta = jnp.sum(both.T, axis=0, keepdims=True)
        dq = jnp.zeros((2 * HEAD_DIM, lanes), F32)
        for m in range(counts[a]):
            pace.place()
            some = slice(m * TILE_K, (m + 1) * TILE_K)
            s = mm_nt(k_ref[some, :], q4)
            if biased:
                e = tiles.strip(a, m)
                s = s + (strip if n == TILE_Q else tail)[e]
            p = jnp.exp(jnp.where(tile_valid(biased, mask, keys_ref, m), s - lse, NEGATIVE))
            ds = p * (mm_nt(v_ref[some, :], do4) - delta)
            low = ds.astype(BF16)
            if biased:
                ref = slope if n == TILE_Q else slope_tail
                ref[e] += ds
            dv_s[some, :] += mm(p.astype(BF16), do4)
            dk_s[some, :] += mm(low, q4)
            dq = dq + mm(kt[:, some], low)
        dq_ref[at : at + n, :] = narrowed(dq).astype(BF16)

    if swap is None:
        dk_ref[...] = dk_s[...].astype(BF16)
        dv_ref[...] = dv_s[...].astype(BF16)
    else:
        place = Place(host.mp)
        swap.give(place, swap_refs, (dk_s, dv_s))
    if biased:
        width = tiles.width
        for h in range(4):
            line[...] = jnp.zeros_like(line)
            for ref in (slope, slope_tail):
                n = ref.shape[2] // 4
                for e, at, runs in tiles.windows(n):
                    for near, far in runs:
                        piece = ref[e, :, n * h + near : n * h + near + tiles.blk]
                        line[:, at + far : at + far + tiles.blk] += piece
            part = line[...]
            height = TILE_K
            while height > 8:
                height //= 2
                part = part[:height] + pltpu.roll(part[height:], width - height, axis=1)
            row = part[0:1]
            for j in range(1, 8):
                row = row + pltpu.roll(part, width - j, axis=1)[j : j + 1]
            dist_ref[0, h : h + 1, :] = row
    pace.end()
    if swap is not None:
        pl.when(pace.group == pace.groups - 1)(lambda: swap.take(place, swap_refs, dv_ref))


def spec(shape, index):
    return pl.BlockSpec(shape, index)


def attention_call(kernel, biased, tiles, outs, scratch, args, name, flops, host):
    steps = args[1].shape[1] // (2 * HEAD_DIM)

    def column(array, lanes):
        return spec((array.shape[0], lanes), lambda i: (0, i))

    def placed(array, kind):
        if kind == "wide":
            return column(array, 4 * HEAD_DIM)
        if kind == "key":
            return column(array, 2 * HEAD_DIM)
        if kind == "head":
            return spec((1,) + array.shape[1:], lambda i: (i, 0, 0))
        return spec(array.shape, lambda i: (0, 0))

    kinds = ["wide", "key", "key"]
    if kernel is backward_kernel:
        kinds += ["wide", "wide", "head"]
    kinds += ["flat", "head" if biased else "flat"]
    specs = [placed(array, kind) for array, kind in zip(args, kinds)]
    shapes = [item for item, _ in outs]
    out_specs = [placed(item, kind) for item, kind in outs]
    own = len(shapes)
    params = pltpu.CompilerParams(vmem_limit_bytes=60 << 20)
    args = list(args)
    if host is not None:
        args += host.args
        specs += host.in_specs
        shapes += host.outs
        out_specs += host.out_specs
        scratch = scratch + host.scratch
        params = host.params(62 << 20)
    found = pl.pallas_call(
        functools.partial(kernel, biased, tiles, host),
        grid=(steps,),
        out_shape=shapes,
        in_specs=specs,
        out_specs=out_specs,
        scratch_shapes=scratch,
        compiler_params=params,
        cost_estimate=pl.CostEstimate(flops=flops, bytes_accessed=16 << 20, transcendentals=0),
        name=name,
    )(*args)
    return found[:own], found[own:]


def strip_scratch(tiles):
    last = tiles.list[-1][1]
    return [
        pltpu.VMEM((tiles.strips, TILE_K, 4 * TILE_Q), F32),
        pltpu.VMEM((tiles.strips, TILE_K, 4 * last), F32),
    ]


def attend_forward(q, k, v, mask, extra, tiles, biased, name, host=None):
    steps = k.shape[1] // (2 * HEAD_DIM)
    outs = [
        (jax.ShapeDtypeStruct(q.shape, BF16), "wide"),
        (jax.ShapeDtypeStruct((steps,) + mask.shape, F32), "head"),
    ]
    scratch = [pltpu.VMEM((2 * HEAD_DIM, k.shape[0]), BF16), pltpu.VMEM((k.shape[0], 4 * TILE_Q), F32)]
    if biased:
        scratch += strip_scratch(tiles)
    flops = 4 * q.shape[0] * k.shape[0] * q.shape[1]
    return attention_call(
        forward_kernel, biased, tiles, outs, scratch, (q, k, v, mask, extra), name, flops, host
    )


def attend_backward(q, k, v, o, do, lse, mask, extra, tiles, biased, name, host=None):
    keys, cols = k.shape
    grad = jax.ShapeDtypeStruct(k.shape, BF16)
    outs = [(jax.ShapeDtypeStruct(q.shape, BF16), "wide")]
    scratch = [
        pltpu.VMEM((2 * HEAD_DIM, keys), BF16),
        pltpu.VMEM((keys, 2 * HEAD_DIM), F32),
        pltpu.VMEM((keys, 2 * HEAD_DIM), F32),
    ]
    if biased:
        outs.append((jax.ShapeDtypeStruct(extra.shape, F32), "head"))
        scratch += strip_scratch(tiles) * 2 + [pltpu.VMEM((TILE_K, tiles.width), F32)]
    if host is None:
        outs += [(grad, "key"), (grad, "key")]
    else:
        outs.append((jax.ShapeDtypeStruct((host.swap.rows, 2 * cols), BF16), "flat"))
        scratch += host.swap.scratch
    flops = 10 * q.shape[0] * keys * q.shape[1]
    return attention_call(
        backward_kernel, biased, tiles, outs, scratch, (q, k, v, o, do, lse, mask, extra), name,
        flops, host,
    )


def inverse_rms(state):
    return lax.rsqrt(jnp.mean(state * state, axis=-1, keepdims=True) + EPSILON)


def norm_back(state, gain, grad_normed):
    scale = inverse_rms(state)
    weighted = grad_normed * gain
    grad_gain = jnp.sum(grad_normed * state * scale, axis=0, keepdims=True)
    inner = jnp.mean(weighted * state, axis=-1, keepdims=True)
    return scale * weighted - state * (scale * scale * scale) * inner, grad_gain


def row_chunk(rows):
    for size in (272, 256, 128):
        if rows % size == 0:
            return size
    return rows


def full(array):
    return pl.BlockSpec(array.shape, lambda j, w: (0,) * len(array.shape))


def lead_block(array):
    return pl.BlockSpec((1,) + array.shape[1:], lambda j, w: (j,) + (0,) * (len(array.shape) - 1))


def col_block(array, parts):
    return pl.BlockSpec((array.shape[0], array.shape[1] // parts), lambda j, w: (0, j))


def row_block(array, parts):
    return pl.BlockSpec((array.shape[0] // parts, array.shape[1]), lambda j, w: (j, 0))


def kernel_call(body, name, steps, where, ins, outs, scratch, flops):
    return pl.pallas_call(
        lambda _, *refs: body(*refs),
        out_shape=[jax.ShapeDtypeStruct(a.shape, a.dtype) for a, _ in outs],
        grid_spec=pltpu.PrefetchScalarGridSpec(
            num_scalar_prefetch=1,
            grid=(steps,),
            in_specs=[s for _, s in ins],
            out_specs=[s for _, s in outs],
            scratch_shapes=scratch,
        ),
        compiler_params=pltpu.CompilerParams(vmem_limit_bytes=60 << 20),
        cost_estimate=pl.CostEstimate(flops=flops, bytes_accessed=16 << 20, transcendentals=0),
        name=name,
    )(where, *[a for a, _ in ins])


def my_rows(array):
    block = (None, array.shape[1], None) + array.shape[3:]
    return array, pl.BlockSpec(block, lambda j, w: (w[0], 0, w[1], 0, 0))


def my_sequence(array):
    return array, pl.BlockSpec((None,) + array.shape[1:], lambda j, w: (w[0], 0, 0))


def flat(ref):
    return ref.reshape(ref.shape[0] * ref.shape[1], ref.shape[2])


def shape(dims, dtype=BF16):
    return jax.ShapeDtypeStruct(dims, dtype)


def project_kernel(x_ref, own_ref, gain_ref, w_ref, q_ref, k_ref, v_ref, n_ref, normed):
    length = x_ref.shape[0]
    qcols = q_ref.shape[1]
    kcols = k_ref.shape[1]
    size = row_chunk(length)

    @pl.when(pl.program_id(0) == 0)
    def _():
        def norm_rows(at):
            x = x_ref[pl.ds(at, size), :].astype(F32)
            normed[pl.ds(at, size), :] = (x * inverse_rms(x) * gain_ref[...]).astype(BF16)

        chunked(length, size, norm_rows)
        x = flat(own_ref)[...].astype(F32)
        n_ref[...] = (x * inverse_rms(x) * gain_ref[...]).astype(BF16)

    q_ref[...] = mm(n_ref[...], w_ref[0, :, :qcols]).astype(BF16)

    def keys(at):
        kv = mm(normed[pl.ds(at, size), :], w_ref[0, :, qcols:]).astype(BF16)
        k_ref[pl.ds(at, size), :] = kv[:, :kcols]
        v_ref[pl.ds(at, size), :] = kv[:, kcols:]

    chunked(length, size, keys)
    k_ref[length:, :] = jnp.zeros((k_ref.shape[0] - length, kcols), BF16)
    v_ref[length:, :] = jnp.zeros((k_ref.shape[0] - length, kcols), BF16)


def self_project(where, x, own, gain, w, reach, rows):
    _, length, width = x.shape
    groups, _, cols = w.shape
    q, k = shape((rows, groups * cols // 2)), shape((reach, groups * cols // 4))
    n = shape((rows, width))
    return kernel_call(
        project_kernel, "self_project", groups, where,
        [my_sequence(x), my_rows(own), (gain, full(gain)), (w, lead_block(w))],
        [(q, col_block(q, groups)), (k, col_block(k, groups)), (k, col_block(k, groups)), (n, full(n))],
        [pltpu.VMEM((length, width), BF16)], (length + rows) * width * groups * cols,
    )


def middle_kernel(o_ref, wo_ref, x_ref, gain_ref, m_ref, w_ref, h_ref, n_ref, q_ref, k_ref, v_ref):
    rows, qcols = q_ref.shape
    kcols = k_ref.shape[1]
    size = row_chunk(rows)
    x_ref = flat(x_ref)

    @pl.when(pl.program_id(0) == 0)
    def _():
        def state(at):
            some = pl.ds(at, size)
            h = x_ref[some, :].astype(F32) + mm(o_ref[some, :], wo_ref[...])
            h_ref[some, :] = h
            n_ref[some, :] = (h * inverse_rms(h) * gain_ref[...]).astype(BF16)

        chunked(rows, size, state)

    q_ref[...] = mm(n_ref[...], w_ref[0, :, :qcols]).astype(BF16)
    kv = mm(m_ref[...], w_ref[0, :, qcols:]).astype(BF16)
    k_ref[...] = kv[:, :kcols]
    v_ref[...] = kv[:, kcols:]


def cross_project(where, o, wo, own, gain, memory, w):
    rows, width = o.shape
    groups, _, cols = w.shape
    h, n = shape((rows, width), F32), shape((rows, width))
    q = shape(o.shape)
    k = shape((memory.shape[1], groups * cols // 4))
    return kernel_call(
        middle_kernel, "cross_project", groups, where,
        [(o, full(o)), (wo, full(wo)), my_rows(own), (gain, full(gain)), my_sequence(memory),
         (w, lead_block(w))],
        [(h, full(h)), (n, full(n)), (q, col_block(q, groups)), (k, col_block(k, groups)),
         (k, col_block(k, groups))],
        [], 6 * rows * width * width,
    )


def gate_parts(value):
    square = value * value
    inner = jnp.tanh(0.7978845608028654 * (value + 0.044715 * square * value))
    half = 0.5 * (1.0 + inner)
    slope = 0.7978845608028654 * (1.0 + 3.0 * 0.044715 * square)
    return value * half, half + 0.5 * value * (1.0 - inner * inner) * slope


def feed_kernel(
    o_ref, wo_ref, h1_ref, gain_ref, up_ref, wg_ref, wu_ref, wd_ref,
    out_ref, g2_ref, gain_out, gwg_ref, gwu_ref, gwd_ref, do_ref, gwo_ref,
    h2, normed, total, back, hidden_s, dgate_s, dup_s,
):
    rows, width = h1_ref.shape
    j = pl.program_id(0)
    size = row_chunk(rows)
    up_ref = flat(up_ref)

    @pl.when(j == 0)
    def _():
        def state(at):
            some = pl.ds(at, size)
            h = h1_ref[some, :] + mm(o_ref[some, :], wo_ref[...])
            h2[some, :] = h
            normed[some, :] = (h * inverse_rms(h) * gain_ref[...]).astype(BF16)
            total[some, :] = h
            back[some, :] = jnp.zeros((size, width), F32)

        chunked(rows, size, state)

    def hidden_rows(at):
        some = pl.ds(at, size)
        n = normed[some, :]
        g = up_ref[some, :]
        gate = mm(n, wg_ref[0])
        up = mm(n, wu_ref[0])
        grad_hidden = mm_nt(g, wd_ref[...])
        active, pull = gate_parts(gate)
        hidden = (active * up).astype(BF16)
        grad_gate = (grad_hidden * up * pull).astype(BF16)
        grad_up = (grad_hidden * active).astype(BF16)
        hidden_s[some, :] = hidden
        dgate_s[some, :] = grad_gate
        dup_s[some, :] = grad_up
        total[some, :] += mm(hidden, wd_ref[...])
        back[some, :] += mm_nt(grad_gate, wg_ref[0]) + mm_nt(grad_up, wu_ref[0])

    chunked(rows, size, hidden_rows)

    def weight_rows(at):
        some = pl.ds(at, 512)
        n = normed[:, some]
        gwg_ref[0, some, :] = mm_tn(n, dgate_s[...]).astype(BF16)
        gwu_ref[0, some, :] = mm_tn(n, dup_s[...]).astype(BF16)
        gwd_ref[:, some] = mm_tn(hidden_s[...], up_ref[:, some]).astype(BF16)

    chunked(width, 512, weight_rows)

    @pl.when(j == pl.num_programs(0) - 1)
    def _():
        gain_out[...] = jnp.zeros_like(gain_out)
        do_ref[...] = jnp.zeros_like(do_ref)

        def finish(at):
            some = pl.ds(at, size)
            out_ref[some, :] = total[some, :].astype(BF16)
            change, grad_gain = norm_back(h2[some, :], gain_ref[...], back[some, :])
            gain_out[...] += grad_gain
            g2 = up_ref[some, :].astype(F32) + change
            g2_ref[some, :] = g2
            low = g2.astype(BF16)
            normed[some, :] = low
            do_ref[some, :] = mm_nt(low, wo_ref[...]).astype(BF16)

        chunked(rows, size, finish)

        def out_rows(at):
            some = pl.ds(at, 512)
            gwo_ref[some, :] = mm_tn(o_ref[0:rows, some], normed[...]).astype(BF16)

        chunked(width, 512, out_rows)


def feed(where, o, wo, h1, gain, upstream, wg, wu, wd):
    rows, width = h1.shape
    groups, _, cols = wg.shape
    out, g2, gg = shape(h1.shape), shape(h1.shape, F32), shape((1, width), F32)
    return kernel_call(
        feed_kernel, "feed", groups, where,
        [(o, full(o)), (wo, full(wo)), (h1, full(h1)), (gain, full(gain)), my_rows(upstream),
         (wg, lead_block(wg)), (wu, lead_block(wu)), (wd, row_block(wd, groups))],
        [(out, full(out)), (g2, full(g2)), (gg, full(gg)), (wg, lead_block(wg)), (wu, lead_block(wu)),
         (wd, row_block(wd, groups)), (o, full(o)), (wo, full(wo))],
        [pltpu.VMEM((rows, width), F32), pltpu.VMEM((rows, width), BF16), pltpu.VMEM((rows, width), F32),
         pltpu.VMEM((rows, width), F32)] + [pltpu.VMEM((rows, cols), BF16)] * 3,
        18 * rows * width * groups * cols,
    )


def back_kernel(
    dq_ref, w_ref, n_ref, h_ref, gain_ref, g2_ref, wo_ref, o_ref,
    gw_ref, g1_ref, gain_out, do_ref, gwo_ref, back, low_s,
):
    rows, width = h_ref.shape
    qcols = dq_ref.shape[1]
    j = pl.program_id(0)
    size = row_chunk(rows)

    @pl.when(j == 0)
    def _():
        back[...] = jnp.zeros_like(back)

    back[...] += mm_nt(dq_ref[0:rows, :], w_ref[0, :, :qcols])

    def weight_rows(at):
        some = pl.ds(at, 512)
        gw_ref[0, some, :] = mm_tn(n_ref[:, some], dq_ref[0:rows, :]).astype(BF16)

    chunked(width, 512, weight_rows)

    @pl.when(j == pl.num_programs(0) - 1)
    def _():
        gain_out[...] = jnp.zeros_like(gain_out)
        do_ref[...] = jnp.zeros_like(do_ref)

        def finish(at):
            some = pl.ds(at, size)
            change, grad_gain = norm_back(h_ref[some, :], gain_ref[...], back[some, :])
            gain_out[...] += grad_gain
            g1 = g2_ref[some, :] + change
            g1_ref[some, :] = g1
            low = g1.astype(BF16)
            low_s[some, :] = low
            do_ref[some, :] = mm_nt(low, wo_ref[...]).astype(BF16)

        chunked(rows, size, finish)

        def out_rows(at):
            some = pl.ds(at, 512)
            gwo_ref[some, :] = mm_tn(o_ref[0:rows, some], low_s[...]).astype(BF16)

        chunked(width, 512, out_rows)


def cross_back(where, dq, w, n, h, gain, g2, wo, o):
    rows, width = h.shape
    groups, _, cols = w.shape
    gw = shape((groups, width, cols // 2))
    gg = shape((1, width), F32)
    return kernel_call(
        back_kernel, "cross_back", groups, where,
        [(dq, col_block(dq, groups)), (w, lead_block(w)), (n, full(n)), (h, full(h)), (gain, full(gain)),
         (g2, full(g2)), (wo, full(wo)), (o, full(o))],
        [(gw, lead_block(gw)), (g2, full(g2)), (gg, full(gg)), (o, full(o)), (wo, full(wo))],
        [pltpu.VMEM((rows, width), F32), pltpu.VMEM((rows, width), BF16)],
        8 * rows * width * width,
    )


def memory_kernel(dk_ref, dv_ref, w_ref, m_ref, gw_ref, gm_ref, back):
    j = pl.program_id(0)
    qcols = w_ref.shape[2] // 2

    @pl.when(j == 0)
    def _():
        back[...] = jnp.zeros_like(back)

    both = jnp.concatenate([dk_ref[...], dv_ref[...]], axis=1)
    back[...] += mm_nt(both, w_ref[0, :, qcols:])
    gw_ref[0] = mm_tn(m_ref[...], both).astype(BF16)

    @pl.when(j == pl.num_programs(0) - 1)
    def _():
        gm_ref[...] = back[...].astype(BF16)


def key_halves(dkv, groups):
    cols = dkv.shape[1] // (2 * groups)
    return [
        (dkv, pl.BlockSpec((dkv.shape[0], cols), lambda j, w: (0, j))),
        (dkv, pl.BlockSpec((dkv.shape[0], cols), lambda j, w: (0, j + groups))),
    ]


def memory_back(where, dkv, w, memory):
    groups, width, cols = w.shape
    gw, gm = shape((groups, width, cols // 2)), shape((dkv.shape[0], width))
    rows = pl.BlockSpec((None,) + gm.shape, lambda j, w: (w[0], w[1], 0))
    return kernel_call(
        memory_kernel, "memory_back", groups, where,
        key_halves(dkv, groups) + [(w, lead_block(w)), (memory, rows)],
        [(gw, lead_block(gw)), (gm, full(gm))],
        [pltpu.VMEM(gm.shape, F32)], 4 * gm.shape[0] * width * width,
    )


def last_kernel(
    dq_ref, dk_ref, dv_ref, w_ref, n_ref, x_ref, gain_ref, g1_ref,
    gwq_ref, gwkv_ref, gx_ref, gain_out, back,
):
    rows, width = g1_ref.shape
    j = pl.program_id(0)
    size = row_chunk(rows)
    x_ref = flat(x_ref)

    @pl.when(j == 0)
    def _():
        back[...] = jnp.zeros_like(back)

    dq = dq_ref[0:rows, :]
    dkv = jnp.concatenate([dk_ref[...], dv_ref[...]], axis=1)
    both = jnp.concatenate([dq, dkv], axis=1)
    back[...] += mm_nt(both, w_ref[0])

    def weight_rows(at):
        some = pl.ds(at, 512)
        gwq_ref[0, some, :] = mm_tn(n_ref[:, some], dq).astype(BF16)
        gwkv_ref[0, some, :] = mm_tn(n_ref[:, some], dkv).astype(BF16)

    chunked(width, 512, weight_rows)

    @pl.when(j == pl.num_programs(0) - 1)
    def _():
        gain_out[...] = jnp.zeros_like(gain_out)

        def finish(at):
            some = pl.ds(at, size)
            change, grad_gain = norm_back(x_ref[some, :].astype(F32), gain_ref[...], back[some, :])
            gain_out[...] += grad_gain
            gx_ref[some, :] = (g1_ref[some, :] + change).astype(BF16)

        chunked(rows, size, finish)


def self_back(where, dq, dkv, w, n, own, gain, g1):
    rows, width = g1.shape
    groups, _, cols = w.shape
    gw = shape((groups, width, cols // 2))
    gx = shape(g1.shape)
    gg = shape((1, width), F32)
    return kernel_call(
        last_kernel, "self_back", groups, where,
        [(dq, col_block(dq, groups))] + key_halves(dkv, groups)
        + [(w, lead_block(w)), (n, full(n)), my_rows(own), (gain, full(gain)), (g1, full(g1))],
        [(gw, lead_block(gw)), (gw, lead_block(gw)), (gx, full(gx)), (gg, full(gg))],
        [pltpu.VMEM((rows, width), F32)],
        8 * rows * width * width,
    )


def gather(shard, dims):
    for axis, name in dims:
        shard = lax.all_gather(shard, name, axis=axis, tiled=True)
    return shard


ROWS_BY_DP = ((0, "dp"), (1, "mp"))
ROWS_BY_MP = ((1, "dp"), (0, "mp"))


def scatter(grad, dims):
    for axis, name in dims:
        grad = lax.psum_scatter(grad, name, scatter_dimension=axis, tiled=True)
    return grad.astype(F32)


def grouped(weight, groups):
    rows, cols = weight.shape
    return weight.reshape(rows, groups, cols // groups).transpose(1, 0, 2)


def ungrouped(weight):
    groups, rows, cols = weight.shape
    return weight.transpose(1, 0, 2).reshape(rows, groups * cols)


def body(
    inputs,
    encoded,
    decoder_segments,
    encoder_segments,
    buckets,
    self_gain,
    self_query,
    self_key,
    self_value,
    self_out,
    position_bias,
    cross_gain,
    cross_query,
    cross_key,
    cross_value,
    cross_out,
    feed_gain,
    feed_gate,
    feed_up,
    feed_down,
    cotangent,
    *,
    dp,
    mp,
):
    batches, length, width = inputs.shape
    enc_length = encoded.shape[1]
    parts = mp // batches
    rows = length // parts
    tiles = Tiles(rows, length, parts)
    place = lax.axis_index("mp")
    sequence = place // parts
    part = place % parts
    where = jnp.stack([sequence, part]).astype(jnp.int32)
    groups = self_key.shape[1] * mp // (2 * HEAD_DIM)
    native = mp == groups and dp == 8 and parts == 2

    if native:
        order = ["by_dp", "by_mp"]
        size = width // dp
        gains = jnp.stack([self_gain, cross_gain, feed_gain])
        little = jnp.pad(position_bias.reshape(1, -1), ((0, 0), (0, size - position_bias.size)))
        little = jnp.pad(jnp.concatenate([gains, little]), ((0, 12), (0, 0)))
        w1 = jnp.concatenate([self_query, self_key, self_value], axis=1)
        w2 = jnp.concatenate([cross_query, cross_key, cross_value], axis=1)
        w1, little, wo1 = Transfers(
            dp, mp, 1, [w1, little, self_out], ["by_dp"] + order
        ).run("gather_self")
        gains = little[0, :, :3].transpose(1, 0, 2).reshape(3, 1, width).astype(F32)
        table = little[:, :, 3, : position_bias.size].reshape((mp, dp) + position_bias.shape)
        table = table.transpose(1, 2, 0, 3).reshape(dp * position_bias.shape[0], -1).astype(F32)
        w1 = w1.reshape(mp, width, w1.shape[3])
    else:
        gains = [gather(g, ((0, "dp"),)).astype(F32)[None] for g in (self_gain, cross_gain, feed_gain)]
        table = gather(position_bias, ROWS_BY_DP).astype(F32)

        def blocks(*shards):
            return jnp.concatenate([grouped(gather(s, ROWS_BY_DP), groups) for s in shards], axis=2)

        w1 = blocks(self_query, self_key, self_value)
        w2 = blocks(cross_query, cross_key, cross_value)
        wg, wu = blocks(feed_gate), blocks(feed_up)
        wo1, wo2, wd = (gather(s, ROWS_BY_MP) for s in (self_out, cross_out, feed_down))
    gain_one, gain_two, gain_three = gains

    def cut(array):
        return array.reshape((array.shape[0], length // 64, parts, 64 // parts) + array.shape[2:])

    own_inputs = cut(inputs)
    docs = lax.dynamic_index_in_dim(decoder_segments, sequence, keepdims=False)
    enc_docs = lax.dynamic_index_in_dim(encoder_segments, sequence, keepdims=False)
    own_docs = lax.dynamic_slice_in_dim(docs.reshape(length // 64, 64), part * tiles.blk, tiles.blk, axis=1)
    own_docs = own_docs.reshape(rows)

    kinds = jnp.arange(4, dtype=jnp.int32)
    before = jnp.sum((docs[None, :] < kinds[:, None]).astype(jnp.int32), axis=1)
    is_doc = (own_docs[:, None] == kinds[None, :]).astype(jnp.int32)
    start = jnp.sum(is_doc * before[None, :], axis=1)

    def by_tile(row):
        found = []
        for at, n in tiles.list:
            piece = jnp.tile(row[at : at + n], 4)
            found.append(jnp.pad(piece, (0, 4 * (TILE_Q - n))))
        return jnp.stack(found)

    mask_one = by_tile(start)
    mask_two = by_tile(own_docs)
    keys_two = jnp.broadcast_to(enc_docs[:, None], (enc_length, TILE_Q))
    onehot = (buckets[:, None] == jnp.arange(table.shape[0], dtype=jnp.int32)).astype(F32)
    by_distance = dot(table, onehot, ((0,), (1,)), HIGHEST)
    heads = by_distance.shape[0]
    vec = jnp.pad(by_distance, ((0, 0), (0, tiles.width)))
    vec = jnp.concatenate([jnp.full((heads, tiles.lead), NEGATIVE, F32), vec], axis=1)
    vec = lax.dynamic_slice_in_dim(vec, part * tiles.blk, tiles.width, axis=1)
    vec = vec.reshape(heads // 4, 4, tiles.width)

    q1, k1, v1, n1 = self_project(where, inputs, own_inputs, gain_one, w1, tiles.reach, rows)
    hosts = [None] * 4
    if native:
        hosts[0] = Transfers(dp, mp, 2, [w2, cross_out, feed_gate], order + ["by_dp"])
        hosts[1] = Transfers(dp, mp, 3, [feed_up, feed_down], order)
    (o1, lse_one), found = attend_forward(
        q1, k1, v1, mask_one, vec, tiles, True, "self_forward", hosts[0]
    )
    if native:
        w2, wo2, wg = found
        w2, wg = (w.reshape(mp, width, w.shape[3]) for w in (w2, wg))
    h1, n2, q2, k2, v2 = cross_project(where, o1, wo1, own_inputs, gain_two, encoded, w2)
    (o2, lse_two), found = attend_forward(
        q2, k2, v2, mask_two, keys_two, tiles, False, "cross_forward", hosts[1]
    )
    if native:
        wu, wd = found
        wu = wu.reshape(mp, width, wu.shape[3])

    result, grad_two, grad_gain_three, gwg, gwu, gwd, do2, gwo2 = feed(
        where, o2, wo2, h1, gain_three, cut(cotangent), wg, wu, wd
    )

    def collect(array):
        array = lax.all_gather(array, "mp", axis=0, tiled=True)
        array = array.reshape(batches, parts, length // 64, tiles.blk, width)
        return array.transpose(0, 2, 1, 3, 4).reshape(batches, length, width)

    def pieces(grad):
        return grad.reshape(grad.shape[0], dp, grad.shape[1] // dp, grad.shape[2])

    sharing = [[s * parts + p for p in range(parts)] for s in range(batches)]

    def share(dk, dv, count):
        both = jnp.concatenate([dk, dv], axis=1)
        both = both.reshape(count, parts, -1, both.shape[1]).transpose(1, 0, 2, 3)
        both = both.reshape(-1, both.shape[3])
        return lax.psum_scatter(
            both, "mp", scatter_dimension=0, axis_index_groups=sharing, tiled=True
        )

    if native:
        hosts[2] = Transfers(
            dp, mp, 4, grads=[gwd], rows=[result.reshape(length // 64, tiles.blk, width)],
            spread=[(batches, length // 64, parts, tiles.blk, width)],
        )
        hosts[2].swap = Exchange(1, enc_length // 2, groups)
    (dq2, *dkv2), sums_down = attend_backward(
        q2, k2, v2, o2, do2, lse_two, mask_two, keys_two, tiles, False, "cross_backward", hosts[2]
    )
    if native:
        dkv2 = dkv2[0]
        *sums_down, outputs = sums_down
        outputs = outputs.reshape(inputs.shape)
    else:
        dkv2 = share(dkv2[1], dkv2[0], 1)
        outputs = collect(result)
    gwq2, grad_one, grad_gain_two, do1, gwo1 = cross_back(
        where, dq2, w2, n2, h1, gain_two, grad_two, wo1, o1
    )
    gwkv2, grad_memory = memory_back(where, dkv2, w2, encoded)

    if native:
        line = grad_memory.reshape(1, -1, width)
        hosts[3] = Transfers(
            dp, mp, 5, grads=[pieces(gwg), pieces(gwu)], rows=[line],
            spread=[(batches, 1, parts, enc_length // parts, width)],
        )
        hosts[3].swap = Exchange(length // 64, tiles.blk, groups)
    (dq1, slopes, *dkv1), sums_feed = attend_backward(
        q1, k1, v1, o1, do1, lse_one, mask_one, vec, tiles, True, "self_backward", hosts[3]
    )
    if native:
        dkv1 = dkv1[0]
        *sums_feed, grad_encoded = sums_feed
        grad_encoded = grad_encoded.reshape(encoded.shape)
    else:
        dkv1 = share(dkv1[1][:length], dkv1[0][:length], length // 64)
        grad_encoded = lax.all_gather(grad_memory, "mp", axis=0, tiled=True).reshape(encoded.shape)
    gwq1, gwkv1, grad_rows, grad_gain_one = self_back(
        where, dq1, dkv1, w1, n1, own_inputs, gain_one, grad_one
    )
    slopes = slopes.reshape(heads, tiles.width)
    slopes = jnp.pad(slopes, ((0, 0), (64, length)))
    slopes = lax.dynamic_slice_in_dim(slopes, 64 + tiles.lead - part * tiles.blk, length, axis=1)
    grad_table = dot(onehot, slopes, ((0,), (1,)), HIGHEST)
    grad_gains = jnp.concatenate([grad_gain_one, grad_gain_two, grad_gain_three])

    kcols = gwkv1.shape[2] // 2
    if native:
        little = grad_gains.reshape(3, dp, size).transpose(1, 0, 2)
        little = jnp.broadcast_to(little[None], (mp, dp, 3, size))
        spots = grad_table.reshape(dp, position_bias.shape[0], mp, position_bias.shape[1])
        spots = spots.transpose(2, 0, 1, 3).reshape(mp, dp, 1, position_bias.size)
        spots = jnp.pad(spots, ((0, 0), (0, 0), (0, 4), (0, size - position_bias.size)))
        little = jnp.concatenate([little, spots], axis=2)
        grads = [pieces(g) for g in (gwq2, gwkv2, gwq1, gwkv1)] + [gwo2, gwo1, little]
        *sums, little, grad_inputs = Transfers(
            dp, mp, 6, grads=grads, rows=[grad_rows.reshape(length // 64, tiles.blk, width)],
            spread=[(batches, length // 64, parts, tiles.blk, width)],
        ).run("scatter_rest")
        grad_inputs = grad_inputs.reshape(inputs.shape)
        sums = sums + list(sums_feed) + list(sums_down)
        gwq2, gwkv2, gwq1, gwkv1, gwo2, gwo1, gwg, gwu, gwd = sums
        gwk2, gwv2, gwk1, gwv1 = (
            g[:, at : at + kcols] for g in (gwkv2, gwkv1) for at in (0, kcols)
        )
        grad_gains = [little[n] for n in range(3)]
        grad_table = little[3, : position_bias.size].reshape(position_bias.shape)
    else:
        grad_inputs = collect(grad_rows)

        def summed(grad):
            return scatter(ungrouped(grad), ROWS_BY_DP)

        gwk1, gwv1 = summed(gwkv1[:, :, :kcols]), summed(gwkv1[:, :, kcols:])
        gwk2, gwv2 = summed(gwkv2[:, :, :kcols]), summed(gwkv2[:, :, kcols:])
        gwq1, gwq2, gwg, gwu = (summed(g) for g in (gwq1, gwq2, gwg, gwu))
        gwo1, gwo2, gwd = (scatter(g, ROWS_BY_MP) for g in (gwo1, gwo2, gwd))
        small = jnp.concatenate([grad_gains.reshape(-1), grad_table.reshape(-1)])
        small = lax.psum(small, ("dp", "mp"))
        data = lax.axis_index("dp")
        grad_gains = lax.dynamic_slice_in_dim(
            small[: 3 * width].reshape(3, dp, width // dp), data, 1, axis=1
        )
        grad_gains = [grad_gains[n, 0] for n in range(3)]
        grad_table = lax.dynamic_slice(
            small[3 * width :].reshape(table.shape),
            (data * position_bias.shape[0], place * position_bias.shape[1]),
            position_bias.shape,
        )

    return (
        outputs, grad_inputs, grad_encoded,
        grad_gains[0], gwq1, gwk1, gwv1, gwo1, grad_table,
        grad_gains[1], gwq2, gwk2, gwv2, gwo2,
        grad_gains[2], gwg, gwu, gwd,
    )


def solution(mesh):
    rows3 = P("dp", None, None)
    by_dp = P("dp", "mp")
    by_mp = P("mp", "dp")
    gain = P("dp")
    return jax.shard_map(
        functools.partial(body, dp=mesh.shape["dp"], mp=mesh.shape["mp"]),
        mesh=mesh,
        in_specs=(
            rows3, rows3, P("dp", None), P("dp", None), P(),
            gain, by_dp, by_dp, by_dp, by_mp, by_dp,
            gain, by_dp, by_dp, by_dp, by_mp,
            gain, by_dp, by_dp, by_mp, rows3,
        ),
        out_specs=(
            rows3, rows3, rows3,
            gain, by_dp, by_dp, by_dp, by_mp, by_dp,
            gain, by_dp, by_dp, by_dp, by_mp,
            gain, by_dp, by_dp, by_mp,
        ),
        check_vma=False,
    )
```

```python
import functools

import jax
import jax.numpy as jnp
from jax import lax
from jax.experimental import pallas as pl
from jax.experimental.pallas import tpu as pltpu
from jax.sharding import PartitionSpec as P

HEAD_DIM = 64
TILE_Q = 128
TILE_K = 256
EPSILON = 1e-06
NEGATIVE = -1e30
HIGHEST = lax.Precision.HIGHEST
F32 = jnp.float32
BF16 = jnp.bfloat16


def dot(left, right, dims, precision=None):
    return lax.dot_general(
        left, right, ((dims[0], dims[1]), ((), ())), precision=precision, preferred_element_type=F32
    )


def mm(left, right):
    return dot(left, right, ((1,), (0,)))


def mm_nt(left, right):
    return dot(left, right, ((1,), (1,)))


def mm_tn(left, right):
    return dot(left, right, ((0,), (0,)))


def round_up(value, unit):
    return (value + unit - 1) // unit * unit


def chunked(total, size, run):
    def once(n, carry):
        run(pl.multiple_of(n * size, size))
        return carry

    lax.fori_loop(0, total // size, once, 0)


MESH = pl.DeviceIdType.MESH


class Place:
    def __init__(self, mp):
        self.mp = mp
        self.i = lax.axis_index("dp")
        self.z = lax.axis_index("mp")
        core = lax.rem(self.i, 2)
        across = lax.rem(lax.div(self.i, 2), 2)
        up = lax.div(self.i, 4)
        self.core, self.across, self.up = core, across, up
        self.ic = self.i + 1 - 2 * core
        self.ix = self.i + 2 - 4 * across
        self.iy = self.i + 4 - 8 * up
        self.ixy = self.ix + 4 - 8 * up


def enter(place):
    barrier = pltpu.get_barrier_semaphore()
    z, mp = place.z, place.mp
    for near in (place.ic, place.ix, place.iy):
        pl.semaphore_signal(barrier, 1, device_id=(near, z), device_id_type=MESH)

    for d in range(1, mp):
        far = lax.rem(z + d, mp)
        pl.semaphore_signal(barrier, 1, device_id=(place.i, far), device_id_type=MESH)
    pl.semaphore_wait(barrier, 3 + mp - 1)


def nearest(z):
    upper = lax.div(z, 2)
    return [z, z + 1 - 2 * lax.rem(z, 2), 2 - upper, 3 - 3 * upper]


def onward(place, z2, act):
    z = place.z
    if z2 is z:
        pl.when(z < place.mp - 1)(lambda: act(True))
        pl.when(z > 0)(lambda: act(False))
    else:
        pl.when(jnp.logical_and(z2 < z, z < place.mp - 1))(lambda: act(True))
        pl.when(jnp.logical_and(z2 > z, z > 0))(lambda: act(False))


def staggered(slots, stages):
    def step(k):
        for late, stage in enumerate(stages):
            if 0 <= k - late < len(slots):
                stage(slots[k - late])

    return [functools.partial(step, k) for k in range(len(slots) + len(stages) - 1)]


def region(ref, i, z, shard):
    if len(ref.shape) == 4:
        return ref.at[z, i]
    rows, cols = shard
    return ref.at[pl.ds(pl.multiple_of(z * rows, rows), rows), pl.ds(pl.multiple_of(i * cols, cols), cols)]


def gather_steps(place, shards, outs, send, recv, local):
    mp, i, z = place.mp, place.i, place.z
    units = range(len(shards))

    def here(u, i2, z2):
        return region(outs[u], i2, z2, shards[u].shape)

    def copy(u, kind, i2, z2, to, src=None):
        spot = here(u, i2, z2)
        return pltpu.make_async_remote_copy(
            src_ref=spot if src is None else src, dst_ref=spot, send_sem=send.at[u, kind, z2],
            recv_sem=recv.at[u, kind, z2], device_id=to, device_id_type=MESH)

    def route(u, z2):
        odd = lax.rem(z2 + u, 2)
        first = place.ix + odd * (place.iy - place.ix)
        second = place.iy + odd * (place.ix - place.iy)
        return odd, first, second

    slots = nearest(z)

    def stage1(z2):
        for u in units:
            src = shards[u] if z2 is z else None
            if z2 is not z:
                copy(u, 0, i, z2, (i, z)).wait_recv()
            copy(u, 2, i, z2, (place.ix, z), src).start()
            copy(u, 3, i, z2, (place.iy, z), src).start()
            copy(u, 5, i, z2, (place.ic, z), src).start()
            if z2 is z:
                pltpu.make_async_copy(shards[u], here(u, i, z), local.at[u]).start()

    def along(u, d, up):
        return pltpu.make_async_remote_copy(
            src_ref=shards[u], dst_ref=here(u, i, z), send_sem=send.at[u, 0 if up else 1, d],
            recv_sem=recv.at[u, 0, z], device_id=(i, z + d if up else z - d),
            device_id_type=MESH)

    def depart():
        for d in range(1, mp):
            for u in units:
                pl.when(z < mp - d)(lambda u=u, d=d: along(u, d, True).start())
                pl.when(z >= d)(lambda u=u, d=d: along(u, d, False).start())

    def stage2(z2):
        for u in units:
            odd, first, second = route(u, z2)
            arrived(u, 2 + odd, first, z2)
            copy(u, 4, first, z2, (second, z)).start()
            copy(u, 6, first, z2, (place.ic, z)).start()

    def stage3(z2):
        for u in units:
            odd, first, second = route(u, z2)
            arrived(u, 3 - odd, second, z2)
            copy(u, 7, second, z2, (place.ic, z)).start()
            copy(u, 4, place.ixy, z2, (second, z)).wait_recv()
            copy(u, 8, place.ixy, z2, (place.ic, z)).start()

    def arrived(u, kind, i2, z2):
        spot = here(u, i2, z2)
        pltpu.make_async_remote_copy(
            src_ref=spot, dst_ref=spot, send_sem=send.at[u, kind, z2], recv_sem=recv.at[u, kind, z2],
            device_id=(i2, z), device_id_type=MESH).wait_recv()

    def other(i2):
        return i2 + place.ic - i

    def finish(z2):
        for u in units:
            odd, first, second = route(u, z2)
            for kind, i2 in ((5, i), (6, first), (7, second), (8, place.ixy)):
                copy(u, kind, other(i2), z2, (place.ic, z)).wait_recv()
            for kind in range(2, 9):
                copy(u, kind, i, z2, (i, z)).wait_send()
            if z2 is z:
                for far in range(1, mp):
                    pl.when(z < mp - far)(lambda u=u, far=far: along(u, far, True).wait_send())
                    pl.when(z >= far)(lambda u=u, far=far: along(u, far, False).wait_send())
                pltpu.make_async_copy(shards[u], here(u, i, z), local.at[u]).wait()

    steps = staggered(slots, (stage1, stage2, stage3))
    return [depart, steps[0]], steps[1:], [functools.partial(finish, slot) for slot in slots]


def gather_shape(shard, kind, dp, mp):
    rows, cols = shard.shape
    if kind == "by_dp":
        return jax.ShapeDtypeStruct((mp, dp, rows, cols), shard.dtype)
    return jax.ShapeDtypeStruct((mp * rows, dp * cols), shard.dtype)


def add_into(target, *others):
    rows = target.shape[0]
    size = 64 if rows % 64 == 0 else rows

    def some(at):
        part = pl.ds(at, size)
        total = target[part, :].astype(F32)
        for other in others:
            total = total + other[part, :].astype(F32)
        target[part, :] = total.astype(target.dtype)

    chunked(rows, size, some)


def scatter_scratch(shards, mp):
    scratch = []
    for dims, dtype in shards:
        scratch += [
            pltpu.VMEM((mp, 4) + dims, dtype),
            pltpu.VMEM((mp, 4) + dims, dtype),
            pltpu.VMEM((mp, 3) + dims, dtype),
            pltpu.VMEM((mp,) + dims, dtype),
        ]
    sems = pltpu.SemaphoreType.DMA((len(shards), 8, mp))
    return scratch + [sems, sems, pltpu.SemaphoreType.DMA((len(shards), 4, mp))]


def scatter_steps(place, grads, outs, scratch):
    mp, i, z = place.mp, place.i, place.z
    units = range(len(grads))
    send, recv, local = scratch[-3:]
    own = [scratch[4 * u] for u in units]
    sibling = [scratch[4 * u + 1] for u in units]
    plane = [scratch[4 * u + 2] for u in units]
    line = [scratch[4 * u + 3] for u in units]
    chips = (place.i, place.ix, place.iy, place.ixy)
    slots = nearest(z)[::-1]

    def piece(u, i2, z2):
        return region(grads[u], i2, z2, own[u].shape[2:])

    def copy(u, kind, z2, src, dst, to):
        return pltpu.make_async_remote_copy(
            src_ref=src, dst_ref=dst, send_sem=send.at[u, kind, z2], recv_sem=recv.at[u, kind, z2],
            device_id=to, device_id_type=MESH)

    def load(u, k, z2):
        return pltpu.make_async_copy(piece(u, chips[k], z2), own[u].at[z2, k], local.at[u, k, z2])

    def across(u, k, z2):
        other = chips[k] + place.ic - i
        return copy(u, k, z2, piece(u, other, z2), sibling[u].at[z2, k], (place.ic, z))

    def route(u, z2):
        odd = lax.rem(z2 + u, 2)
        first = place.ix + odd * (place.iy - place.ix)
        second = place.iy + odd * (place.ix - place.iy)
        return 1 + odd, 2 - odd, first, second

    def to_second(u, z2, far):
        _, ks, _, second = route(u, z2)
        src = own[u].at[z2, 3] if far else own[u].at[z2, ks]
        return copy(u, 4 if far else 5, z2, src, plane[u].at[z2, 0 if far else 1], (second, z))

    def to_first(u, z2):
        kf, _, first, _ = route(u, z2)
        return copy(u, 6, z2, own[u].at[z2, kf], plane[u].at[z2, 2], (first, z))

    def along(u, z2):
        return pltpu.make_async_remote_copy(
            src_ref=own[u].at[z2, 0], dst_ref=line[u].at[z], send_sem=send.at[u, 7, z2],
            recv_sem=recv.at[u, 7, z], device_id=(i, z2), device_id_type=MESH)

    def arrival(u, z2):
        return pltpu.make_async_remote_copy(
            src_ref=own[u].at[z, 0], dst_ref=line[u].at[z2], send_sem=send.at[u, 7, z],
            recv_sem=recv.at[u, 7, z2], device_id=(i, z), device_id_type=MESH)

    def begin(z2):
        for u in units:
            for k in (3, 2, 1, 0):
                load(u, k, z2).start()
                across(u, k, z2).start()

    def stage1(z2):
        for u in units:
            for k in (3, 2, 1, 0):
                load(u, k, z2).wait()
                across(u, k, z2).wait_recv()
                add_into(own[u].at[z2, k], sibling[u].at[z2, k])
                if k == 3:
                    to_second(u, z2, True).start()
            to_second(u, z2, False).start()

    def stage2(z2):
        for u in units:
            kf = route(u, z2)[0]
            to_second(u, z2, True).wait_recv()
            add_into(own[u].at[z2, kf], plane[u].at[z2, 0])
            to_first(u, z2).start()

    def stage3(z2):
        for u in units:
            mine = own[u].at[z2, 0]
            to_second(u, z2, False).wait_recv()
            to_first(u, z2).wait_recv()
            add_into(mine, plane[u].at[z2, 1], plane[u].at[z2, 2])
            if z2 is not z:
                along(u, z2).start()

    def collect(z2):
        for u in units:
            if z2 is z:
                outs[u][...] = own[u][z, 0].astype(F32)
            else:
                arrival(u, z2).wait_recv()
                add_into(outs[u], line[u].at[z2])

    def finish(z2):
        for u in units:
            for k in range(4):
                across(u, k, z2).wait_send()
            to_second(u, z2, True).wait_send()
            to_second(u, z2, False).wait_send()
            to_first(u, z2).wait_send()
            if z2 is not z:
                along(u, z2).wait_send()

    steps = staggered(slots, (stage1, stage2, stage3))
    head = [functools.partial(begin, z2) for z2 in slots]
    last = [functools.partial(collect, z2) for z2 in nearest(z)]
    return head, steps, last + [functools.partial(finish, z2) for z2 in slots]


def shard_of(grad, dp, mp):
    if len(grad.shape) == 4:
        return grad.shape[2:]
    return (grad.shape[0] // mp, grad.shape[1] // dp)


def line_steps(place, rows, outs, send, recv, local):
    mp, i, z = place.mp, place.i, place.z

    def spot(u, z2):
        parts = outs[u].shape[2]
        return outs[u].at[lax.div(z2, parts), :, lax.rem(z2, parts)]

    def copy(u, up, z2, to, src=None):
        here = spot(u, z2)
        kind = 0 if up else 1
        return pltpu.make_async_remote_copy(
            src_ref=here if src is None else src, dst_ref=here, send_sem=send.at[u, kind, z2],
            recv_sem=recv.at[u, kind, z2], device_id=(i, to), device_id_type=MESH)

    def keep(u):
        return pltpu.make_async_copy(rows[u], spot(u, z), local.at[u])

    def move(z2):
        for u in range(len(rows)):
            src = None
            if z2 is z:
                src = rows[u]
                keep(u).start()
            else:
                pl.when(z2 < z)(lambda: copy(u, True, z2, z).wait_recv())
                pl.when(z2 > z)(lambda: copy(u, False, z2, z).wait_recv())
            onward(place, z2, lambda up: copy(u, up, z2, z + 1 if up else z - 1, src).start())

    def finish(z2):
        for u in range(len(rows)):
            if z2 is z:
                keep(u).wait()
            onward(place, z2, lambda up: copy(u, up, z2, z).wait_send())

    slots = nearest(z)
    steps = [functools.partial(move, z2) for z2 in slots]
    return steps[:1], steps[1:], [functools.partial(finish, z2) for z2 in slots]


def woven(lists):
    placed = [(place, k, n) for k, (_, places) in enumerate(lists) for n, place in enumerate(places)]
    return [lists[k][0][n] for _, k, n in sorted(placed)]


class Transfers:
    swap = None

    def __init__(self, dp, mp, cid, shards=(), kinds=(), grads=(), rows=(), spread=()):
        self.dp, self.mp, self.cid = dp, mp, cid
        self.shards, self.kinds, self.grads = list(shards), list(kinds), list(grads)
        self.rows = list(rows)
        self.args = self.shards + self.grads + self.rows
        spots = [(shard_of(g, dp, mp), g.dtype) for g in self.grads]
        self.outs = [gather_shape(s, k, dp, mp) for s, k in zip(shards, kinds)]
        self.outs += [jax.ShapeDtypeStruct(s, F32) for s, _ in spots]
        any_space = pl.BlockSpec(memory_space=pl.ANY)
        self.in_specs = [any_space] * len(self.args)
        self.out_specs = [any_space] * len(self.shards)
        self.out_specs += [pl.BlockSpec(s, lambda *_: (0, 0)) for s, _ in spots]
        self.outs += [jax.ShapeDtypeStruct(dims, r.dtype) for r, dims in zip(self.rows, spread)]
        self.out_specs += [any_space] * len(self.rows)
        self.scratch = []
        if self.rows:
            sems = pltpu.SemaphoreType.DMA((len(self.rows), 2, mp))
            self.scratch += [sems, sems, pltpu.SemaphoreType.DMA((len(self.rows),))]
        if self.shards:
            sems = pltpu.SemaphoreType.DMA((len(self.shards), 9, mp))
            self.scratch += [sems, sems, pltpu.SemaphoreType.DMA((len(self.shards),))]
        if self.grads:
            self.scratch += scatter_scratch(spots, mp)

    def steps(self, ins, outs, scratch):
        place = Place(self.mp)
        first, lists, last = [functools.partial(enter, place)], [], []

        def take(head, steps, ends, slow=False):
            first.extend(head)
            paces = [0.45 * (n + 1) if slow else n / len(steps) for n in range(len(steps))]
            lists.append((steps, paces))
            last.extend(ends)

        count, more = len(self.shards), len(self.shards) + len(self.grads)
        if self.rows:
            take(*line_steps(place, ins[more:], outs[more:], *scratch[:3]), slow=True)
            scratch = scratch[3:]
        if count:
            take(*gather_steps(place, ins[:count], outs[:count], *scratch[:3]))
            scratch = scratch[3:]
        if self.grads:
            take(*scatter_steps(place, ins[count:more], outs[count:more], scratch))
        return first, woven(lists), last

    def params(self, limit):
        return pltpu.CompilerParams(
            collective_id=self.cid, has_side_effects=True, vmem_limit_bytes=limit
        )

    def run(self, name):
        count = len(self.args)

        def kernel(*refs):
            outs = refs[count : count + len(self.outs)]
            first, steps, last = self.steps(refs[:count], outs, refs[count + len(self.outs) :])
            for step in first + steps + last:
                step()

        return pl.pallas_call(
            kernel, grid=(1,), out_shape=self.outs, in_specs=self.in_specs, out_specs=self.out_specs,
            scratch_shapes=self.scratch, compiler_params=self.params(60 << 20), name=name,
        )(*self.args)


class Pace:
    def __init__(self, found, each):
        self.first, self.steps, self.last = found
        self.group, self.groups, self.each, self.at = pl.program_id(0), pl.num_programs(0), each, 0

    def place(self):
        total = self.groups * self.each

        def begin():
            for step in self.first:
                step()

        if self.at == 0 and self.first:
            pl.when(self.group == 0)(begin)
        for n, step in enumerate(self.steps):
            group, at = divmod((n + 1) * total // (len(self.steps) + 1), self.each)
            if at == self.at:
                pl.when(self.group == group)(step)
        self.at += 1

    def end(self):
        @pl.when(self.group == self.groups - 1)
        def _():
            for step in self.last:
                step()


def skew(row, height):
    wide = jnp.broadcast_to(row, (height, row.shape[1]))
    return pltpu.roll(wide, 0, axis=1, stride=1, stride_axis=0)


def widened(tile):
    zero = jnp.zeros((tile.shape[0], HEAD_DIM), tile.dtype)
    found = []
    for h in range(4):
        piece = tile[:, HEAD_DIM * h : HEAD_DIM * (h + 1)]
        found.append(jnp.concatenate([piece, zero] if h < 2 else [zero, piece], axis=1))
    return jnp.concatenate(found, axis=0)


def narrowed(wide):
    n = wide.shape[1] // 4
    found = []
    for h in range(4):
        base = HEAD_DIM * (h // 2)
        found.append(wide[base : base + HEAD_DIM, n * h : n * (h + 1)])
    return jnp.concatenate(found, axis=0).T


def four(row):
    return jnp.concatenate([row] * 4, axis=1)


class Tiles:
    def __init__(self, rows, length, parts):
        self.rows, self.parts, self.blk = rows, parts, 64 // parts
        self.list = [(at, min(TILE_Q, rows - at)) for at in range(0, rows, TILE_Q)]
        self.span = TILE_Q * parts // TILE_K
        self.reach = round_up(length, TILE_K)
        self.strips = len(self.list) * self.span
        self.lead = self.span * TILE_K
        self.width = self.lead + self.strips * TILE_K

    def keys(self, a):
        return min((a + 1) * self.span, self.reach // TILE_K)

    def strip(self, a, m):
        return (a + 1) * self.span - 1 - m

    def windows(self, n):
        runs = [(s * self.blk, 64 * s) for s in range(n // self.blk)]
        return [(e, self.lead + (e + 1 - self.span) * TILE_K, runs) for e in range(self.strips)]


def build_strips(tiles, vec_ref, strip, tail):
    for h in range(4):
        moved = skew(vec_ref[0, h : h + 1, :], TILE_K)
        for ref in (strip, tail):
            n = ref.shape[2] // 4
            for e, at, runs in tiles.windows(n):
                cut = [moved[:, at + far : at + far + tiles.blk] for _, far in runs]
                ref[e, :, n * h : n * (h + 1)] = jnp.concatenate(cut, axis=1)


def split_refs(refs, host, ins, outs):
    if host is None:
        return list(refs), ([], [], [])
    a, b = len(host.args), len(host.outs)
    cut = [0, ins, ins + a, ins + a + outs, ins + a + outs + b, len(refs) - len(host.scratch), len(refs)]
    part = [list(refs[i:j]) for i, j in zip(cut, cut[1:])]
    return part[0] + part[2] + part[4], host.steps(part[1], part[3], part[5])


def tile_valid(biased, mask, keys_ref, m):
    if biased:
        index = lax.broadcasted_iota(jnp.int32, (TILE_K, mask.shape[1]), 0)
        return index >= mask - m * TILE_K
    keys = keys_ref[pl.ds(m * TILE_K, TILE_K), :]
    reps = -(-mask.shape[1] // keys.shape[1])
    return jnp.concatenate([keys] * reps, axis=1)[:, : mask.shape[1]] == mask


def forward_kernel(biased, tiles, host, *refs):
    refs, steps = split_refs(refs, host, 5, 2)
    if biased:
        q_ref, k_ref, v_ref, mask_ref, vec_ref, o_ref, lse_ref, vt, s_s, strip, tail = refs
        keys_ref = None
        build_strips(tiles, vec_ref, strip, tail)
    else:
        q_ref, k_ref, v_ref, mask_ref, keys_ref, o_ref, lse_ref, vt, s_s = refs
    vt[...] = v_ref[...].T
    counts = [tiles.keys(a) if biased else k_ref.shape[0] // TILE_K for a in range(len(tiles.list))]
    pace = Pace(steps, 2 * sum(counts))
    for a, (at, n) in enumerate(tiles.list):
        lanes = 4 * n
        q4 = widened(q_ref[at : at + n, :])
        mask = mask_ref[a : a + 1, :lanes]
        count = counts[a]
        top = None
        for m in range(count):
            pace.place()
            some = slice(m * TILE_K, (m + 1) * TILE_K)
            s = mm_nt(k_ref[some, :], q4)
            if biased:
                s = s + (strip if n == TILE_Q else tail)[tiles.strip(a, m)]
            s = jnp.where(tile_valid(biased, mask, keys_ref, m), s, NEGATIVE)
            s_s[some, :lanes] = s
            here = jnp.max(s, axis=0, keepdims=True)
            top = here if top is None else jnp.maximum(top, here)
        total = jnp.zeros((1, lanes), F32)
        acc = jnp.zeros((2 * HEAD_DIM, lanes), F32)
        for m in range(count):
            pace.place()
            some = slice(m * TILE_K, (m + 1) * TILE_K)
            p = jnp.exp(s_s[some, :lanes] - top)
            total = total + jnp.sum(p, axis=0, keepdims=True)
            acc = acc + mm(vt[:, some], p.astype(BF16))
        o_ref[at : at + n, :] = narrowed(acc / total).astype(BF16)
        lse_ref[0, a : a + 1, :lanes] = top + jnp.log(total)
    pace.end()


class Exchange:
    def __init__(self, groups, blk, steps):
        self.groups, self.blk, self.steps = groups, blk, steps
        self.rows = groups * blk
        block = (steps, 2, groups, blk, 2 * HEAD_DIM)
        self.scratch = [pltpu.VMEM(block, BF16), pltpu.VMEM(block, BF16), pltpu.VMEM(block, F32)]
        sems = pltpu.SemaphoreType.DMA((steps,))
        self.scratch += [sems, sems]

    def copy(self, place, refs, n):
        gone, come, _, send, recv = refs
        mate = place.z + 1 - 2 * lax.rem(place.z, 2)
        return pltpu.make_async_remote_copy(
            src_ref=gone.at[n], dst_ref=come.at[n], send_sem=send.at[n], recv_sem=recv.at[n],
            device_id=(place.i, mate), device_id_type=MESH)

    def part_of(self, ref, part):
        base = pl.multiple_of(part * self.blk, self.blk)
        if self.groups == 1:
            return ref[pl.ds(base, self.blk), :][None]
        view = ref.reshape(ref.shape[0] // (2 * self.blk), 2 * self.blk, ref.shape[1])
        return view[0 : self.groups, pl.ds(base, self.blk), :]

    def give(self, place, refs, sums):
        n = pl.program_id(0)
        gone, _, kept, _, _ = refs
        part = lax.rem(place.z, 2)
        for which, ref in enumerate(sums):
            gone[n, which] = self.part_of(ref, 1 - part).astype(BF16)
            kept[n, which] = self.part_of(ref, part)
        self.copy(place, refs, n).start()

    def take(self, place, refs, out):
        _, come, kept, _, _ = refs
        cols = 2 * HEAD_DIM
        for n in range(self.steps):
            self.copy(place, refs, n).wait()
            for which in range(2):
                total = kept[n, which] + come[n, which].astype(F32)
                at = (which * self.steps + n) * cols
                out[:, at : at + cols] = total.reshape(self.rows, cols).astype(BF16)


def backward_kernel(biased, tiles, host, *refs):
    swap = None if host is None else host.swap
    refs, steps = split_refs(refs, host, 8, (4 if biased else 3) - (swap is not None))
    if swap is not None:
        swap_refs = refs[-len(swap.scratch) :]
        first = 10 + biased
        refs = refs[:first] + [None] + refs[first : -len(swap.scratch)]
    if biased:
        (
            q_ref, k_ref, v_ref, o_ref, do_ref, lse_ref, mask_ref, vec_ref,
            dq_ref, dist_ref, dv_ref, dk_ref, kt, dk_s, dv_s, strip, tail, slope, slope_tail, line,
        ) = refs
        keys_ref = None
        build_strips(tiles, vec_ref, strip, tail)
        slope[...] = jnp.zeros_like(slope)
        slope_tail[...] = jnp.zeros_like(slope_tail)
    else:
        (
            q_ref, k_ref, v_ref, o_ref, do_ref, lse_ref, mask_ref, keys_ref,
            dq_ref, dv_ref, dk_ref, kt, dk_s, dv_s,
        ) = refs
    kt[...] = k_ref[...].T
    dk_s[...] = jnp.zeros_like(dk_s)
    dv_s[...] = jnp.zeros_like(dv_s)
    counts = [tiles.keys(a) if biased else k_ref.shape[0] // TILE_K for a in range(len(tiles.list))]
    pace = Pace(steps, sum(counts))
    for a, (at, n) in enumerate(tiles.list):
        lanes = 4 * n
        q4 = widened(q_ref[at : at + n, :])
        do4 = widened(do_ref[at : at + n, :])
        mask = mask_ref[a : a + 1, :lanes]
        lse = lse_ref[0, a : a + 1, :lanes]
        both = widened(o_ref[at : at + n, :]).astype(F32) * do4.astype(F32)
        delta = jnp.sum(both.T, axis=0, keepdims=True)
        dq = jnp.zeros((2 * HEAD_DIM, lanes), F32)
        for m in range(counts[a]):
            pace.place()
            some = slice(m * TILE_K, (m + 1) * TILE_K)
            s = mm_nt(k_ref[some, :], q4)
            if biased:
                e = tiles.strip(a, m)
                s = s + (strip if n == TILE_Q else tail)[e]
            p = jnp.exp(jnp.where(tile_valid(biased, mask, keys_ref, m), s - lse, NEGATIVE))
            ds = p * (mm_nt(v_ref[some, :], do4) - delta)
            low = ds.astype(BF16)
            if biased:
                ref = slope if n == TILE_Q else slope_tail
                ref[e] += ds
            dv_s[some, :] += mm(p.astype(BF16), do4)
            dk_s[some, :] += mm(low, q4)
            dq = dq + mm(kt[:, some], low)
        dq_ref[at : at + n, :] = narrowed(dq).astype(BF16)

    if swap is None:
        dk_ref[...] = dk_s[...].astype(BF16)
        dv_ref[...] = dv_s[...].astype(BF16)
    else:
        place = Place(host.mp)
        swap.give(place, swap_refs, (dk_s, dv_s))
    if biased:
        width = tiles.width
        for h in range(4):
            line[...] = jnp.zeros_like(line)
            for ref in (slope, slope_tail):
                n = ref.shape[2] // 4
                for e, at, runs in tiles.windows(n):
                    for near, far in runs:
                        piece = ref[e, :, n * h + near : n * h + near + tiles.blk]
                        line[:, at + far : at + far + tiles.blk] += piece
            part = line[...]
            height = TILE_K
            while height > 8:
                height //= 2
                part = part[:height] + pltpu.roll(part[height:], width - height, axis=1)
            row = part[0:1]
            for j in range(1, 8):
                row = row + pltpu.roll(part, width - j, axis=1)[j : j + 1]
            dist_ref[0, h : h + 1, :] = row
    pace.end()
    if swap is not None:
        pl.when(pace.group == pace.groups - 1)(lambda: swap.take(place, swap_refs, dv_ref))


def spec(shape, index):
    return pl.BlockSpec(shape, index)


def attention_call(kernel, biased, tiles, outs, scratch, args, name, flops, host):
    steps = args[1].shape[1] // (2 * HEAD_DIM)

    def column(array, lanes):
        return spec((array.shape[0], lanes), lambda i: (0, i))

    def placed(array, kind):
        if kind == "wide":
            return column(array, 4 * HEAD_DIM)
        if kind == "key":
            return column(array, 2 * HEAD_DIM)
        if kind == "head":
            return spec((1,) + array.shape[1:], lambda i: (i, 0, 0))
        return spec(array.shape, lambda i: (0, 0))

    kinds = ["wide", "key", "key"]
    if kernel is backward_kernel:
        kinds += ["wide", "wide", "head"]
    kinds += ["flat", "head" if biased else "flat"]
    specs = [placed(array, kind) for array, kind in zip(args, kinds)]
    shapes = [item for item, _ in outs]
    out_specs = [placed(item, kind) for item, kind in outs]
    own = len(shapes)
    params = pltpu.CompilerParams(vmem_limit_bytes=60 << 20)
    args = list(args)
    if host is not None:
        args += host.args
        specs += host.in_specs
        shapes += host.outs
        out_specs += host.out_specs
        scratch = scratch + host.scratch
        params = host.params(62 << 20)
    found = pl.pallas_call(
        functools.partial(kernel, biased, tiles, host),
        grid=(steps,),
        out_shape=shapes,
        in_specs=specs,
        out_specs=out_specs,
        scratch_shapes=scratch,
        compiler_params=params,
        cost_estimate=pl.CostEstimate(flops=flops, bytes_accessed=16 << 20, transcendentals=0),
        name=name,
    )(*args)
    return found[:own], found[own:]


def strip_scratch(tiles):
    last = tiles.list[-1][1]
    return [
        pltpu.VMEM((tiles.strips, TILE_K, 4 * TILE_Q), F32),
        pltpu.VMEM((tiles.strips, TILE_K, 4 * last), F32),
    ]


def attend_forward(q, k, v, mask, extra, tiles, biased, name, host=None):
    steps = k.shape[1] // (2 * HEAD_DIM)
    outs = [
        (jax.ShapeDtypeStruct(q.shape, BF16), "wide"),
        (jax.ShapeDtypeStruct((steps,) + mask.shape, F32), "head"),
    ]
    scratch = [pltpu.VMEM((2 * HEAD_DIM, k.shape[0]), BF16), pltpu.VMEM((k.shape[0], 4 * TILE_Q), F32)]
    if biased:
        scratch += strip_scratch(tiles)
    flops = 4 * q.shape[0] * k.shape[0] * q.shape[1]
    return attention_call(
        forward_kernel, biased, tiles, outs, scratch, (q, k, v, mask, extra), name, flops, host
    )


def attend_backward(q, k, v, o, do, lse, mask, extra, tiles, biased, name, host=None):
    keys, cols = k.shape
    grad = jax.ShapeDtypeStruct(k.shape, BF16)
    outs = [(jax.ShapeDtypeStruct(q.shape, BF16), "wide")]
    scratch = [
        pltpu.VMEM((2 * HEAD_DIM, keys), BF16),
        pltpu.VMEM((keys, 2 * HEAD_DIM), F32),
        pltpu.VMEM((keys, 2 * HEAD_DIM), F32),
    ]
    if biased:
        outs.append((jax.ShapeDtypeStruct(extra.shape, F32), "head"))
        scratch += strip_scratch(tiles) * 2 + [pltpu.VMEM((TILE_K, tiles.width), F32)]
    if host is None:
        outs += [(grad, "key"), (grad, "key")]
    else:
        outs.append((jax.ShapeDtypeStruct((host.swap.rows, 2 * cols), BF16), "flat"))
        scratch += host.swap.scratch
    flops = 10 * q.shape[0] * keys * q.shape[1]
    return attention_call(
        backward_kernel, biased, tiles, outs, scratch, (q, k, v, o, do, lse, mask, extra), name,
        flops, host,
    )


def inverse_rms(state):
    return lax.rsqrt(jnp.mean(state * state, axis=-1, keepdims=True) + EPSILON)


def norm_back(state, gain, grad_normed):
    scale = inverse_rms(state)
    weighted = grad_normed * gain
    grad_gain = jnp.sum(grad_normed * state * scale, axis=0, keepdims=True)
    inner = jnp.mean(weighted * state, axis=-1, keepdims=True)
    return scale * weighted - state * (scale * scale * scale) * inner, grad_gain


def row_chunk(rows):
    for size in (544, 272, 256, 128):
        if rows % size == 0:
            return size
    return rows


def full(array):
    return pl.BlockSpec(array.shape, lambda j, w: (0,) * len(array.shape))


def lead_block(array):
    return pl.BlockSpec((1,) + array.shape[1:], lambda j, w: (j,) + (0,) * (len(array.shape) - 1))


def col_block(array, parts):
    return pl.BlockSpec((array.shape[0], array.shape[1] // parts), lambda j, w: (0, j))


def row_block(array, parts):
    return pl.BlockSpec((array.shape[0] // parts, array.shape[1]), lambda j, w: (j, 0))


def kernel_call(body, name, steps, where, ins, outs, scratch, flops):
    return pl.pallas_call(
        lambda _, *refs: body(*refs),
        out_shape=[jax.ShapeDtypeStruct(a.shape, a.dtype) for a, _ in outs],
        grid_spec=pltpu.PrefetchScalarGridSpec(
            num_scalar_prefetch=1,
            grid=(steps,),
            in_specs=[s for _, s in ins],
            out_specs=[s for _, s in outs],
            scratch_shapes=scratch,
        ),
        compiler_params=pltpu.CompilerParams(vmem_limit_bytes=60 << 20),
        cost_estimate=pl.CostEstimate(flops=flops, bytes_accessed=16 << 20, transcendentals=0),
        name=name,
    )(where, *[a for a, _ in ins])


def my_rows(array):
    block = (None, array.shape[1], None) + array.shape[3:]
    return array, pl.BlockSpec(block, lambda j, w: (w[0], 0, w[1], 0, 0))


def my_sequence(array):
    return array, pl.BlockSpec((None,) + array.shape[1:], lambda j, w: (w[0], 0, 0))


def flat(ref):
    return ref.reshape(ref.shape[0] * ref.shape[1], ref.shape[2])


def shape(dims, dtype=BF16):
    return jax.ShapeDtypeStruct(dims, dtype)


def project_kernel(x_ref, own_ref, gain_ref, w_ref, q_ref, k_ref, v_ref, n_ref, normed):
    length = x_ref.shape[0]
    qcols = q_ref.shape[1]
    kcols = k_ref.shape[1]
    size = row_chunk(length)

    @pl.when(pl.program_id(0) == 0)
    def _():
        def norm_rows(at):
            x = x_ref[pl.ds(at, size), :].astype(F32)
            normed[pl.ds(at, size), :] = (x * inverse_rms(x) * gain_ref[...]).astype(BF16)

        chunked(length, size, norm_rows)
        x = flat(own_ref)[...].astype(F32)
        n_ref[...] = (x * inverse_rms(x) * gain_ref[...]).astype(BF16)

    q_ref[...] = mm(n_ref[...], w_ref[0, :, :qcols]).astype(BF16)

    def keys(at):
        kv = mm(normed[pl.ds(at, size), :], w_ref[0, :, qcols:]).astype(BF16)
        k_ref[pl.ds(at, size), :] = kv[:, :kcols]
        v_ref[pl.ds(at, size), :] = kv[:, kcols:]

    chunked(length, size, keys)
    k_ref[length:, :] = jnp.zeros((k_ref.shape[0] - length, kcols), BF16)
    v_ref[length:, :] = jnp.zeros((k_ref.shape[0] - length, kcols), BF16)


def self_project(where, x, own, gain, w, reach, rows):
    _, length, width = x.shape
    groups, _, cols = w.shape
    q, k = shape((rows, groups * cols // 2)), shape((reach, groups * cols // 4))
    n = shape((rows, width))
    return kernel_call(
        project_kernel, "self_project", groups, where,
        [my_sequence(x), my_rows(own), (gain, full(gain)), (w, lead_block(w))],
        [(q, col_block(q, groups)), (k, col_block(k, groups)), (k, col_block(k, groups)), (n, full(n))],
        [pltpu.VMEM((length, width), BF16)], (length + rows) * width * groups * cols,
    )


def middle_kernel(o_ref, wo_ref, x_ref, gain_ref, m_ref, w_ref, h_ref, n_ref, q_ref, k_ref, v_ref):
    rows, qcols = q_ref.shape
    kcols = k_ref.shape[1]
    size = row_chunk(rows)
    x_ref = flat(x_ref)

    @pl.when(pl.program_id(0) == 0)
    def _():
        def state(at):
            some = pl.ds(at, size)
            h = x_ref[some, :].astype(F32) + mm(o_ref[some, :], wo_ref[...])
            h_ref[some, :] = h
            n_ref[some, :] = (h * inverse_rms(h) * gain_ref[...]).astype(BF16)

        chunked(rows, size, state)

    q_ref[...] = mm(n_ref[...], w_ref[0, :, :qcols]).astype(BF16)
    kv = mm(m_ref[...], w_ref[0, :, qcols:]).astype(BF16)
    k_ref[...] = kv[:, :kcols]
    v_ref[...] = kv[:, kcols:]


def cross_project(where, o, wo, own, gain, memory, w):
    rows, width = o.shape
    groups, _, cols = w.shape
    h, n = shape((rows, width), F32), shape((rows, width))
    q = shape(o.shape)
    k = shape((memory.shape[1], groups * cols // 4))
    return kernel_call(
        middle_kernel, "cross_project", groups, where,
        [(o, full(o)), (wo, full(wo)), my_rows(own), (gain, full(gain)), my_sequence(memory),
         (w, lead_block(w))],
        [(h, full(h)), (n, full(n)), (q, col_block(q, groups)), (k, col_block(k, groups)),
         (k, col_block(k, groups))],
        [], 6 * rows * width * width,
    )


def gate_parts(value):
    square = value * value
    inner = jnp.tanh(0.7978845608028654 * (value + 0.044715 * square * value))
    half = 0.5 * (1.0 + inner)
    slope = 0.7978845608028654 * (1.0 + 3.0 * 0.044715 * square)
    return value * half, half + 0.5 * value * (1.0 - inner * inner) * slope


def feed_kernel(
    o_ref, wo_ref, h1_ref, gain_ref, up_ref, wa_ref, wb_ref, wd_ref,
    out_ref, g2_ref, gain_out, gwa_ref, gwb_ref, gwd_ref, do_ref, gwo_ref,
    h2, normed, total, back, hidden_s, grad_s,
):
    rows, width = h1_ref.shape
    j = pl.program_id(0)
    size = row_chunk(rows)
    up_ref = flat(up_ref)
    cols = wd_ref.shape[0]
    cut = wa_ref.shape[2]

    @pl.when(j == 0)
    def _():
        def state(at):
            some = pl.ds(at, size)
            h = h1_ref[some, :] + mm(o_ref[some, :], wo_ref[...])
            h2[some, :] = h
            normed[some, :] = (h * inverse_rms(h) * gain_ref[...]).astype(BF16)
            total[some, :] = h
            back[some, :] = jnp.zeros((size, width), F32)

        chunked(rows, size, state)

    def hidden_rows(at):
        some = pl.ds(at, size)
        n = normed[some, :]
        g = up_ref[some, :]
        both = jnp.concatenate([mm(n, wa_ref[0]), mm(n, wb_ref[0])], axis=1)
        gate, up = both[:, :cols], both[:, cols:]
        grad_hidden = mm_nt(g, wd_ref[...])
        active, pull = gate_parts(gate)
        hidden = (active * up).astype(BF16)
        grad_gate = (grad_hidden * up * pull).astype(BF16)
        grad_up = (grad_hidden * active).astype(BF16)
        hidden_s[some, :] = hidden
        grads = jnp.concatenate([grad_gate, grad_up], axis=1)
        grad_s[some, :] = grads
        total[some, :] += mm(hidden, wd_ref[...])
        back[some, :] += mm_nt(grads[:, :cut], wa_ref[0]) + mm_nt(grads[:, cut:], wb_ref[0])

    chunked(rows, size, hidden_rows)

    def weight_rows(at):
        some = pl.ds(at, 512)
        n = normed[:, some]
        gw = mm_tn(n, grad_s[...]).astype(BF16)
        gwa_ref[0, some, :] = gw[:, :cut]
        gwb_ref[0, some, :] = gw[:, cut:]
        gwd_ref[:, some] = mm_tn(hidden_s[...], up_ref[:, some]).astype(BF16)

    chunked(width, 512, weight_rows)

    @pl.when(j == pl.num_programs(0) - 1)
    def _():
        gain_out[...] = jnp.zeros_like(gain_out)
        do_ref[...] = jnp.zeros_like(do_ref)

        def finish(at):
            some = pl.ds(at, size)
            out_ref[some, :] = total[some, :].astype(BF16)
            change, grad_gain = norm_back(h2[some, :], gain_ref[...], back[some, :])
            gain_out[...] += grad_gain
            g2 = up_ref[some, :].astype(F32) + change
            g2_ref[some, :] = g2
            low = g2.astype(BF16)
            normed[some, :] = low
            do_ref[some, :] = mm_nt(low, wo_ref[...]).astype(BF16)

        chunked(rows, size, finish)

        def out_rows(at):
            some = pl.ds(at, 512)
            gwo_ref[some, :] = mm_tn(o_ref[0:rows, some], normed[...]).astype(BF16)

        chunked(width, 512, out_rows)


def feed(where, o, wo, h1, gain, upstream, wa, wb, wd):
    rows, width = h1.shape
    groups = wa.shape[0]
    cols = wa.shape[2] + wb.shape[2]
    out, g2, gg = shape(h1.shape), shape(h1.shape, F32), shape((1, width), F32)
    return kernel_call(
        feed_kernel, "feed", groups, where,
        [(o, full(o)), (wo, full(wo)), (h1, full(h1)), (gain, full(gain)), my_rows(upstream),
         (wa, lead_block(wa)), (wb, lead_block(wb)), (wd, row_block(wd, groups))],
        [(out, full(out)), (g2, full(g2)), (gg, full(gg)), (wa, lead_block(wa)), (wb, lead_block(wb)),
         (wd, row_block(wd, groups)), (o, full(o)), (wo, full(wo))],
        [pltpu.VMEM((rows, width), F32), pltpu.VMEM((rows, width), BF16), pltpu.VMEM((rows, width), F32),
         pltpu.VMEM((rows, width), F32)] + [pltpu.VMEM((rows, cols // 2), BF16), pltpu.VMEM((rows, cols), BF16)],
        9 * rows * width * groups * cols,
    )


def back_kernel(
    dq_ref, w_ref, n_ref, h_ref, gain_ref, g2_ref, wo_ref, o_ref,
    gw_ref, g1_ref, gain_out, do_ref, gwo_ref, back, low_s,
):
    rows, width = h_ref.shape
    qcols = dq_ref.shape[1]
    j = pl.program_id(0)
    size = row_chunk(rows)

    @pl.when(j == 0)
    def _():
        back[...] = jnp.zeros_like(back)

    back[...] += mm_nt(dq_ref[0:rows, :], w_ref[0, :, :qcols])

    def weight_rows(at):
        some = pl.ds(at, 512)
        gw_ref[0, some, :] = mm_tn(n_ref[:, some], dq_ref[0:rows, :]).astype(BF16)

    chunked(width, 512, weight_rows)

    @pl.when(j == pl.num_programs(0) - 1)
    def _():
        gain_out[...] = jnp.zeros_like(gain_out)
        do_ref[...] = jnp.zeros_like(do_ref)

        def finish(at):
            some = pl.ds(at, size)
            change, grad_gain = norm_back(h_ref[some, :], gain_ref[...], back[some, :])
            gain_out[...] += grad_gain
            g1 = g2_ref[some, :] + change
            g1_ref[some, :] = g1
            low = g1.astype(BF16)
            low_s[some, :] = low
            do_ref[some, :] = mm_nt(low, wo_ref[...]).astype(BF16)

        chunked(rows, size, finish)

        def out_rows(at):
            some = pl.ds(at, 512)
            gwo_ref[some, :] = mm_tn(o_ref[0:rows, some], low_s[...]).astype(BF16)

        chunked(width, 512, out_rows)


def cross_back(where, dq, w, n, h, gain, g2, wo, o):
    rows, width = h.shape
    groups, _, cols = w.shape
    gw = shape((groups, width, cols // 2))
    gg = shape((1, width), F32)
    return kernel_call(
        back_kernel, "cross_back", groups, where,
        [(dq, col_block(dq, groups)), (w, lead_block(w)), (n, full(n)), (h, full(h)), (gain, full(gain)),
         (g2, full(g2)), (wo, full(wo)), (o, full(o))],
        [(gw, lead_block(gw)), (g2, full(g2)), (gg, full(gg)), (o, full(o)), (wo, full(wo))],
        [pltpu.VMEM((rows, width), F32), pltpu.VMEM((rows, width), BF16)],
        8 * rows * width * width,
    )


def memory_kernel(dk_ref, dv_ref, w_ref, m_ref, gw_ref, gm_ref, back):
    j = pl.program_id(0)
    qcols = w_ref.shape[2] // 2

    @pl.when(j == 0)
    def _():
        back[...] = jnp.zeros_like(back)

    both = jnp.concatenate([dk_ref[...], dv_ref[...]], axis=1)
    back[...] += mm_nt(both, w_ref[0, :, qcols:])
    gw_ref[0] = mm_tn(m_ref[...], both).astype(BF16)

    @pl.when(j == pl.num_programs(0) - 1)
    def _():
        gm_ref[...] = back[...].astype(BF16)


def key_halves(dkv, groups):
    cols = dkv.shape[1] // (2 * groups)
    return [
        (dkv, pl.BlockSpec((dkv.shape[0], cols), lambda j, w: (0, j))),
        (dkv, pl.BlockSpec((dkv.shape[0], cols), lambda j, w: (0, j + groups))),
    ]


def memory_back(where, dkv, w, memory):
    groups, width, cols = w.shape
    gw, gm = shape((groups, width, cols // 2)), shape((dkv.shape[0], width))
    rows = pl.BlockSpec((None,) + gm.shape, lambda j, w: (w[0], w[1], 0))
    return kernel_call(
        memory_kernel, "memory_back", groups, where,
        key_halves(dkv, groups) + [(w, lead_block(w)), (memory, rows)],
        [(gw, lead_block(gw)), (gm, full(gm))],
        [pltpu.VMEM(gm.shape, F32)], 4 * gm.shape[0] * width * width,
    )


def last_kernel(
    dq_ref, dk_ref, dv_ref, w_ref, n_ref, x_ref, gain_ref, g1_ref,
    gwq_ref, gwkv_ref, gx_ref, gain_out, back,
):
    rows, width = g1_ref.shape
    j = pl.program_id(0)
    size = row_chunk(rows)
    x_ref = flat(x_ref)

    @pl.when(j == 0)
    def _():
        back[...] = jnp.zeros_like(back)

    dq = dq_ref[0:rows, :]
    dkv = jnp.concatenate([dk_ref[...], dv_ref[...]], axis=1)
    both = jnp.concatenate([dq, dkv], axis=1)
    back[...] += mm_nt(both, w_ref[0])

    def weight_rows(at):
        some = pl.ds(at, 512)
        gwq_ref[0, some, :] = mm_tn(n_ref[:, some], dq).astype(BF16)
        gwkv_ref[0, some, :] = mm_tn(n_ref[:, some], dkv).astype(BF16)

    chunked(width, 512, weight_rows)

    @pl.when(j == pl.num_programs(0) - 1)
    def _():
        gain_out[...] = jnp.zeros_like(gain_out)

        def finish(at):
            some = pl.ds(at, size)
            change, grad_gain = norm_back(x_ref[some, :].astype(F32), gain_ref[...], back[some, :])
            gain_out[...] += grad_gain
            gx_ref[some, :] = (g1_ref[some, :] + change).astype(BF16)

        chunked(rows, size, finish)


def self_back(where, dq, dkv, w, n, own, gain, g1):
    rows, width = g1.shape
    groups, _, cols = w.shape
    gw = shape((groups, width, cols // 2))
    gx = shape(g1.shape)
    gg = shape((1, width), F32)
    return kernel_call(
        last_kernel, "self_back", groups, where,
        [(dq, col_block(dq, groups))] + key_halves(dkv, groups)
        + [(w, lead_block(w)), (n, full(n)), my_rows(own), (gain, full(gain)), (g1, full(g1))],
        [(gw, lead_block(gw)), (gw, lead_block(gw)), (gx, full(gx)), (gg, full(gg))],
        [pltpu.VMEM((rows, width), F32)],
        8 * rows * width * width,
    )


def gather(shard, dims):
    for axis, name in dims:
        shard = lax.all_gather(shard, name, axis=axis, tiled=True)
    return shard


ROWS_BY_DP = ((0, "dp"), (1, "mp"))
ROWS_BY_MP = ((1, "dp"), (0, "mp"))


def scatter(grad, dims):
    for axis, name in dims:
        grad = lax.psum_scatter(grad, name, scatter_dimension=axis, tiled=True)
    return grad.astype(F32)


def grouped(weight, groups):
    rows, cols = weight.shape
    return weight.reshape(rows, groups, cols // groups).transpose(1, 0, 2)


def ungrouped(weight):
    groups, rows, cols = weight.shape
    return weight.transpose(1, 0, 2).reshape(rows, groups * cols)


def body(
    inputs,
    encoded,
    decoder_segments,
    encoder_segments,
    buckets,
    self_gain,
    self_query,
    self_key,
    self_value,
    self_out,
    position_bias,
    cross_gain,
    cross_query,
    cross_key,
    cross_value,
    cross_out,
    feed_gain,
    feed_gate,
    feed_up,
    feed_down,
    cotangent,
    *,
    dp,
    mp,
):
    batches, length, width = inputs.shape
    enc_length = encoded.shape[1]
    parts = mp // batches
    rows = length // parts
    tiles = Tiles(rows, length, parts)
    place = lax.axis_index("mp")
    sequence = place // parts
    part = place % parts
    where = jnp.stack([sequence, part]).astype(jnp.int32)
    groups = self_key.shape[1] * mp // (2 * HEAD_DIM)
    native = mp == groups and dp == 8 and parts == 2

    if native:
        order = ["by_dp", "by_mp"]
        size = width // dp
        gains = jnp.stack([self_gain, cross_gain, feed_gain])
        little = jnp.pad(position_bias.reshape(1, -1), ((0, 0), (0, size - position_bias.size)))
        little = jnp.pad(jnp.concatenate([gains, little]), ((0, 12), (0, 0)))
        w1 = jnp.concatenate([self_query, self_key, self_value], axis=1)
        w2 = jnp.concatenate([cross_query, cross_key, cross_value], axis=1)
        w1, little, wo1 = Transfers(
            dp, mp, 1, [w1, little, self_out], ["by_dp"] + order
        ).run("gather_self")
        gains = little[0, :, :3].transpose(1, 0, 2).reshape(3, 1, width).astype(F32)
        table = little[:, :, 3, : position_bias.size].reshape((mp, dp) + position_bias.shape)
        table = table.transpose(1, 2, 0, 3).reshape(dp * position_bias.shape[0], -1).astype(F32)
        w1 = w1.reshape(mp, width, w1.shape[3])
    else:
        gains = [gather(g, ((0, "dp"),)).astype(F32)[None] for g in (self_gain, cross_gain, feed_gain)]
        table = gather(position_bias, ROWS_BY_DP).astype(F32)

        def blocks(*shards):
            return jnp.concatenate([grouped(gather(s, ROWS_BY_DP), groups) for s in shards], axis=2)

        w1 = blocks(self_query, self_key, self_value)
        w2 = blocks(cross_query, cross_key, cross_value)
        w3 = blocks(feed_gate, feed_up)
        wa, wb = w3[:, :, : w3.shape[2] // 2], w3[:, :, w3.shape[2] // 2 :]
        wo1, wo2, wd = (gather(s, ROWS_BY_MP) for s in (self_out, cross_out, feed_down))
    gain_one, gain_two, gain_three = gains

    def cut(array):
        return array.reshape((array.shape[0], length // 64, parts, 64 // parts) + array.shape[2:])

    own_inputs = cut(inputs)
    docs = lax.dynamic_index_in_dim(decoder_segments, sequence, keepdims=False)
    enc_docs = lax.dynamic_index_in_dim(encoder_segments, sequence, keepdims=False)
    own_docs = lax.dynamic_slice_in_dim(docs.reshape(length // 64, 64), part * tiles.blk, tiles.blk, axis=1)
    own_docs = own_docs.reshape(rows)

    kinds = jnp.arange(4, dtype=jnp.int32)
    before = jnp.sum((docs[None, :] < kinds[:, None]).astype(jnp.int32), axis=1)
    is_doc = (own_docs[:, None] == kinds[None, :]).astype(jnp.int32)
    start = jnp.sum(is_doc * before[None, :], axis=1)

    def by_tile(row):
        found = []
        for at, n in tiles.list:
            piece = jnp.tile(row[at : at + n], 4)
            found.append(jnp.pad(piece, (0, 4 * (TILE_Q - n))))
        return jnp.stack(found)

    mask_one = by_tile(start)
    mask_two = by_tile(own_docs)
    keys_two = jnp.broadcast_to(enc_docs[:, None], (enc_length, TILE_Q))
    onehot = (buckets[:, None] == jnp.arange(table.shape[0], dtype=jnp.int32)).astype(F32)
    by_distance = dot(table, onehot, ((0,), (1,)), HIGHEST)
    heads = by_distance.shape[0]
    vec = jnp.pad(by_distance, ((0, 0), (0, tiles.width)))
    vec = jnp.concatenate([jnp.full((heads, tiles.lead), NEGATIVE, F32), vec], axis=1)
    vec = lax.dynamic_slice_in_dim(vec, part * tiles.blk, tiles.width, axis=1)
    vec = vec.reshape(heads // 4, 4, tiles.width)

    q1, k1, v1, n1 = self_project(where, inputs, own_inputs, gain_one, w1, tiles.reach, rows)
    hosts = [None] * 4
    if native:
        w3 = jnp.concatenate([feed_gate, feed_up], axis=1)
        hosts[0] = Transfers(dp, mp, 2, [w2, cross_out, feed_down], order + ["by_mp"])
        middle = round_up(w3.shape[1] // 2, 128)
        hosts[1] = Transfers(dp, mp, 3, [w3[:, :middle], w3[:, middle:]], ["by_dp", "by_dp"])
    (o1, lse_one), found = attend_forward(
        q1, k1, v1, mask_one, vec, tiles, True, "self_forward", hosts[0]
    )
    if native:
        w2, wo2, wd = found
        w2 = w2.reshape(mp, width, w2.shape[3])
    h1, n2, q2, k2, v2 = cross_project(where, o1, wo1, own_inputs, gain_two, encoded, w2)
    (o2, lse_two), found = attend_forward(
        q2, k2, v2, mask_two, keys_two, tiles, False, "cross_forward", hosts[1]
    )
    if native:
        wa, wb = (w.reshape(mp, width, w.shape[3]) for w in found)

    result, grad_two, grad_gain_three, gwa, gwb, gwd, do2, gwo2 = feed(
        where, o2, wo2, h1, gain_three, cut(cotangent), wa, wb, wd
    )

    def collect(array):
        array = lax.all_gather(array, "mp", axis=0, tiled=True)
        array = array.reshape(batches, parts, length // 64, tiles.blk, width)
        return array.transpose(0, 2, 1, 3, 4).reshape(batches, length, width)

    outputs = collect(result)

    def pieces(grad):
        return grad.reshape(grad.shape[0], dp, grad.shape[1] // dp, grad.shape[2])

    sharing = [[s * parts + p for p in range(parts)] for s in range(batches)]

    def share(dk, dv, count):
        both = jnp.concatenate([dk, dv], axis=1)
        both = both.reshape(count, parts, -1, both.shape[1]).transpose(1, 0, 2, 3)
        both = both.reshape(-1, both.shape[3])
        return lax.psum_scatter(
            both, "mp", scatter_dimension=0, axis_index_groups=sharing, tiled=True
        )

    if native:
        hosts[2] = Transfers(dp, mp, 4, grads=[gwd])
        hosts[2].swap = Exchange(1, enc_length // 2, groups)
    (dq2, *dkv2), sums_down = attend_backward(
        q2, k2, v2, o2, do2, lse_two, mask_two, keys_two, tiles, False, "cross_backward", hosts[2]
    )
    dkv2 = dkv2[0] if native else share(dkv2[1], dkv2[0], 1)
    gwq2, grad_one, grad_gain_two, do1, gwo1 = cross_back(
        where, dq2, w2, n2, h1, gain_two, grad_two, wo1, o1
    )
    gwkv2, grad_memory = memory_back(where, dkv2, w2, encoded)

    if native:
        grads = [pieces(gwa), pieces(gwb)]
        hosts[3] = Transfers(dp, mp, 5, grads=grads)
        hosts[3].swap = Exchange(length // 64, tiles.blk, groups)
    (dq1, slopes, *dkv1), sums_feed = attend_backward(
        q1, k1, v1, o1, do1, lse_one, mask_one, vec, tiles, True, "self_backward", hosts[3]
    )
    if native:
        dkv1 = dkv1[0]
    else:
        dkv1 = share(dkv1[1][:length], dkv1[0][:length], length // 64)
    grad_encoded = lax.all_gather(grad_memory, "mp", axis=0, tiled=True).reshape(encoded.shape)
    gwq1, gwkv1, grad_rows, grad_gain_one = self_back(
        where, dq1, dkv1, w1, n1, own_inputs, gain_one, grad_one
    )
    slopes = slopes.reshape(heads, tiles.width)
    slopes = jnp.pad(slopes, ((0, 0), (64, length)))
    slopes = lax.dynamic_slice_in_dim(slopes, 64 + tiles.lead - part * tiles.blk, length, axis=1)
    grad_table = dot(onehot, slopes, ((0,), (1,)), HIGHEST)
    grad_gains = jnp.concatenate([grad_gain_one, grad_gain_two, grad_gain_three])

    kcols = gwkv1.shape[2] // 2
    if native:
        little = grad_gains.reshape(3, dp, size).transpose(1, 0, 2)
        little = jnp.broadcast_to(little[None], (mp, dp, 3, size))
        spots = grad_table.reshape(dp, position_bias.shape[0], mp, position_bias.shape[1])
        spots = spots.transpose(2, 0, 1, 3).reshape(mp, dp, 1, position_bias.size)
        spots = jnp.pad(spots, ((0, 0), (0, 0), (0, 4), (0, size - position_bias.size)))
        little = jnp.concatenate([little, spots], axis=2)
        grads = [pieces(g) for g in (gwq2, gwkv2, gwq1, gwkv1)] + [gwo2, gwo1, little]
        *sums, little, grad_inputs = Transfers(
            dp, mp, 6, grads=grads, rows=[grad_rows.reshape(length // 64, tiles.blk, width)],
            spread=[(batches, length // 64, parts, tiles.blk, width)],
        ).run("scatter_rest")
        grad_inputs = grad_inputs.reshape(inputs.shape)
        sums = sums + list(sums_feed) + list(sums_down)
        gwq2, gwkv2, gwq1, gwkv1, gwo2, gwo1, gwa, gwb, gwd = sums
        gw3 = jnp.concatenate([gwa, gwb], axis=1)
        half = gw3.shape[1] // 2
        gwg, gwu = gw3[:, :half], gw3[:, half:]
        gwk2, gwv2, gwk1, gwv1 = (
            g[:, at : at + kcols] for g in (gwkv2, gwkv1) for at in (0, kcols)
        )
        grad_gains = [little[n] for n in range(3)]
        grad_table = little[3, : position_bias.size].reshape(position_bias.shape)
    else:
        grad_inputs = collect(grad_rows)

        def summed(grad):
            return scatter(ungrouped(grad), ROWS_BY_DP)

        gwk1, gwv1 = summed(gwkv1[:, :, :kcols]), summed(gwkv1[:, :, kcols:])
        gwk2, gwv2 = summed(gwkv2[:, :, :kcols]), summed(gwkv2[:, :, kcols:])
        gwg, gwu = summed(gwa), summed(gwb)
        gwq1, gwq2 = summed(gwq1), summed(gwq2)
        gwo1, gwo2, gwd = (scatter(g, ROWS_BY_MP) for g in (gwo1, gwo2, gwd))
        small = jnp.concatenate([grad_gains.reshape(-1), grad_table.reshape(-1)])
        small = lax.psum(small, ("dp", "mp"))
        data = lax.axis_index("dp")
        grad_gains = lax.dynamic_slice_in_dim(
            small[: 3 * width].reshape(3, dp, width // dp), data, 1, axis=1
        )
        grad_gains = [grad_gains[n, 0] for n in range(3)]
        grad_table = lax.dynamic_slice(
            small[3 * width :].reshape(table.shape),
            (data * position_bias.shape[0], place * position_bias.shape[1]),
            position_bias.shape,
        )

    return (
        outputs, grad_inputs, grad_encoded,
        grad_gains[0], gwq1, gwk1, gwv1, gwo1, grad_table,
        grad_gains[1], gwq2, gwk2, gwv2, gwo2,
        grad_gains[2], gwg, gwu, gwd,
    )


def solution(mesh):
    rows3 = P("dp", None, None)
    by_dp = P("dp", "mp")
    by_mp = P("mp", "dp")
    gain = P("dp")
    return jax.shard_map(
        functools.partial(body, dp=mesh.shape["dp"], mp=mesh.shape["mp"]),
        mesh=mesh,
        in_specs=(
            rows3, rows3, P("dp", None), P("dp", None), P(),
            gain, by_dp, by_dp, by_dp, by_mp, by_dp,
            gain, by_dp, by_dp, by_dp, by_mp,
            gain, by_dp, by_dp, by_mp, rows3,
        ),
        out_specs=(
            rows3, rows3, rows3,
            gain, by_dp, by_dp, by_dp, by_mp, by_dp,
            gain, by_dp, by_dp, by_dp, by_mp,
            gain, by_dp, by_dp, by_mp,
        ),
        check_vma=False,
    )
```

```python
import functools

import jax
import jax.numpy as jnp
from jax import lax
from jax.experimental import pallas as pl
from jax.experimental.pallas import tpu as pltpu
from jax.sharding import PartitionSpec as P

HEAD_DIM = 64
TILE_Q = 128
TILE_K = 256
EPSILON = 1e-06
NEGATIVE = -1e30
HIGHEST = lax.Precision.HIGHEST
F32 = jnp.float32
BF16 = jnp.bfloat16


def dot(left, right, dims, precision=None):
    return lax.dot_general(
        left, right, ((dims[0], dims[1]), ((), ())), precision=precision, preferred_element_type=F32
    )


def mm(left, right):
    return dot(left, right, ((1,), (0,)))


def mm_nt(left, right):
    return dot(left, right, ((1,), (1,)))


def mm_tn(left, right):
    return dot(left, right, ((0,), (0,)))


def round_up(value, unit):
    return (value + unit - 1) // unit * unit


def chunked(total, size, run):
    def once(n, carry):
        run(pl.multiple_of(n * size, size))
        return carry

    lax.fori_loop(0, total // size, once, 0)


MESH = pl.DeviceIdType.MESH


class Place:
    def __init__(self, mp):
        self.mp = mp
        self.i = lax.axis_index("dp")
        self.z = lax.axis_index("mp")
        core = lax.rem(self.i, 2)
        across = lax.rem(lax.div(self.i, 2), 2)
        up = lax.div(self.i, 4)
        self.core, self.across, self.up = core, across, up
        self.ic = self.i + 1 - 2 * core
        self.ix = self.i + 2 - 4 * across
        self.iy = self.i + 4 - 8 * up
        self.ixy = self.ix + 4 - 8 * up


def enter(place):
    barrier = pltpu.get_barrier_semaphore()
    z, mp = place.z, place.mp
    for near in (place.ic, place.ix, place.iy):
        pl.semaphore_signal(barrier, 1, device_id=(near, z), device_id_type=MESH)

    for d in range(1, mp):
        far = lax.rem(z + d, mp)
        pl.semaphore_signal(barrier, 1, device_id=(place.i, far), device_id_type=MESH)
    pl.semaphore_wait(barrier, 3 + mp - 1)


def nearest(z):
    upper = lax.div(z, 2)
    return [z, z + 1 - 2 * lax.rem(z, 2), 2 - upper, 3 - 3 * upper]


def onward(place, z2, act):
    z = place.z
    if z2 is z:
        pl.when(z < place.mp - 1)(lambda: act(True))
        pl.when(z > 0)(lambda: act(False))
    else:
        pl.when(jnp.logical_and(z2 < z, z < place.mp - 1))(lambda: act(True))
        pl.when(jnp.logical_and(z2 > z, z > 0))(lambda: act(False))


def staggered(slots, stages):
    def step(k):
        for late, stage in enumerate(stages):
            if 0 <= k - late < len(slots):
                stage(slots[k - late])

    return [functools.partial(step, k) for k in range(len(slots) + len(stages) - 1)]


def region(ref, i, z, shard):
    if len(ref.shape) == 4:
        return ref.at[z, i]
    rows, cols = shard
    return ref.at[pl.ds(pl.multiple_of(z * rows, rows), rows), pl.ds(pl.multiple_of(i * cols, cols), cols)]


def gather_steps(place, shards, outs, send, recv, local):
    mp, i, z = place.mp, place.i, place.z
    units = range(len(shards))

    def here(u, i2, z2):
        return region(outs[u], i2, z2, shards[u].shape)

    def copy(u, kind, i2, z2, to, src=None):
        spot = here(u, i2, z2)
        return pltpu.make_async_remote_copy(
            src_ref=spot if src is None else src, dst_ref=spot, send_sem=send.at[u, kind, z2],
            recv_sem=recv.at[u, kind, z2], device_id=to, device_id_type=MESH)

    def route(u, z2):
        odd = lax.rem(z2 + u, 2)
        first = place.ix + odd * (place.iy - place.ix)
        second = place.iy + odd * (place.ix - place.iy)
        return odd, first, second

    slots = nearest(z)

    def stage1(z2):
        for u in units:
            src = shards[u] if z2 is z else None
            if z2 is not z:
                copy(u, 0, i, z2, (i, z)).wait_recv()
            copy(u, 2, i, z2, (place.ix, z), src).start()
            copy(u, 3, i, z2, (place.iy, z), src).start()
            copy(u, 5, i, z2, (place.ic, z), src).start()
            if z2 is z:
                pltpu.make_async_copy(shards[u], here(u, i, z), local.at[u]).start()

    def along(u, d, up):
        return pltpu.make_async_remote_copy(
            src_ref=shards[u], dst_ref=here(u, i, z), send_sem=send.at[u, 0 if up else 1, d],
            recv_sem=recv.at[u, 0, z], device_id=(i, z + d if up else z - d),
            device_id_type=MESH)

    def depart():
        for d in range(1, mp):
            for u in units:
                pl.when(z < mp - d)(lambda u=u, d=d: along(u, d, True).start())
                pl.when(z >= d)(lambda u=u, d=d: along(u, d, False).start())

    def stage2(z2):
        for u in units:
            odd, first, second = route(u, z2)
            arrived(u, 2 + odd, first, z2)
            copy(u, 4, first, z2, (second, z)).start()
            copy(u, 6, first, z2, (place.ic, z)).start()

    def stage3(z2):
        for u in units:
            odd, first, second = route(u, z2)
            arrived(u, 3 - odd, second, z2)
            copy(u, 7, second, z2, (place.ic, z)).start()
            copy(u, 4, place.ixy, z2, (second, z)).wait_recv()
            copy(u, 8, place.ixy, z2, (place.ic, z)).start()

    def arrived(u, kind, i2, z2):
        spot = here(u, i2, z2)
        pltpu.make_async_remote_copy(
            src_ref=spot, dst_ref=spot, send_sem=send.at[u, kind, z2], recv_sem=recv.at[u, kind, z2],
            device_id=(i2, z), device_id_type=MESH).wait_recv()

    def other(i2):
        return i2 + place.ic - i

    def finish(z2):
        for u in units:
            odd, first, second = route(u, z2)
            for kind, i2 in ((5, i), (6, first), (7, second), (8, place.ixy)):
                copy(u, kind, other(i2), z2, (place.ic, z)).wait_recv()
            for kind in range(2, 9):
                copy(u, kind, i, z2, (i, z)).wait_send()
            if z2 is z:
                for far in range(1, mp):
                    pl.when(z < mp - far)(lambda u=u, far=far: along(u, far, True).wait_send())
                    pl.when(z >= far)(lambda u=u, far=far: along(u, far, False).wait_send())
                pltpu.make_async_copy(shards[u], here(u, i, z), local.at[u]).wait()

    steps = staggered(slots, (stage1, stage2, stage3))
    return [depart, steps[0]], steps[1:], [functools.partial(finish, slot) for slot in slots]


def gather_shape(shard, kind, dp, mp):
    rows, cols = shard.shape
    if kind == "by_dp":
        return jax.ShapeDtypeStruct((mp, dp, rows, cols), shard.dtype)
    return jax.ShapeDtypeStruct((mp * rows, dp * cols), shard.dtype)


def add_into(target, *others):
    rows = target.shape[0]
    size = 64 if rows % 64 == 0 else rows

    def some(at):
        part = pl.ds(at, size)
        total = target[part, :].astype(F32)
        for other in others:
            total = total + other[part, :].astype(F32)
        target[part, :] = total.astype(target.dtype)

    chunked(rows, size, some)


def scatter_scratch(shards, mp):
    scratch = []
    for dims, dtype in shards:
        scratch += [
            pltpu.VMEM((mp, 4) + dims, dtype),
            pltpu.VMEM((mp, 4) + dims, dtype),
            pltpu.VMEM((mp, 3) + dims, dtype),
            pltpu.VMEM((mp,) + dims, dtype),
        ]
    sems = pltpu.SemaphoreType.DMA((len(shards), 8, mp))
    return scratch + [sems, sems, pltpu.SemaphoreType.DMA((len(shards), 4, mp))]


def scatter_steps(place, grads, outs, scratch):
    mp, i, z = place.mp, place.i, place.z
    units = range(len(grads))
    send, recv, local = scratch[-3:]
    own = [scratch[4 * u] for u in units]
    sibling = [scratch[4 * u + 1] for u in units]
    plane = [scratch[4 * u + 2] for u in units]
    line = [scratch[4 * u + 3] for u in units]
    chips = (place.i, place.ix, place.iy, place.ixy)
    slots = nearest(z)[::-1]

    def piece(u, i2, z2):
        return region(grads[u], i2, z2, own[u].shape[2:])

    def copy(u, kind, z2, src, dst, to):
        return pltpu.make_async_remote_copy(
            src_ref=src, dst_ref=dst, send_sem=send.at[u, kind, z2], recv_sem=recv.at[u, kind, z2],
            device_id=to, device_id_type=MESH)

    def load(u, k, z2):
        return pltpu.make_async_copy(piece(u, chips[k], z2), own[u].at[z2, k], local.at[u, k, z2])

    def across(u, k, z2):
        other = chips[k] + place.ic - i
        return copy(u, k, z2, piece(u, other, z2), sibling[u].at[z2, k], (place.ic, z))

    def route(u, z2):
        odd = lax.rem(z2 + u, 2)
        first = place.ix + odd * (place.iy - place.ix)
        second = place.iy + odd * (place.ix - place.iy)
        return 1 + odd, 2 - odd, first, second

    def to_second(u, z2, far):
        _, ks, _, second = route(u, z2)
        src = own[u].at[z2, 3] if far else own[u].at[z2, ks]
        return copy(u, 4 if far else 5, z2, src, plane[u].at[z2, 0 if far else 1], (second, z))

    def to_first(u, z2):
        kf, _, first, _ = route(u, z2)
        return copy(u, 6, z2, own[u].at[z2, kf], plane[u].at[z2, 2], (first, z))

    def along(u, z2):
        return pltpu.make_async_remote_copy(
            src_ref=own[u].at[z2, 0], dst_ref=line[u].at[z], send_sem=send.at[u, 7, z2],
            recv_sem=recv.at[u, 7, z], device_id=(i, z2), device_id_type=MESH)

    def arrival(u, z2):
        return pltpu.make_async_remote_copy(
            src_ref=own[u].at[z, 0], dst_ref=line[u].at[z2], send_sem=send.at[u, 7, z],
            recv_sem=recv.at[u, 7, z2], device_id=(i, z), device_id_type=MESH)

    def begin(z2):
        for u in units:
            for k in (3, 2, 1, 0):
                load(u, k, z2).start()
                across(u, k, z2).start()

    def stage1(z2):
        for u in units:
            for k in (3, 2, 1, 0):
                load(u, k, z2).wait()
                across(u, k, z2).wait_recv()
                add_into(own[u].at[z2, k], sibling[u].at[z2, k])
                if k == 3:
                    to_second(u, z2, True).start()
            to_second(u, z2, False).start()

    def stage2(z2):
        for u in units:
            kf = route(u, z2)[0]
            to_second(u, z2, True).wait_recv()
            add_into(own[u].at[z2, kf], plane[u].at[z2, 0])
            to_first(u, z2).start()

    def stage3(z2):
        for u in units:
            mine = own[u].at[z2, 0]
            to_second(u, z2, False).wait_recv()
            to_first(u, z2).wait_recv()
            add_into(mine, plane[u].at[z2, 1], plane[u].at[z2, 2])
            if z2 is not z:
                along(u, z2).start()

    def collect(z2):
        for u in units:
            if z2 is z:
                outs[u][...] = own[u][z, 0].astype(F32)
            else:
                arrival(u, z2).wait_recv()
                add_into(outs[u], line[u].at[z2])

    def finish(z2):
        for u in units:
            for k in range(4):
                across(u, k, z2).wait_send()
            to_second(u, z2, True).wait_send()
            to_second(u, z2, False).wait_send()
            to_first(u, z2).wait_send()
            if z2 is not z:
                along(u, z2).wait_send()

    steps = staggered(slots, (stage1, stage2, stage3))
    head = [functools.partial(begin, z2) for z2 in slots]
    last = [functools.partial(collect, z2) for z2 in nearest(z)]
    return head, steps, last + [functools.partial(finish, z2) for z2 in slots]


def shard_of(grad, dp, mp):
    if len(grad.shape) == 4:
        return grad.shape[2:]
    return (grad.shape[0] // mp, grad.shape[1] // dp)


def line_steps(place, rows, outs, send, recv, local):
    mp, i, z = place.mp, place.i, place.z

    def spot(u, z2):
        parts = outs[u].shape[2]
        return outs[u].at[lax.div(z2, parts), :, lax.rem(z2, parts)]

    def copy(u, up, z2, to, src=None):
        here = spot(u, z2)
        kind = 0 if up else 1
        return pltpu.make_async_remote_copy(
            src_ref=here if src is None else src, dst_ref=here, send_sem=send.at[u, kind, z2],
            recv_sem=recv.at[u, kind, z2], device_id=(i, to), device_id_type=MESH)

    def keep(u):
        return pltpu.make_async_copy(rows[u], spot(u, z), local.at[u])

    def move(z2):
        for u in range(len(rows)):
            src = None
            if z2 is z:
                src = rows[u]
                keep(u).start()
            else:
                pl.when(z2 < z)(lambda: copy(u, True, z2, z).wait_recv())
                pl.when(z2 > z)(lambda: copy(u, False, z2, z).wait_recv())
            onward(place, z2, lambda up: copy(u, up, z2, z + 1 if up else z - 1, src).start())

    def finish(z2):
        for u in range(len(rows)):
            if z2 is z:
                keep(u).wait()
            onward(place, z2, lambda up: copy(u, up, z2, z).wait_send())

    slots = nearest(z)
    steps = [functools.partial(move, z2) for z2 in slots]
    return steps[:1], steps[1:], [functools.partial(finish, z2) for z2 in slots]


def woven(lists):
    placed = [(place, k, n) for k, (_, places) in enumerate(lists) for n, place in enumerate(places)]
    return [lists[k][0][n] for _, k, n in sorted(placed)]


class Transfers:
    swap = None

    def __init__(self, dp, mp, cid, shards=(), kinds=(), grads=(), rows=(), spread=()):
        self.dp, self.mp, self.cid = dp, mp, cid
        self.shards, self.kinds, self.grads = list(shards), list(kinds), list(grads)
        self.rows = list(rows)
        self.args = self.shards + self.grads + self.rows
        spots = [(shard_of(g, dp, mp), g.dtype) for g in self.grads]
        self.outs = [gather_shape(s, k, dp, mp) for s, k in zip(shards, kinds)]
        self.outs += [jax.ShapeDtypeStruct(s, F32) for s, _ in spots]
        any_space = pl.BlockSpec(memory_space=pl.ANY)
        self.in_specs = [any_space] * len(self.args)
        self.out_specs = [any_space] * len(self.shards)
        self.out_specs += [pl.BlockSpec(s, lambda *_: (0, 0)) for s, _ in spots]
        self.outs += [jax.ShapeDtypeStruct(dims, r.dtype) for r, dims in zip(self.rows, spread)]
        self.out_specs += [any_space] * len(self.rows)
        self.scratch = []
        if self.rows:
            sems = pltpu.SemaphoreType.DMA((len(self.rows), 2, mp))
            self.scratch += [sems, sems, pltpu.SemaphoreType.DMA((len(self.rows),))]
        if self.shards:
            sems = pltpu.SemaphoreType.DMA((len(self.shards), 9, mp))
            self.scratch += [sems, sems, pltpu.SemaphoreType.DMA((len(self.shards),))]
        if self.grads:
            self.scratch += scatter_scratch(spots, mp)

    def steps(self, ins, outs, scratch):
        place = Place(self.mp)
        first, lists, last = [functools.partial(enter, place)], [], []

        def take(head, steps, ends, slow=False):
            first.extend(head)
            paces = [0.45 * (n + 1) if slow else n / len(steps) for n in range(len(steps))]
            lists.append((steps, paces))
            last.extend(ends)

        count, more = len(self.shards), len(self.shards) + len(self.grads)
        if self.rows:
            take(*line_steps(place, ins[more:], outs[more:], *scratch[:3]), slow=True)
            scratch = scratch[3:]
        if count:
            take(*gather_steps(place, ins[:count], outs[:count], *scratch[:3]))
            scratch = scratch[3:]
        if self.grads:
            take(*scatter_steps(place, ins[count:more], outs[count:more], scratch))
        return first, woven(lists), last

    def params(self, limit):
        return pltpu.CompilerParams(
            collective_id=self.cid, has_side_effects=True, vmem_limit_bytes=limit
        )

    def run(self, name):
        count = len(self.args)

        def kernel(*refs):
            outs = refs[count : count + len(self.outs)]
            first, steps, last = self.steps(refs[:count], outs, refs[count + len(self.outs) :])
            for step in first + steps + last:
                step()

        return pl.pallas_call(
            kernel, grid=(1,), out_shape=self.outs, in_specs=self.in_specs, out_specs=self.out_specs,
            scratch_shapes=self.scratch, compiler_params=self.params(60 << 20), name=name,
        )(*self.args)


class Pace:
    def __init__(self, found, each):
        self.first, self.steps, self.last = found
        self.group, self.groups, self.each, self.at = pl.program_id(0), pl.num_programs(0), each, 0

    def place(self):
        total = self.groups * self.each

        def begin():
            for step in self.first:
                step()

        if self.at == 0 and self.first:
            pl.when(self.group == 0)(begin)
        for n, step in enumerate(self.steps):
            group, at = divmod((n + 1) * total // (len(self.steps) + 1), self.each)
            if at == self.at:
                pl.when(self.group == group)(step)
        self.at += 1

    def end(self):
        @pl.when(self.group == self.groups - 1)
        def _():
            for step in self.last:
                step()


def skew(row, height):
    wide = jnp.broadcast_to(row, (height, row.shape[1]))
    return pltpu.roll(wide, 0, axis=1, stride=1, stride_axis=0)


def widened(tile):
    zero = jnp.zeros((tile.shape[0], HEAD_DIM), tile.dtype)
    found = []
    for h in range(4):
        piece = tile[:, HEAD_DIM * h : HEAD_DIM * (h + 1)]
        found.append(jnp.concatenate([piece, zero] if h < 2 else [zero, piece], axis=1))
    return jnp.concatenate(found, axis=0)


def narrowed(wide):
    n = wide.shape[1] // 4
    found = []
    for h in range(4):
        base = HEAD_DIM * (h // 2)
        found.append(wide[base : base + HEAD_DIM, n * h : n * (h + 1)])
    return jnp.concatenate(found, axis=0).T


def four(row):
    return jnp.concatenate([row] * 4, axis=1)


class Tiles:
    def __init__(self, rows, length, parts):
        self.rows, self.parts, self.blk = rows, parts, 64 // parts
        self.list = [(at, min(TILE_Q, rows - at)) for at in range(0, rows, TILE_Q)]
        self.span = TILE_Q * parts // TILE_K
        self.reach = round_up(length, TILE_K)
        self.strips = len(self.list) * self.span
        self.lead = self.span * TILE_K
        self.width = self.lead + self.strips * TILE_K

    def keys(self, a):
        return min((a + 1) * self.span, self.reach // TILE_K)

    def strip(self, a, m):
        return (a + 1) * self.span - 1 - m

    def windows(self, n):
        runs = [(s * self.blk, 64 * s) for s in range(n // self.blk)]
        return [(e, self.lead + (e + 1 - self.span) * TILE_K, runs) for e in range(self.strips)]


def build_strips(tiles, vec_ref, strip, tail):
    for h in range(4):
        moved = skew(vec_ref[0, h : h + 1, :], TILE_K)
        for ref in (strip, tail):
            n = ref.shape[2] // 4
            for e, at, runs in tiles.windows(n):
                cut = [moved[:, at + far : at + far + tiles.blk] for _, far in runs]
                ref[e, :, n * h : n * (h + 1)] = jnp.concatenate(cut, axis=1)


def split_refs(refs, host, ins, outs):
    if host is None:
        return list(refs), ([], [], [])
    a, b = len(host.args), len(host.outs)
    cut = [0, ins, ins + a, ins + a + outs, ins + a + outs + b, len(refs) - len(host.scratch), len(refs)]
    part = [list(refs[i:j]) for i, j in zip(cut, cut[1:])]
    return part[0] + part[2] + part[4], host.steps(part[1], part[3], part[5])


def tile_valid(biased, mask, keys_ref, m):
    if biased:
        index = lax.broadcasted_iota(jnp.int32, (TILE_K, mask.shape[1]), 0)
        return index >= mask - m * TILE_K
    keys = keys_ref[pl.ds(m * TILE_K, TILE_K), :]
    reps = -(-mask.shape[1] // keys.shape[1])
    return jnp.concatenate([keys] * reps, axis=1)[:, : mask.shape[1]] == mask


def forward_kernel(biased, tiles, host, *refs):
    refs, steps = split_refs(refs, host, 5, 2)
    if biased:
        q_ref, k_ref, v_ref, mask_ref, vec_ref, o_ref, lse_ref, vt, s_s, strip, tail = refs
        keys_ref = None
        build_strips(tiles, vec_ref, strip, tail)
    else:
        q_ref, k_ref, v_ref, mask_ref, keys_ref, o_ref, lse_ref, vt, s_s = refs
    vt[...] = v_ref[...].T
    counts = [tiles.keys(a) if biased else k_ref.shape[0] // TILE_K for a in range(len(tiles.list))]
    pace = Pace(steps, 2 * sum(counts))
    for a, (at, n) in enumerate(tiles.list):
        lanes = 4 * n
        q4 = widened(q_ref[at : at + n, :])
        mask = mask_ref[a : a + 1, :lanes]
        count = counts[a]
        top = None
        for m in range(count):
            pace.place()
            some = slice(m * TILE_K, (m + 1) * TILE_K)
            s = mm_nt(k_ref[some, :], q4)
            if biased:
                s = s + (strip if n == TILE_Q else tail)[tiles.strip(a, m)]
            s = jnp.where(tile_valid(biased, mask, keys_ref, m), s, NEGATIVE)
            s_s[some, :lanes] = s
            here = jnp.max(s, axis=0, keepdims=True)
            top = here if top is None else jnp.maximum(top, here)
        total = jnp.zeros((1, lanes), F32)
        acc = jnp.zeros((2 * HEAD_DIM, lanes), F32)
        for m in range(count):
            pace.place()
            some = slice(m * TILE_K, (m + 1) * TILE_K)
            p = jnp.exp(s_s[some, :lanes] - top)
            total = total + jnp.sum(p, axis=0, keepdims=True)
            acc = acc + mm(vt[:, some], p.astype(BF16))
        o_ref[at : at + n, :] = narrowed(acc / total).astype(BF16)
        lse_ref[0, a : a + 1, :lanes] = top + jnp.log(total)
    pace.end()


class Exchange:
    def __init__(self, groups, blk, steps):
        self.groups, self.blk, self.steps = groups, blk, steps
        self.rows = groups * blk
        block = (steps, 2, groups, blk, 2 * HEAD_DIM)
        self.scratch = [pltpu.VMEM(block, BF16), pltpu.VMEM(block, BF16), pltpu.VMEM(block, F32)]
        sems = pltpu.SemaphoreType.DMA((steps,))
        self.scratch += [sems, sems]

    def copy(self, place, refs, n):
        gone, come, _, send, recv = refs
        mate = place.z + 1 - 2 * lax.rem(place.z, 2)
        return pltpu.make_async_remote_copy(
            src_ref=gone.at[n], dst_ref=come.at[n], send_sem=send.at[n], recv_sem=recv.at[n],
            device_id=(place.i, mate), device_id_type=MESH)

    def part_of(self, ref, part):
        base = pl.multiple_of(part * self.blk, self.blk)
        if self.groups == 1:
            return ref[pl.ds(base, self.blk), :][None]
        view = ref.reshape(ref.shape[0] // (2 * self.blk), 2 * self.blk, ref.shape[1])
        return view[0 : self.groups, pl.ds(base, self.blk), :]

    def give(self, place, refs, sums):
        n = pl.program_id(0)
        gone, _, kept, _, _ = refs
        part = lax.rem(place.z, 2)
        for which, ref in enumerate(sums):
            gone[n, which] = self.part_of(ref, 1 - part).astype(BF16)
            kept[n, which] = self.part_of(ref, part)
        self.copy(place, refs, n).start()

    def take(self, place, refs, out):
        _, come, kept, _, _ = refs
        cols = 2 * HEAD_DIM
        for n in range(self.steps):
            self.copy(place, refs, n).wait()
            for which in range(2):
                total = kept[n, which] + come[n, which].astype(F32)
                at = (which * self.steps + n) * cols
                out[:, at : at + cols] = total.reshape(self.rows, cols).astype(BF16)


def backward_kernel(biased, tiles, host, *refs):
    swap = None if host is None else host.swap
    refs, steps = split_refs(refs, host, 8, (4 if biased else 3) - (swap is not None))
    if swap is not None:
        swap_refs = refs[-len(swap.scratch) :]
        first = 10 + biased
        refs = refs[:first] + [None] + refs[first : -len(swap.scratch)]
    if biased:
        (
            q_ref, k_ref, v_ref, o_ref, do_ref, lse_ref, mask_ref, vec_ref,
            dq_ref, dist_ref, dv_ref, dk_ref, kt, dk_s, dv_s, strip, tail, slope, slope_tail, line,
        ) = refs
        keys_ref = None
        build_strips(tiles, vec_ref, strip, tail)
        slope[...] = jnp.zeros_like(slope)
        slope_tail[...] = jnp.zeros_like(slope_tail)
    else:
        (
            q_ref, k_ref, v_ref, o_ref, do_ref, lse_ref, mask_ref, keys_ref,
            dq_ref, dv_ref, dk_ref, kt, dk_s, dv_s,
        ) = refs
    kt[...] = k_ref[...].T
    dk_s[...] = jnp.zeros_like(dk_s)
    dv_s[...] = jnp.zeros_like(dv_s)
    counts = [tiles.keys(a) if biased else k_ref.shape[0] // TILE_K for a in range(len(tiles.list))]
    pace = Pace(steps, sum(counts))
    for a, (at, n) in enumerate(tiles.list):
        lanes = 4 * n
        q4 = widened(q_ref[at : at + n, :])
        do4 = widened(do_ref[at : at + n, :])
        mask = mask_ref[a : a + 1, :lanes]
        lse = lse_ref[0, a : a + 1, :lanes]
        both = widened(o_ref[at : at + n, :]).astype(F32) * do4.astype(F32)
        delta = jnp.sum(both.T, axis=0, keepdims=True)
        dq = jnp.zeros((2 * HEAD_DIM, lanes), F32)
        for m in range(counts[a]):
            pace.place()
            some = slice(m * TILE_K, (m + 1) * TILE_K)
            s = mm_nt(k_ref[some, :], q4)
            if biased:
                e = tiles.strip(a, m)
                s = s + (strip if n == TILE_Q else tail)[e]
            p = jnp.exp(jnp.where(tile_valid(biased, mask, keys_ref, m), s - lse, NEGATIVE))
            ds = p * (mm_nt(v_ref[some, :], do4) - delta)
            low = ds.astype(BF16)
            if biased:
                ref = slope if n == TILE_Q else slope_tail
                ref[e] += ds
            dv_s[some, :] += mm(p.astype(BF16), do4)
            dk_s[some, :] += mm(low, q4)
            dq = dq + mm(kt[:, some], low)
        dq_ref[at : at + n, :] = narrowed(dq).astype(BF16)

    if swap is None:
        dk_ref[...] = dk_s[...].astype(BF16)
        dv_ref[...] = dv_s[...].astype(BF16)
    else:
        place = Place(host.mp)
        swap.give(place, swap_refs, (dk_s, dv_s))
    if biased:
        width = tiles.width
        for h in range(4):
            line[...] = jnp.zeros_like(line)
            for ref in (slope, slope_tail):
                n = ref.shape[2] // 4
                for e, at, runs in tiles.windows(n):
                    for near, far in runs:
                        piece = ref[e, :, n * h + near : n * h + near + tiles.blk]
                        line[:, at + far : at + far + tiles.blk] += piece
            part = line[...]
            height = TILE_K
            while height > 8:
                height //= 2
                part = part[:height] + pltpu.roll(part[height:], width - height, axis=1)
            row = part[0:1]
            for j in range(1, 8):
                row = row + pltpu.roll(part, width - j, axis=1)[j : j + 1]
            dist_ref[0, h : h + 1, :] = row
    pace.end()
    if swap is not None:
        pl.when(pace.group == pace.groups - 1)(lambda: swap.take(place, swap_refs, dv_ref))


def spec(shape, index):
    return pl.BlockSpec(shape, index)


def attention_call(kernel, biased, tiles, outs, scratch, args, name, flops, host):
    steps = args[1].shape[1] // (2 * HEAD_DIM)

    def column(array, lanes):
        return spec((array.shape[0], lanes), lambda i: (0, i))

    def placed(array, kind):
        if kind == "wide":
            return column(array, 4 * HEAD_DIM)
        if kind == "key":
            return column(array, 2 * HEAD_DIM)
        if kind == "head":
            return spec((1,) + array.shape[1:], lambda i: (i, 0, 0))
        return spec(array.shape, lambda i: (0, 0))

    kinds = ["wide", "key", "key"]
    if kernel is backward_kernel:
        kinds += ["wide", "wide", "head"]
    kinds += ["flat", "head" if biased else "flat"]
    specs = [placed(array, kind) for array, kind in zip(args, kinds)]
    shapes = [item for item, _ in outs]
    out_specs = [placed(item, kind) for item, kind in outs]
    own = len(shapes)
    params = pltpu.CompilerParams(vmem_limit_bytes=60 << 20)
    args = list(args)
    if host is not None:
        args += host.args
        specs += host.in_specs
        shapes += host.outs
        out_specs += host.out_specs
        scratch = scratch + host.scratch
        params = host.params(62 << 20)
    found = pl.pallas_call(
        functools.partial(kernel, biased, tiles, host),
        grid=(steps,),
        out_shape=shapes,
        in_specs=specs,
        out_specs=out_specs,
        scratch_shapes=scratch,
        compiler_params=params,
        cost_estimate=pl.CostEstimate(flops=flops, bytes_accessed=16 << 20, transcendentals=0),
        name=name,
    )(*args)
    return found[:own], found[own:]


def strip_scratch(tiles):
    last = tiles.list[-1][1]
    return [
        pltpu.VMEM((tiles.strips, TILE_K, 4 * TILE_Q), F32),
        pltpu.VMEM((tiles.strips, TILE_K, 4 * last), F32),
    ]


def attend_forward(q, k, v, mask, extra, tiles, biased, name, host=None):
    steps = k.shape[1] // (2 * HEAD_DIM)
    outs = [
        (jax.ShapeDtypeStruct(q.shape, BF16), "wide"),
        (jax.ShapeDtypeStruct((steps,) + mask.shape, F32), "head"),
    ]
    scratch = [pltpu.VMEM((2 * HEAD_DIM, k.shape[0]), BF16), pltpu.VMEM((k.shape[0], 4 * TILE_Q), F32)]
    if biased:
        scratch += strip_scratch(tiles)
    flops = 4 * q.shape[0] * k.shape[0] * q.shape[1]
    return attention_call(
        forward_kernel, biased, tiles, outs, scratch, (q, k, v, mask, extra), name, flops, host
    )


def attend_backward(q, k, v, o, do, lse, mask, extra, tiles, biased, name, host=None):
    keys, cols = k.shape
    grad = jax.ShapeDtypeStruct(k.shape, BF16)
    outs = [(jax.ShapeDtypeStruct(q.shape, BF16), "wide")]
    scratch = [
        pltpu.VMEM((2 * HEAD_DIM, keys), BF16),
        pltpu.VMEM((keys, 2 * HEAD_DIM), F32),
        pltpu.VMEM((keys, 2 * HEAD_DIM), F32),
    ]
    if biased:
        outs.append((jax.ShapeDtypeStruct(extra.shape, F32), "head"))
        scratch += strip_scratch(tiles) * 2 + [pltpu.VMEM((TILE_K, tiles.width), F32)]
    if host is None:
        outs += [(grad, "key"), (grad, "key")]
    else:
        outs.append((jax.ShapeDtypeStruct((host.swap.rows, 2 * cols), BF16), "flat"))
        scratch += host.swap.scratch
    flops = 10 * q.shape[0] * keys * q.shape[1]
    return attention_call(
        backward_kernel, biased, tiles, outs, scratch, (q, k, v, o, do, lse, mask, extra), name,
        flops, host,
    )


def inverse_rms(state):
    return lax.rsqrt(jnp.mean(state * state, axis=-1, keepdims=True) + EPSILON)


def norm_back(state, gain, grad_normed):
    scale = inverse_rms(state)
    weighted = grad_normed * gain
    grad_gain = jnp.sum(grad_normed * state * scale, axis=0, keepdims=True)
    inner = jnp.mean(weighted * state, axis=-1, keepdims=True)
    return scale * weighted - state * (scale * scale * scale) * inner, grad_gain


def row_chunk(rows):
    for size in (544, 272, 256, 128):
        if rows % size == 0:
            return size
    return rows


def full(array):
    return pl.BlockSpec(array.shape, lambda j, w: (0,) * len(array.shape))


def lead_block(array):
    return pl.BlockSpec((1,) + array.shape[1:], lambda j, w: (j,) + (0,) * (len(array.shape) - 1))


def col_block(array, parts):
    return pl.BlockSpec((array.shape[0], array.shape[1] // parts), lambda j, w: (0, j))


def row_block(array, parts):
    return pl.BlockSpec((array.shape[0] // parts, array.shape[1]), lambda j, w: (j, 0))


def kernel_call(body, name, steps, where, ins, outs, scratch, flops):
    return pl.pallas_call(
        lambda _, *refs: body(*refs),
        out_shape=[jax.ShapeDtypeStruct(a.shape, a.dtype) for a, _ in outs],
        grid_spec=pltpu.PrefetchScalarGridSpec(
            num_scalar_prefetch=1,
            grid=(steps,),
            in_specs=[s for _, s in ins],
            out_specs=[s for _, s in outs],
            scratch_shapes=scratch,
        ),
        compiler_params=pltpu.CompilerParams(vmem_limit_bytes=60 << 20),
        cost_estimate=pl.CostEstimate(flops=flops, bytes_accessed=16 << 20, transcendentals=0),
        name=name,
    )(where, *[a for a, _ in ins])


def my_rows(array):
    block = (None, array.shape[1], None) + array.shape[3:]
    return array, pl.BlockSpec(block, lambda j, w: (w[0], 0, w[1], 0, 0))


def my_sequence(array):
    return array, pl.BlockSpec((None,) + array.shape[1:], lambda j, w: (w[0], 0, 0))


def flat(ref):
    return ref.reshape(ref.shape[0] * ref.shape[1], ref.shape[2])


def shape(dims, dtype=BF16):
    return jax.ShapeDtypeStruct(dims, dtype)


def project_kernel(x_ref, own_ref, gain_ref, w_ref, q_ref, k_ref, v_ref, n_ref, normed):
    length = x_ref.shape[0]
    qcols = q_ref.shape[1]
    kcols = k_ref.shape[1]
    size = row_chunk(length)

    @pl.when(pl.program_id(0) == 0)
    def _():
        def norm_rows(at):
            x = x_ref[pl.ds(at, size), :].astype(F32)
            normed[pl.ds(at, size), :] = (x * inverse_rms(x) * gain_ref[...]).astype(BF16)

        chunked(length, size, norm_rows)
        x = flat(own_ref)[...].astype(F32)
        n_ref[...] = (x * inverse_rms(x) * gain_ref[...]).astype(BF16)

    q_ref[...] = mm(n_ref[...], w_ref[0, :, :qcols]).astype(BF16)

    def keys(at):
        kv = mm(normed[pl.ds(at, size), :], w_ref[0, :, qcols:]).astype(BF16)
        k_ref[pl.ds(at, size), :] = kv[:, :kcols]
        v_ref[pl.ds(at, size), :] = kv[:, kcols:]

    chunked(length, size, keys)
    k_ref[length:, :] = jnp.zeros((k_ref.shape[0] - length, kcols), BF16)
    v_ref[length:, :] = jnp.zeros((k_ref.shape[0] - length, kcols), BF16)


def self_project(where, x, own, gain, w, reach, rows):
    _, length, width = x.shape
    groups, _, cols = w.shape
    q, k = shape((rows, groups * cols // 2)), shape((reach, groups * cols // 4))
    n = shape((rows, width))
    return kernel_call(
        project_kernel, "self_project", groups, where,
        [my_sequence(x), my_rows(own), (gain, full(gain)), (w, lead_block(w))],
        [(q, col_block(q, groups)), (k, col_block(k, groups)), (k, col_block(k, groups)), (n, full(n))],
        [pltpu.VMEM((length, width), BF16)], (length + rows) * width * groups * cols,
    )


def middle_kernel(o_ref, wo_ref, x_ref, gain_ref, m_ref, w_ref, h_ref, n_ref, q_ref, k_ref, v_ref):
    rows, qcols = q_ref.shape
    kcols = k_ref.shape[1]
    size = row_chunk(rows)
    x_ref = flat(x_ref)

    @pl.when(pl.program_id(0) == 0)
    def _():
        def state(at):
            some = pl.ds(at, size)
            h = x_ref[some, :].astype(F32) + mm(o_ref[some, :], wo_ref[...])
            h_ref[some, :] = h
            n_ref[some, :] = (h * inverse_rms(h) * gain_ref[...]).astype(BF16)

        chunked(rows, size, state)

    q_ref[...] = mm(n_ref[...], w_ref[0, :, :qcols]).astype(BF16)
    kv = mm(m_ref[...], w_ref[0, :, qcols:]).astype(BF16)
    k_ref[...] = kv[:, :kcols]
    v_ref[...] = kv[:, kcols:]


def cross_project(where, o, wo, own, gain, memory, w):
    rows, width = o.shape
    groups, _, cols = w.shape
    h, n = shape((rows, width), F32), shape((rows, width))
    q = shape(o.shape)
    k = shape((memory.shape[1], groups * cols // 4))
    return kernel_call(
        middle_kernel, "cross_project", groups, where,
        [(o, full(o)), (wo, full(wo)), my_rows(own), (gain, full(gain)), my_sequence(memory),
         (w, lead_block(w))],
        [(h, full(h)), (n, full(n)), (q, col_block(q, groups)), (k, col_block(k, groups)),
         (k, col_block(k, groups))],
        [], 6 * rows * width * width,
    )


def gate_parts(value):
    square = value * value
    inner = jnp.tanh(0.7978845608028654 * (value + 0.044715 * square * value))
    half = 0.5 * (1.0 + inner)
    slope = 0.7978845608028654 * (1.0 + 3.0 * 0.044715 * square)
    return value * half, half + 0.5 * value * (1.0 - inner * inner) * slope


def feed_kernel(
    o_ref, wo_ref, h1_ref, gain_ref, up_ref, wa_ref, wb_ref, wd_ref,
    out_ref, g2_ref, gain_out, gwa_ref, gwb_ref, gwd_ref, do_ref, gwo_ref,
    h2, normed, total, back, hidden_s, grad_s,
):
    rows, width = h1_ref.shape
    j = pl.program_id(0)
    size = row_chunk(rows)
    up_ref = flat(up_ref)
    cols = wd_ref.shape[0]
    cut = wa_ref.shape[2]

    @pl.when(j == 0)
    def _():
        def state(at):
            some = pl.ds(at, size)
            h = h1_ref[some, :] + mm(o_ref[some, :], wo_ref[...])
            h2[some, :] = h
            normed[some, :] = (h * inverse_rms(h) * gain_ref[...]).astype(BF16)
            total[some, :] = h
            back[some, :] = jnp.zeros((size, width), F32)

        chunked(rows, size, state)

    def hidden_rows(at):
        some = pl.ds(at, size)
        n = normed[some, :]
        g = up_ref[some, :]
        both = jnp.concatenate([mm(n, wa_ref[0]), mm(n, wb_ref[0])], axis=1)
        gate, up = both[:, :cols], both[:, cols:]
        grad_hidden = mm_nt(g, wd_ref[...])
        active, pull = gate_parts(gate)
        hidden = (active * up).astype(BF16)
        grad_gate = (grad_hidden * up * pull).astype(BF16)
        grad_up = (grad_hidden * active).astype(BF16)
        hidden_s[some, :] = hidden
        grads = jnp.concatenate([grad_gate, grad_up], axis=1)
        grad_s[some, :] = grads
        total[some, :] += mm(hidden, wd_ref[...])
        back[some, :] += mm_nt(grads[:, :cut], wa_ref[0]) + mm_nt(grads[:, cut:], wb_ref[0])

    chunked(rows, size, hidden_rows)

    def weight_rows(at):
        some = pl.ds(at, 512)
        n = normed[:, some]
        gw = mm_tn(n, grad_s[...]).astype(BF16)
        gwa_ref[0, some, :] = gw[:, :cut]
        gwb_ref[0, some, :] = gw[:, cut:]
        gwd_ref[:, some] = mm_tn(hidden_s[...], up_ref[:, some]).astype(BF16)

    chunked(width, 512, weight_rows)

    @pl.when(j == pl.num_programs(0) - 1)
    def _():
        gain_out[...] = jnp.zeros_like(gain_out)
        do_ref[...] = jnp.zeros_like(do_ref)

        def finish(at):
            some = pl.ds(at, size)
            out_ref[some, :] = total[some, :].astype(BF16)
            change, grad_gain = norm_back(h2[some, :], gain_ref[...], back[some, :])
            gain_out[...] += grad_gain
            g2 = up_ref[some, :].astype(F32) + change
            g2_ref[some, :] = g2
            low = g2.astype(BF16)
            normed[some, :] = low
            do_ref[some, :] = mm_nt(low, wo_ref[...]).astype(BF16)

        chunked(rows, size, finish)

        def out_rows(at):
            some = pl.ds(at, 512)
            gwo_ref[some, :] = mm_tn(o_ref[0:rows, some], normed[...]).astype(BF16)

        chunked(width, 512, out_rows)


def feed(where, o, wo, h1, gain, upstream, wa, wb, wd):
    rows, width = h1.shape
    groups = wa.shape[0]
    cols = wa.shape[2] + wb.shape[2]
    out, g2, gg = shape(h1.shape), shape(h1.shape, F32), shape((1, width), F32)
    return kernel_call(
        feed_kernel, "feed", groups, where,
        [(o, full(o)), (wo, full(wo)), (h1, full(h1)), (gain, full(gain)), my_rows(upstream),
         (wa, lead_block(wa)), (wb, lead_block(wb)), (wd, row_block(wd, groups))],
        [(out, full(out)), (g2, full(g2)), (gg, full(gg)), (wa, lead_block(wa)), (wb, lead_block(wb)),
         (wd, row_block(wd, groups)), (o, full(o)), (wo, full(wo))],
        [pltpu.VMEM((rows, width), F32), pltpu.VMEM((rows, width), BF16), pltpu.VMEM((rows, width), F32),
         pltpu.VMEM((rows, width), F32)] + [pltpu.VMEM((rows, cols // 2), BF16), pltpu.VMEM((rows, cols), BF16)],
        9 * rows * width * groups * cols,
    )


def back_kernel(
    dq_ref, w_ref, n_ref, h_ref, gain_ref, g2_ref, wo_ref, o_ref,
    gw_ref, g1_ref, gain_out, do_ref, gwo_ref, back, low_s,
):
    rows, width = h_ref.shape
    qcols = dq_ref.shape[1]
    j = pl.program_id(0)
    size = row_chunk(rows)

    @pl.when(j == 0)
    def _():
        back[...] = jnp.zeros_like(back)

    back[...] += mm_nt(dq_ref[0:rows, :], w_ref[0, :, :qcols])

    def weight_rows(at):
        some = pl.ds(at, 512)
        gw_ref[0, some, :] = mm_tn(n_ref[:, some], dq_ref[0:rows, :]).astype(BF16)

    chunked(width, 512, weight_rows)

    @pl.when(j == pl.num_programs(0) - 1)
    def _():
        gain_out[...] = jnp.zeros_like(gain_out)
        do_ref[...] = jnp.zeros_like(do_ref)

        def finish(at):
            some = pl.ds(at, size)
            change, grad_gain = norm_back(h_ref[some, :], gain_ref[...], back[some, :])
            gain_out[...] += grad_gain
            g1 = g2_ref[some, :] + change
            g1_ref[some, :] = g1
            low = g1.astype(BF16)
            low_s[some, :] = low
            do_ref[some, :] = mm_nt(low, wo_ref[...]).astype(BF16)

        chunked(rows, size, finish)

        def out_rows(at):
            some = pl.ds(at, 512)
            gwo_ref[some, :] = mm_tn(o_ref[0:rows, some], low_s[...]).astype(BF16)

        chunked(width, 512, out_rows)


def cross_back(where, dq, w, n, h, gain, g2, wo, o):
    rows, width = h.shape
    groups, _, cols = w.shape
    gw = shape((groups, width, cols // 2))
    gg = shape((1, width), F32)
    return kernel_call(
        back_kernel, "cross_back", groups, where,
        [(dq, col_block(dq, groups)), (w, lead_block(w)), (n, full(n)), (h, full(h)), (gain, full(gain)),
         (g2, full(g2)), (wo, full(wo)), (o, full(o))],
        [(gw, lead_block(gw)), (g2, full(g2)), (gg, full(gg)), (o, full(o)), (wo, full(wo))],
        [pltpu.VMEM((rows, width), F32), pltpu.VMEM((rows, width), BF16)],
        8 * rows * width * width,
    )


def memory_kernel(dk_ref, dv_ref, w_ref, m_ref, gw_ref, gm_ref, back):
    j = pl.program_id(0)
    qcols = w_ref.shape[2] // 2

    @pl.when(j == 0)
    def _():
        back[...] = jnp.zeros_like(back)

    both = jnp.concatenate([dk_ref[...], dv_ref[...]], axis=1)
    back[...] += mm_nt(both, w_ref[0, :, qcols:])
    gw_ref[0] = mm_tn(m_ref[...], both).astype(BF16)

    @pl.when(j == pl.num_programs(0) - 1)
    def _():
        gm_ref[...] = back[...].astype(BF16)


def key_halves(dkv, groups):
    cols = dkv.shape[1] // (2 * groups)
    return [
        (dkv, pl.BlockSpec((dkv.shape[0], cols), lambda j, w: (0, j))),
        (dkv, pl.BlockSpec((dkv.shape[0], cols), lambda j, w: (0, j + groups))),
    ]


def memory_back(where, dkv, w, memory):
    groups, width, cols = w.shape
    gw, gm = shape((groups, width, cols // 2)), shape((dkv.shape[0], width))
    rows = pl.BlockSpec((None,) + gm.shape, lambda j, w: (w[0], w[1], 0))
    return kernel_call(
        memory_kernel, "memory_back", groups, where,
        key_halves(dkv, groups) + [(w, lead_block(w)), (memory, rows)],
        [(gw, lead_block(gw)), (gm, full(gm))],
        [pltpu.VMEM(gm.shape, F32)], 4 * gm.shape[0] * width * width,
    )


def last_kernel(
    dq_ref, dk_ref, dv_ref, w_ref, n_ref, x_ref, gain_ref, g1_ref,
    gwq_ref, gwkv_ref, gx_ref, gain_out, back,
):
    rows, width = g1_ref.shape
    j = pl.program_id(0)
    size = row_chunk(rows)
    x_ref = flat(x_ref)

    @pl.when(j == 0)
    def _():
        back[...] = jnp.zeros_like(back)

    dq = dq_ref[0:rows, :]
    dkv = jnp.concatenate([dk_ref[...], dv_ref[...]], axis=1)
    both = jnp.concatenate([dq, dkv], axis=1)
    back[...] += mm_nt(both, w_ref[0])

    def weight_rows(at):
        some = pl.ds(at, 512)
        gwq_ref[0, some, :] = mm_tn(n_ref[:, some], dq).astype(BF16)
        gwkv_ref[0, some, :] = mm_tn(n_ref[:, some], dkv).astype(BF16)

    chunked(width, 512, weight_rows)

    @pl.when(j == pl.num_programs(0) - 1)
    def _():
        gain_out[...] = jnp.zeros_like(gain_out)

        def finish(at):
            some = pl.ds(at, size)
            change, grad_gain = norm_back(x_ref[some, :].astype(F32), gain_ref[...], back[some, :])
            gain_out[...] += grad_gain
            gx_ref[some, :] = (g1_ref[some, :] + change).astype(BF16)

        chunked(rows, size, finish)


def self_back(where, dq, dkv, w, n, own, gain, g1):
    rows, width = g1.shape
    groups, _, cols = w.shape
    gw = shape((groups, width, cols // 2))
    gx = shape(g1.shape)
    gg = shape((1, width), F32)
    return kernel_call(
        last_kernel, "self_back", groups, where,
        [(dq, col_block(dq, groups))] + key_halves(dkv, groups)
        + [(w, lead_block(w)), (n, full(n)), my_rows(own), (gain, full(gain)), (g1, full(g1))],
        [(gw, lead_block(gw)), (gw, lead_block(gw)), (gx, full(gx)), (gg, full(gg))],
        [pltpu.VMEM((rows, width), F32)],
        8 * rows * width * width,
    )


def gather(shard, dims):
    for axis, name in dims:
        shard = lax.all_gather(shard, name, axis=axis, tiled=True)
    return shard


ROWS_BY_DP = ((0, "dp"), (1, "mp"))
ROWS_BY_MP = ((1, "dp"), (0, "mp"))


def scatter(grad, dims):
    for axis, name in dims:
        grad = lax.psum_scatter(grad, name, scatter_dimension=axis, tiled=True)
    return grad.astype(F32)


def grouped(weight, groups):
    rows, cols = weight.shape
    return weight.reshape(rows, groups, cols // groups).transpose(1, 0, 2)


def ungrouped(weight):
    groups, rows, cols = weight.shape
    return weight.transpose(1, 0, 2).reshape(rows, groups * cols)


def body(
    inputs,
    encoded,
    decoder_segments,
    encoder_segments,
    buckets,
    self_gain,
    self_query,
    self_key,
    self_value,
    self_out,
    position_bias,
    cross_gain,
    cross_query,
    cross_key,
    cross_value,
    cross_out,
    feed_gain,
    feed_gate,
    feed_up,
    feed_down,
    cotangent,
    *,
    dp,
    mp,
):
    batches, length, width = inputs.shape
    enc_length = encoded.shape[1]
    parts = mp // batches
    rows = length // parts
    tiles = Tiles(rows, length, parts)
    place = lax.axis_index("mp")
    sequence = place // parts
    part = place % parts
    where = jnp.stack([sequence, part]).astype(jnp.int32)
    groups = self_key.shape[1] * mp // (2 * HEAD_DIM)
    native = mp == groups and dp == 8 and parts == 2

    if native:
        order = ["by_dp", "by_mp"]
        size = width // dp
        gains = jnp.stack([self_gain, cross_gain, feed_gain])
        little = jnp.pad(position_bias.reshape(1, -1), ((0, 0), (0, size - position_bias.size)))
        little = jnp.pad(jnp.concatenate([gains, little]), ((0, 12), (0, 0)))
        w1 = jnp.concatenate([self_query, self_key, self_value], axis=1)
        w2 = jnp.concatenate([cross_query, cross_key, cross_value], axis=1)
        w1, little, wo1 = Transfers(
            dp, mp, 1, [w1, little, self_out], ["by_dp"] + order
        ).run("gather_self")
        gains = little[0, :, :3].transpose(1, 0, 2).reshape(3, 1, width).astype(F32)
        table = little[:, :, 3, : position_bias.size].reshape((mp, dp) + position_bias.shape)
        table = table.transpose(1, 2, 0, 3).reshape(dp * position_bias.shape[0], -1).astype(F32)
        w1 = w1.reshape(mp, width, w1.shape[3])
    else:
        gains = [gather(g, ((0, "dp"),)).astype(F32)[None] for g in (self_gain, cross_gain, feed_gain)]
        table = gather(position_bias, ROWS_BY_DP).astype(F32)

        def blocks(*shards):
            return jnp.concatenate([grouped(gather(s, ROWS_BY_DP), groups) for s in shards], axis=2)

        w1 = blocks(self_query, self_key, self_value)
        w2 = blocks(cross_query, cross_key, cross_value)
        w3 = blocks(feed_gate, feed_up)
        wa, wb = w3[:, :, : w3.shape[2] // 2], w3[:, :, w3.shape[2] // 2 :]
        wo1, wo2, wd = (gather(s, ROWS_BY_MP) for s in (self_out, cross_out, feed_down))
    gain_one, gain_two, gain_three = gains

    def cut(array):
        return array.reshape((array.shape[0], length // 64, parts, 64 // parts) + array.shape[2:])

    own_inputs = cut(inputs)
    docs = lax.dynamic_index_in_dim(decoder_segments, sequence, keepdims=False)
    enc_docs = lax.dynamic_index_in_dim(encoder_segments, sequence, keepdims=False)
    own_docs = lax.dynamic_slice_in_dim(docs.reshape(length // 64, 64), part * tiles.blk, tiles.blk, axis=1)
    own_docs = own_docs.reshape(rows)

    kinds = jnp.arange(4, dtype=jnp.int32)
    before = jnp.sum((docs[None, :] < kinds[:, None]).astype(jnp.int32), axis=1)
    is_doc = (own_docs[:, None] == kinds[None, :]).astype(jnp.int32)
    start = jnp.sum(is_doc * before[None, :], axis=1)

    def by_tile(row):
        found = []
        for at, n in tiles.list:
            piece = jnp.tile(row[at : at + n], 4)
            found.append(jnp.pad(piece, (0, 4 * (TILE_Q - n))))
        return jnp.stack(found)

    mask_one = by_tile(start)
    mask_two = by_tile(own_docs)
    keys_two = jnp.broadcast_to(enc_docs[:, None], (enc_length, TILE_Q))
    onehot = (buckets[:, None] == jnp.arange(table.shape[0], dtype=jnp.int32)).astype(F32)
    by_distance = dot(table, onehot, ((0,), (1,)), HIGHEST)
    heads = by_distance.shape[0]
    vec = jnp.pad(by_distance, ((0, 0), (0, tiles.width)))
    vec = jnp.concatenate([jnp.full((heads, tiles.lead), NEGATIVE, F32), vec], axis=1)
    vec = lax.dynamic_slice_in_dim(vec, part * tiles.blk, tiles.width, axis=1)
    vec = vec.reshape(heads // 4, 4, tiles.width)

    q1, k1, v1, n1 = self_project(where, inputs, own_inputs, gain_one, w1, tiles.reach, rows)
    hosts = [None] * 4
    if native:
        w3 = jnp.concatenate([feed_gate, feed_up], axis=1)
        hosts[0] = Transfers(dp, mp, 2, [w2, cross_out, feed_down], order + ["by_mp"])
        middle = round_up(w3.shape[1] // 2, 128)
        hosts[1] = Transfers(dp, mp, 3, [w3[:, :middle], w3[:, middle:]], ["by_dp", "by_dp"])
    (o1, lse_one), found = attend_forward(
        q1, k1, v1, mask_one, vec, tiles, True, "self_forward", hosts[0]
    )
    if native:
        w2, wo2, wd = found
        w2 = w2.reshape(mp, width, w2.shape[3])
    h1, n2, q2, k2, v2 = cross_project(where, o1, wo1, own_inputs, gain_two, encoded, w2)
    (o2, lse_two), found = attend_forward(
        q2, k2, v2, mask_two, keys_two, tiles, False, "cross_forward", hosts[1]
    )
    if native:
        wa, wb = (w.reshape(mp, width, w.shape[3]) for w in found)

    result, grad_two, grad_gain_three, gwa, gwb, gwd, do2, gwo2 = feed(
        where, o2, wo2, h1, gain_three, cut(cotangent), wa, wb, wd
    )

    def collect(array):
        array = lax.all_gather(array, "mp", axis=0, tiled=True)
        array = array.reshape(batches, parts, length // 64, tiles.blk, width)
        return array.transpose(0, 2, 1, 3, 4).reshape(batches, length, width)

    outputs = collect(result)

    def pieces(grad):
        return grad.reshape(grad.shape[0], dp, grad.shape[1] // dp, grad.shape[2])

    sharing = [[s * parts + p for p in range(parts)] for s in range(batches)]

    def share(dk, dv, count):
        both = jnp.concatenate([dk, dv], axis=1)
        both = both.reshape(count, parts, -1, both.shape[1]).transpose(1, 0, 2, 3)
        both = both.reshape(-1, both.shape[3])
        return lax.psum_scatter(
            both, "mp", scatter_dimension=0, axis_index_groups=sharing, tiled=True
        )

    if native:
        hosts[2] = Transfers(dp, mp, 4, grads=[gwd, gwo2])
        hosts[2].swap = Exchange(1, enc_length // 2, groups)
    (dq2, *dkv2), sums_down = attend_backward(
        q2, k2, v2, o2, do2, lse_two, mask_two, keys_two, tiles, False, "cross_backward", hosts[2]
    )
    dkv2 = dkv2[0] if native else share(dkv2[1], dkv2[0], 1)
    gwq2, grad_one, grad_gain_two, do1, gwo1 = cross_back(
        where, dq2, w2, n2, h1, gain_two, grad_two, wo1, o1
    )
    gwkv2, grad_memory = memory_back(where, dkv2, w2, encoded)

    if native:
        grads = [pieces(gwa), pieces(gwb)]
        hosts[3] = Transfers(dp, mp, 5, grads=grads)
        hosts[3].swap = Exchange(length // 64, tiles.blk, groups)
    (dq1, slopes, *dkv1), sums_feed = attend_backward(
        q1, k1, v1, o1, do1, lse_one, mask_one, vec, tiles, True, "self_backward", hosts[3]
    )
    if native:
        dkv1 = dkv1[0]
    else:
        dkv1 = share(dkv1[1][:length], dkv1[0][:length], length // 64)
    grad_encoded = lax.all_gather(grad_memory, "mp", axis=0, tiled=True).reshape(encoded.shape)
    gwq1, gwkv1, grad_rows, grad_gain_one = self_back(
        where, dq1, dkv1, w1, n1, own_inputs, gain_one, grad_one
    )
    slopes = slopes.reshape(heads, tiles.width)
    slopes = jnp.pad(slopes, ((0, 0), (64, length)))
    slopes = lax.dynamic_slice_in_dim(slopes, 64 + tiles.lead - part * tiles.blk, length, axis=1)
    grad_table = dot(onehot, slopes, ((0,), (1,)), HIGHEST)
    grad_gains = jnp.concatenate([grad_gain_one, grad_gain_two, grad_gain_three])

    kcols = gwkv1.shape[2] // 2
    if native:
        little = grad_gains.reshape(3, dp, size).transpose(1, 0, 2)
        little = jnp.broadcast_to(little[None], (mp, dp, 3, size))
        spots = grad_table.reshape(dp, position_bias.shape[0], mp, position_bias.shape[1])
        spots = spots.transpose(2, 0, 1, 3).reshape(mp, dp, 1, position_bias.size)
        spots = jnp.pad(spots, ((0, 0), (0, 0), (0, 4), (0, size - position_bias.size)))
        little = jnp.concatenate([little, spots], axis=2)
        grads = [pieces(g) for g in (gwq2, gwkv2, gwq1, gwkv1)] + [gwo1, little]
        *sums, little, grad_inputs = Transfers(
            dp, mp, 6, grads=grads, rows=[grad_rows.reshape(length // 64, tiles.blk, width)],
            spread=[(batches, length // 64, parts, tiles.blk, width)],
        ).run("scatter_rest")
        grad_inputs = grad_inputs.reshape(inputs.shape)
        sums = sums + list(sums_feed) + list(sums_down)
        gwq2, gwkv2, gwq1, gwkv1, gwo1, gwa, gwb, gwd, gwo2 = sums
        gw3 = jnp.concatenate([gwa, gwb], axis=1)
        half = gw3.shape[1] // 2
        gwg, gwu = gw3[:, :half], gw3[:, half:]
        gwk2, gwv2, gwk1, gwv1 = (
            g[:, at : at + kcols] for g in (gwkv2, gwkv1) for at in (0, kcols)
        )
        grad_gains = [little[n] for n in range(3)]
        grad_table = little[3, : position_bias.size].reshape(position_bias.shape)
    else:
        grad_inputs = collect(grad_rows)

        def summed(grad):
            return scatter(ungrouped(grad), ROWS_BY_DP)

        gwk1, gwv1 = summed(gwkv1[:, :, :kcols]), summed(gwkv1[:, :, kcols:])
        gwk2, gwv2 = summed(gwkv2[:, :, :kcols]), summed(gwkv2[:, :, kcols:])
        gwg, gwu = summed(gwa), summed(gwb)
        gwq1, gwq2 = summed(gwq1), summed(gwq2)
        gwo1, gwo2, gwd = (scatter(g, ROWS_BY_MP) for g in (gwo1, gwo2, gwd))
        small = jnp.concatenate([grad_gains.reshape(-1), grad_table.reshape(-1)])
        small = lax.psum(small, ("dp", "mp"))
        data = lax.axis_index("dp")
        grad_gains = lax.dynamic_slice_in_dim(
            small[: 3 * width].reshape(3, dp, width // dp), data, 1, axis=1
        )
        grad_gains = [grad_gains[n, 0] for n in range(3)]
        grad_table = lax.dynamic_slice(
            small[3 * width :].reshape(table.shape),
            (data * position_bias.shape[0], place * position_bias.shape[1]),
            position_bias.shape,
        )

    return (
        outputs, grad_inputs, grad_encoded,
        grad_gains[0], gwq1, gwk1, gwv1, gwo1, grad_table,
        grad_gains[1], gwq2, gwk2, gwv2, gwo2,
        grad_gains[2], gwg, gwu, gwd,
    )


def solution(mesh):
    rows3 = P("dp", None, None)
    by_dp = P("dp", "mp")
    by_mp = P("mp", "dp")
    gain = P("dp")
    return jax.shard_map(
        functools.partial(body, dp=mesh.shape["dp"], mp=mesh.shape["mp"]),
        mesh=mesh,
        in_specs=(
            rows3, rows3, P("dp", None), P("dp", None), P(),
            gain, by_dp, by_dp, by_dp, by_mp, by_dp,
            gain, by_dp, by_dp, by_dp, by_mp,
            gain, by_dp, by_dp, by_mp, rows3,
        ),
        out_specs=(
            rows3, rows3, rows3,
            gain, by_dp, by_dp, by_dp, by_mp, by_dp,
            gain, by_dp, by_dp, by_dp, by_mp,
            gain, by_dp, by_dp, by_mp,
        ),
        check_vma=False,
    )
```
